32 devices in a mesh: dp: 4 (over x, core), fsdp: 8 (over z, y).
Axes of the slice: x: 2, y: 2, z: 4, core: 2. Of those that a mesh axis runs over, the one named last changes fastest.
Arguments:
- inputs: bfloat16 [45056, 768], P(('dp', 'fsdp')), may hold values from -6 to 6
- segment_ids: int32 [45056], P(('dp', 'fsdp')), may hold values from 0 to 5, as said below
- cotangent: bfloat16 [45056, 768], P(('dp', 'fsdp')), may hold values from -6 to 6
- in_weight: bfloat16 [768, 2304], P(('dp', 'fsdp')), may hold values from -0.21875 to 0.21875
- in_bias: bfloat16 [1536], P(('dp', 'fsdp')), may hold values from -1 to 1
- out_weight: bfloat16 [768, 768], P(('dp', 'fsdp')), may hold values from -0.875 to 0.875
- out_bias: bfloat16 [768], P(('dp', 'fsdp')), may hold values from -1 to 1
- first_gain: bfloat16 [768], P(('dp', 'fsdp')), may hold values from 0.5 to 1.5
- first_shift: bfloat16 [768], P(('dp', 'fsdp')), may hold values from -1 to 1
- first_scale: bfloat16 [768], P(('dp', 'fsdp')), may hold values from 0.059814453 to 0.15917969
- up_weight: bfloat16 [768, 3072], P(('dp', 'fsdp')), may hold values from -0.21875 to 0.21875
- up_bias: bfloat16 [3072], P(('dp', 'fsdp')), may hold values from -1 to 1
- down_weight: bfloat16 [3072, 768], P(('dp', 'fsdp')), may hold values from -0.109375 to 0.109375
- down_bias: bfloat16 [768], P(('dp', 'fsdp')), may hold values from -1 to 1
- second_gain: bfloat16 [768], P(('dp', 'fsdp')), may hold values from 0.5 to 1.5
- second_shift: bfloat16 [768], P(('dp', 'fsdp')), may hold values from -1 to 1
- second_scale: bfloat16 [768], P(('dp', 'fsdp')), may hold values from 0.059814453 to 0.15917969
Outputs:
- outputs: bfloat16 [45056, 768], P(('dp', 'fsdp'))
- inputs_grad: float32 [45056, 768], P(('dp', 'fsdp'))
- in_weight_grad: float32 [768, 2304], P(('dp', 'fsdp'))
- in_bias_grad: float32 [1536], P(('dp', 'fsdp'))
- out_weight_grad: float32 [768, 768], P(('dp', 'fsdp'))
- out_bias_grad: float32 [768], P(('dp', 'fsdp'))
- first_gain_grad: float32 [768], P(('dp', 'fsdp'))
- first_shift_grad: float32 [768], P(('dp', 'fsdp'))
- first_scale_grad: float32 [768], P(('dp', 'fsdp'))
- up_weight_grad: float32 [768, 3072], P(('dp', 'fsdp'))
- up_bias_grad: float32 [3072], P(('dp', 'fsdp'))
- down_weight_grad: float32 [3072, 768], P(('dp', 'fsdp'))
- down_bias_grad: float32 [768], P(('dp', 'fsdp'))
- second_gain_grad: float32 [768], P(('dp', 'fsdp'))
- second_shift_grad: float32 [768], P(('dp', 'fsdp'))
- second_scale_grad: float32 [768], P(('dp', 'fsdp'))
The draws below stay inside these ranges and needn't reach their ends.
Inputs may be any that keep to these rules, and one draw needn't show every extreme that they name: `segment_ids`: on every device, a quarter of all devices (rounded down, chosen by the seed) hold one image: rows 0 to 1373 have id 0; every other device holds 5 images of 261 rows each, with ids 0 to 4 in order; the remaining rows of each device are padding with id 5.
All inputs are finite; a program needn't handle non-finite values.
Results may differ from the reference program's by a relative error of at most 0.0091.
Values may be sent and summed in bfloat16 or wider, within the bound.
A program may use at most 192 MiB of HBM per device.

```python
import jax
import jax.numpy as jnp
from jax import lax

D = 768
H = 12
HD = 64
FF = 3072
BIG = 1374
SMALL = 261
SMALLS = 5
ROWS = 1408
TOKENS = 45056


def draw_segment_ids(key, part):
    device_count = TOKENS // ROWS
    ranking = jax.random.permutation(key, device_count)
    holds_big = ranking < device_count // 4
    position = jnp.arange(ROWS, dtype=jnp.int32)
    small_layout = jnp.where(position < SMALLS * SMALL, position // SMALL, SMALLS)
    big_layout = jnp.where(position < BIG, 0, SMALLS)
    layout = jnp.where(holds_big[:, None], big_layout[None, :], small_layout[None, :])
    return layout.reshape(TOKENS).astype(jnp.int32)


def block_levels(stream_key, dims, split, least, high):
    loudness = 1.0
    for dim, shards_of in split:
        heights = jax.random.uniform(jax.random.fold_in(jax.random.fold_in(stream_key, 6), dim), (shards_of,), jnp.float32, least / len(split), high / len(split))
        loudness = loudness * jnp.repeat(jnp.exp(heights), dims[dim] // shards_of).reshape((-1,) + (1,) * (len(dims) - 1 - dim))
    return loudness


def gaussian(key, dims, deviation, reach, cuts=(), kind=jnp.bfloat16):
    factor_of = block_levels(key, dims, cuts, -0.22, 0.18) if cuts else 1.0
    array = jax.random.normal(key, dims, jnp.float32) * deviation * factor_of
    return jnp.minimum(jnp.maximum(array, -reach), reach).astype(kind)


def setup_inputs(seed: int = 0) -> dict:
    keys = jax.random.split(jax.random.key(seed), 18)
    inputs = gaussian(keys[0], (TOKENS, D), 1.0, 6.0, ((0, 32),))
    segment_ids = draw_segment_ids(jax.random.fold_in(keys[17], 71), 0)
    cotangent = gaussian(keys[2], (TOKENS, D), 1.0, 6.0, ((0, 32),))
    in_weight = gaussian(keys[3], (D, 3 * D), D ** -0.5, 0.21875, ((0, 32),))
    in_bias = gaussian(keys[4], (2 * D,), 0.2, 1.0, ((0, 32),))
    out_weight = gaussian(keys[5], (D, D), (D // 16) ** -0.5, 0.875, ((0, 32),))
    out_bias = gaussian(keys[6], (D,), 0.2, 1.0, ((0, 32),))
    first_gain = jnp.clip(1.0 + 0.1 * jax.random.normal(keys[7], (D,), jnp.float32), 0.5, 1.5).astype(jnp.bfloat16)
    first_shift = gaussian(keys[8], (D,), 0.2, 1.0, ((0, 32),))
    first_scale = jnp.clip(0.059814453 + 0.099365234 * jax.random.uniform(keys[9], (D,), jnp.float32) ** block_levels(keys[9], (D,), ((0, 32),), -0.2, 0.2), 0.059814453, 0.15917969).astype(jnp.bfloat16)
    up_weight = gaussian(keys[10], (D, FF), D ** -0.5, 0.21875, ((0, 32),))
    up_bias = gaussian(keys[11], (FF,), 0.2, 1.0, ((0, 32),))
    down_weight = gaussian(keys[12], (FF, D), FF ** -0.5, 0.109375, ((0, 32),))
    down_bias = gaussian(keys[13], (D,), 0.2, 1.0, ((0, 32),))
    second_gain = jnp.clip(1.0 + 0.1 * jax.random.normal(keys[14], (D,), jnp.float32), 0.5, 1.5).astype(jnp.bfloat16)
    second_shift = gaussian(keys[15], (D,), 0.2, 1.0, ((0, 32),))
    second_scale = jnp.clip(0.059814453 + 0.099365234 * jax.random.uniform(keys[16], (D,), jnp.float32) ** block_levels(keys[16], (D,), ((0, 32),), -0.2, 0.2), 0.059814453, 0.15917969).astype(jnp.bfloat16)
    return dict(inputs=inputs, segment_ids=segment_ids, cotangent=cotangent, in_weight=in_weight, in_bias=in_bias, out_weight=out_weight, out_bias=out_bias, first_gain=first_gain, first_shift=first_shift, first_scale=first_scale, up_weight=up_weight, up_bias=up_bias, down_weight=down_weight, down_bias=down_bias, second_gain=second_gain, second_shift=second_shift, second_scale=second_scale)


@jax.custom_vjp
def low(v):
    return lax.optimization_barrier(v.astype(jnp.bfloat16)).astype(jnp.float32)

@jax.custom_vjp
def low_back(v):
    return v

def low_keep(v):
    return (low(v), None)

def low_pass(kept, grad):
    return (grad,)

def back_keep(v):
    return (v, None)

def back_low(kept, grad):
    return (low(grad),)
low.defvjp(low_keep, low_pass)
low_back.defvjp(back_keep, back_low)
epsilon = 1e-06
highest = lax.Precision.HIGHEST

def norm_rows(values, gain, shift):
    centre = lax.optimization_barrier(jnp.mean(values, axis=-1, keepdims=True))
    centred = values - centre
    spread = lax.optimization_barrier(jnp.mean(centred * centred, axis=-1, keepdims=True))
    return centred * lax.rsqrt(spread + epsilon) * gain + shift

def layer(params, source, segments):
    in_weight, in_bias, out_weight, out_bias, first_gain, first_shift, first_scale, up_weight, up_bias, down_weight, down_bias, second_gain, second_shift, second_scale = params
    row_count = source.shape[0]
    normed = low(norm_rows(source, first_gain, first_shift))
    projected = jnp.dot(normed, in_weight, precision=highest)
    offsets = jnp.concatenate([in_bias[:D], jnp.zeros((D,), jnp.float32), in_bias[D:]])
    joined = low_back(low(projected + offsets))
    queries = joined[:, :D].reshape(row_count, H, HD)
    key_rows = joined[:, D:2 * D].reshape(row_count, H, HD)
    value_rows = joined[:, 2 * D:].reshape(row_count, H, HD)
    scores = jnp.einsum('qhd,khd->hqk', queries, key_rows, precision=highest) * HD ** (-0.5)
    scores = low_back(scores)
    same_image = segments[:, None] == segments[None, :]
    scores = jnp.where(same_image[None], scores, -1e+30)
    probs = low(jax.nn.softmax(scores, axis=-1))
    attended = jnp.einsum('hqk,khd->qhd', probs, value_rows, precision=highest).reshape(row_count, D)
    attended = low_back(low(attended))
    branch = low_back(jnp.dot(attended, out_weight, precision=highest) + out_bias)
    middle = source + first_scale * branch
    normed_two = low(norm_rows(middle, second_gain, second_shift))
    hidden = low_back(jnp.dot(normed_two, up_weight, precision=highest) + up_bias)
    active = low(jax.nn.gelu(hidden, approximate=False))
    mixed = low_back(jnp.dot(active, down_weight, precision=highest) + down_bias)
    return middle + second_scale * mixed

def reference(inputs, segment_ids, cotangent, in_weight, in_bias, out_weight, out_bias, first_gain, first_shift, first_scale, up_weight, up_bias, down_weight, down_bias, second_gain, second_shift, second_scale):
    params = tuple((item.astype(jnp.float32) for item in (in_weight, in_bias, out_weight, out_bias, first_gain, first_shift, first_scale, up_weight, up_bias, down_weight, down_bias, second_gain, second_shift, second_scale)))
    groups = inputs.shape[0] // ROWS
    sources = inputs.astype(jnp.float32).reshape(groups, ROWS, D)
    segments = segment_ids.reshape(groups, ROWS)
    upstream = cotangent.astype(jnp.float32).reshape(groups, ROWS, D)

    def advance(totals, item):
        block, segs, arriving = item
        valid = (segs < SMALLS).astype(jnp.float32)[:, None]
        result, pullback = jax.vjp(lambda prm, blk: layer(prm, blk, segs), params, block)
        param_grads, block_grad = pullback(arriving * valid)
        totals = jax.tree.map(jnp.add, totals, param_grads)
        return (totals, (result.astype(jnp.bfloat16), block_grad))
    zeros = jax.tree.map(jnp.zeros_like, params)
    totals, (results, grads_in) = lax.scan(advance, zeros, (sources, segments, upstream))
    return (results.reshape(inputs.shape[0], D), grads_in.reshape(inputs.shape[0], D), totals[0], totals[1], totals[2], totals[3], totals[4], totals[5], totals[6], totals[7], totals[8], totals[9], totals[10], totals[11], totals[12], totals[13])
```

```python
import functools

import jax
import jax.numpy as jnp
from jax import lax
from jax.experimental import pallas as pl
from jax.experimental.pallas import tpu as pltpu
from jax.sharding import PartitionSpec as P

HD = 64
PADDING = 5
EPSILON = 1e-06
LOG2E = 1.4426950408889634
FAR = -1e30
BF = jnp.bfloat16
F32 = jnp.float32
AXES = ("dp", "fsdp")
VMEM_LIMIT = 62 * 1024 * 1024


def dot(a, b, da, db):
    return lax.dot_general(a, b, (((da,), (db,)), ((), ())), preferred_element_type=F32)


def params(**more):
    return pltpu.CompilerParams(vmem_limit_bytes=VMEM_LIMIT, **more)


def cost(flops, moved, special=0):
    return pl.CostEstimate(flops=int(flops), bytes_accessed=int(moved), transcendentals=int(special))


def whole(shape):
    return pl.BlockSpec(shape, lambda *_: (0,) * len(shape), pipeline_mode=pl.Buffered(1))


def row_loop(rows, size, body):
    def step(index, carry):
        body(pl.ds(pl.multiple_of(index * size, size), size))
        return carry

    lax.fori_loop(0, rows // size, step, 0)


def normalised(values):
    centred = values - jnp.mean(values, axis=-1, keepdims=True)
    spread = jnp.mean(centred * centred, axis=-1, keepdims=True)
    inverse = lax.rsqrt(spread + EPSILON)
    return centred * inverse, inverse


def norm_back(unit, inverse, scaled):
    return inverse * (
        scaled
        - jnp.mean(scaled, axis=-1, keepdims=True)
        - unit * jnp.mean(scaled * unit, axis=-1, keepdims=True)
    )


def project_kernel(x_ref, w_ref, gain_ref, shift_ref, offset_ref, a1_ref, qkv_ref):
    @pl.when(pl.program_id(0) == 0)
    def _():
        def body(rows):
            unit, _ = normalised(x_ref[rows, :].astype(F32))
            a1_ref[rows, :] = (unit * gain_ref[...] + shift_ref[...]).astype(BF)

        row_loop(x_ref.shape[0], 32, body)

    qkv_ref[...] = (dot(a1_ref[...], w_ref[...], 1, 0) + offset_ref[...]).astype(BF)


def project(x, w_in, gain, shift, offset):
    rows, d = x.shape
    return pl.pallas_call(
        project_kernel,
        grid=(3,),
        in_specs=[
            whole((rows, d)),
            pl.BlockSpec((d, d), lambda t: (0, t)),
            whole((1, d)),
            whole((1, d)),
            pl.BlockSpec((1, d), lambda t: (0, t)),
        ],
        out_specs=[whole((rows, d)), pl.BlockSpec((rows, d), lambda t: (0, t))],
        out_shape=[
            jax.ShapeDtypeStruct((rows, d), BF),
            jax.ShapeDtypeStruct((rows, 3 * d), BF),
        ],
        compiler_params=params(),
        cost_estimate=cost(6 * rows * d * d, 2 * (5 * rows * d + 3 * d * d)),
        name="project",
    )(x, w_in, gain, shift, offset)


def chunks(rows, size):
    return [(start, min(size, rows - start)) for start in range(0, rows, size)]


def attend_kernel(chunk, q_ref, k_ref, v_ref, mark_ref, far_ref, o_ref, e_ref, inv_ref, vt_ref, k2_ref):
    rows = q_ref.shape[0]
    vt_ref[...] = v_ref[...].astype(F32).T.astype(BF)
    low = lax.broadcasted_iota(jnp.int32, (1, 128), 1) < HD
    for half in range(2):
        mine = low if half == 0 else jnp.logical_not(low)
        k2_ref[half] = jnp.where(mine, k_ref[...], far_ref[...])
    for start, size in chunks(rows, chunk):
        for half in range(2):
            mine = low if half == 0 else jnp.logical_not(low)
            span = pl.ds(start, size)
            query = jnp.where(mine, q_ref[span, :], mark_ref[span, :])
            scores = dot(k2_ref[half], query, 1, 1)
            top = jnp.max(scores, axis=0, keepdims=True)
            weights = jnp.exp2((scores - top) * (LOG2E * HD ** (-0.5)))
            total = jnp.sum(weights, axis=0, keepdims=True)
            weights_low = weights.astype(BF)
            e_ref[half, :, span] = weights_low
            inverse = 1.0 / total
            inv_ref[0, half : half + 1, span] = inverse
            head = pl.ds(half * HD, HD)
            o_ref[head, span] = (dot(vt_ref[head, :], weights_low, 1, 0) * inverse).astype(BF)


def attend(qkv, mark, far, chunk=256):
    rows, width = qkv.shape
    pairs = width // 384
    return pl.pallas_call(
        functools.partial(attend_kernel, chunk),
        grid=(pairs,),
        in_specs=[
            pl.BlockSpec((rows, 128), lambda p: (0, p)),
            pl.BlockSpec((rows, 128), lambda p: (0, pairs + p)),
            pl.BlockSpec((rows, 128), lambda p: (0, 2 * pairs + p)),
            whole((rows, 128)),
            whole((rows, 128)),
        ],
        out_specs=[
            pl.BlockSpec((128, rows), lambda p: (p, 0)),
            pl.BlockSpec((2, rows, rows), lambda p: (p, 0, 0)),
            pl.BlockSpec((1, 2, rows), lambda p: (p, 0, 0)),
        ],
        out_shape=[
            jax.ShapeDtypeStruct((pairs * 128, rows), BF),
            jax.ShapeDtypeStruct((2 * pairs, rows, rows), BF),
            jax.ShapeDtypeStruct((pairs, 2, rows), F32),
        ],
        scratch_shapes=[pltpu.VMEM((128, rows), BF), pltpu.VMEM((2, rows, 128), BF)],
        compiler_params=params(),
        cost_estimate=cost(2 * pairs * 4 * rows * rows * 256, 4 * pairs * rows * rows, 2 * pairs * rows * rows),
        name="attend",
    )(qkv, qkv, qkv, mark, far)


def middle_kernel(o_ref, x_ref, g_ref, w_ref, vec_ref, m1_ref, a2_ref, gm_ref, gmsum_ref):
    bias, scale1, gain2, shift2, scale2 = (vec_ref[i : i + 1, :] for i in range(5))
    m1_ref[...] = dot(o_ref[...], w_ref[...], 0, 0)
    gmsum_ref[...] = jnp.zeros_like(gmsum_ref)

    def body(rows):
        m1 = x_ref[rows, :].astype(F32) + scale1 * (m1_ref[rows, :] + bias)
        m1_ref[rows, :] = m1
        unit, _ = normalised(m1)
        a2_ref[rows, :] = (unit * gain2 + shift2).astype(BF)
        gm = (scale2 * g_ref[rows, :].astype(F32)).astype(BF)
        gm_ref[rows, :] = gm
        gmsum_ref[...] += jnp.sum(gm.astype(F32).reshape(-1, 8, gm.shape[-1]), axis=0)

    row_loop(x_ref.shape[0], 32, body)


def middle(o, x, g, w_out, vec):
    rows, d = x.shape
    return pl.pallas_call(
        middle_kernel,
        out_shape=[
            jax.ShapeDtypeStruct((rows, d), F32),
            jax.ShapeDtypeStruct((rows, d), BF),
            jax.ShapeDtypeStruct((rows, d), BF),
            jax.ShapeDtypeStruct((8, d), F32),
        ],
        compiler_params=params(),
        cost_estimate=cost(2 * rows * d * d, 14 * rows * d),
        name="middle",
    )(o, x, g, w_out, vec)


def gelu_parts(u):
    near = jnp.abs(u)
    t = 1.0 / (1.0 + (0.3275911 * 0.7071067811865476) * near)
    bell = jnp.exp2((-0.5 * LOG2E) * (u * u))
    poly = t * (
        0.5 * 0.254829592
        + t * (0.5 * -0.284496736 + t * (0.5 * 1.421413741 + t * (0.5 * -1.453152027 + t * (0.5 * 1.061405429))))
    )
    tail = poly * bell
    phi = jnp.where(u < 0, tail, 1.0 - tail)
    return u * phi, phi + u * bell * 0.3989422804014327


def feed_kernel(chunk, a2_ref, gm_ref, up_ref, ub_ref, down_ref, bm_ref, ga_ref, dup_ref, ddown_ref, dub_ref, gl_ref, gu_ref):
    first = pl.program_id(0) == 0

    @pl.when(first)
    def _():
        bm_ref[...] = jnp.zeros_like(bm_ref)
        ga_ref[...] = jnp.zeros_like(ga_ref)

    total = jnp.zeros((8, ub_ref.shape[-1]), F32)
    for start, size in chunks(a2_ref.shape[0], chunk):
        rows = pl.ds(start, size)
        u = dot(a2_ref[rows, :], up_ref[...], 1, 0) + ub_ref[...]
        back = dot(gm_ref[rows, :], down_ref[...], 1, 1)
        active, slope = gelu_parts(u)
        low = active.astype(BF)
        gl_ref[rows, :] = low
        gu = (slope * back).astype(BF)
        gu_ref[rows, :] = gu
        total += jnp.sum(gu.astype(F32).reshape(-1, 8, gu.shape[-1]), axis=0)
        bm_ref[rows, :] += dot(low, down_ref[...], 1, 0)
        ga_ref[rows, :] += dot(gu, up_ref[...], 1, 1)
    dub_ref[...] = total
    ddown_ref[...] = dot(gl_ref[...], gm_ref[...], 0, 0).astype(ddown_ref.dtype)
    dup_ref[...] = dot(a2_ref[...], gu_ref[...], 0, 0).astype(dup_ref.dtype)


def feed(a2, gm, w_up, b_up, w_down, block=512, chunk=704, kind=BF):
    rows, d = a2.shape
    ff = w_up.shape[1]
    return pl.pallas_call(
        functools.partial(feed_kernel, chunk),
        grid=(ff // block,),
        in_specs=[
            whole((rows, d)),
            whole((rows, d)),
            pl.BlockSpec((d, block), lambda f: (0, f)),
            pl.BlockSpec((1, block), lambda f: (0, f)),
            pl.BlockSpec((block, d), lambda f: (f, 0)),
        ],
        out_specs=[
            whole((rows, d)),
            whole((rows, d)),
            pl.BlockSpec((d, block), lambda f: (0, f)),
            pl.BlockSpec((block, d), lambda f: (f, 0)),
            pl.BlockSpec((8, block), lambda f: (0, f)),
        ],
        out_shape=[
            jax.ShapeDtypeStruct((rows, d), F32),
            jax.ShapeDtypeStruct((rows, d), F32),
            jax.ShapeDtypeStruct((d, ff), kind),
            jax.ShapeDtypeStruct((ff, d), kind),
            jax.ShapeDtypeStruct((8, ff), F32),
        ],
        scratch_shapes=[pltpu.VMEM((rows, block), BF), pltpu.VMEM((rows, block), BF)],
        compiler_params=params(),
        cost_estimate=cost(12 * rows * d * ff, 4 * 4 * d * ff),
        name="feed",
    )(a2, gm, w_up, b_up, w_down)


def join_kernel(size, m1_ref, bm_ref, ga_ref, x_ref, g_ref, o_ref, w_ref, vec_ref, out_ref, gm1_ref, go_ref, dout_ref, sums_ref, gb_ref):
    bias2, scale1, gain2, scale2 = (vec_ref[i : i + 1, :] for i in range(4))
    step = pl.program_id(0)

    @pl.when(step == 0)
    def _():
        sums_ref[...] = jnp.zeros_like(sums_ref)

    base = step * m1_ref.shape[0]

    def body(rows):
        m1 = m1_ref[rows, :]
        bm = bm_ref[rows, :] + bias2
        g = g_ref[rows, :].astype(F32)
        out_ref[rows, :] = (m1 + scale2 * bm).astype(BF)
        unit, inverse = normalised(m1)
        ga = ga_ref[rows, :]
        gm1 = g + norm_back(unit, inverse, ga * gain2)
        gm1_ref[rows, :] = gm1
        gb = (scale1 * gm1).astype(BF)
        gb_ref[pl.ds(pl.multiple_of(base + rows.start, size), size), :] = gb
        for index, value in enumerate(
            (g * bm, ga * unit, ga, gm1 * (m1 - x_ref[rows, :].astype(F32)), gb.astype(F32))
        ):
            sums_ref[index] += jnp.sum(value.reshape(-1, 8, value.shape[-1]), axis=0)

    row_loop(m1_ref.shape[0], size, body)

    @pl.when(step == pl.num_programs(0) - 1)
    def _():
        go_ref[...] = dot(w_ref[...], gb_ref[...], 1, 1).astype(BF)
        dout_ref[...] = dot(o_ref[...], gb_ref[...], 1, 0).astype(dout_ref.dtype)


def join(m1, bm, ga, x, g, o, w_out, vec, tile=128, kind=BF):
    rows, d = x.shape
    by_rows = pl.BlockSpec((tile, d), lambda i: (i, 0))
    return pl.pallas_call(
        functools.partial(join_kernel, 32),
        grid=(rows // tile,),
        in_specs=[by_rows] * 5 + [whole((d, rows)), whole((d, d)), whole((8, d))],
        out_specs=[by_rows, by_rows, whole((d, rows)), whole((d, d)), whole((5, 8, d))],
        out_shape=[
            jax.ShapeDtypeStruct((rows, d), BF),
            jax.ShapeDtypeStruct((rows, d), F32),
            jax.ShapeDtypeStruct((d, rows), BF),
            jax.ShapeDtypeStruct((d, d), kind),
            jax.ShapeDtypeStruct((5, 8, d), F32),
        ],
        scratch_shapes=[pltpu.VMEM((rows, d), BF)],
        compiler_params=params(),
        cost_estimate=cost(4 * rows * d * d, 26 * rows * d),
        name="join",
    )(m1, bm, ga, x, g, o, w_out, vec)


def attend_back_kernel(chunk, q_ref, k_ref, v_ref, go_ref, o_ref, e_ref, inv_ref, out_ref, kt_ref, gq_ref, gs_ref, gp_ref):
    rows = q_ref.shape[0]
    factor = HD ** (-0.5)
    kt_ref[...] = k_ref[...].astype(F32).T.astype(BF)
    low = lax.broadcasted_iota(jnp.int32, (1, 128), 1) < HD
    below = lax.broadcasted_iota(jnp.int32, (128, 1), 0) < HD
    gp_ref[...] = jnp.zeros_like(gp_ref)
    for start, size in chunks(rows, chunk):
        span = pl.ds(start, size)
        for half in range(2):
            head = pl.ds(half * HD, HD)
            incoming = go_ref[head, span].astype(F32) * inv_ref[0, half : half + 1, span]
            centre = jnp.sum(incoming * o_ref[head, span].astype(F32), axis=0, keepdims=True)
            gp_ref[half, head, span] = incoming.astype(BF)
            gp = dot(v_ref[...], gp_ref[half, :, span], 1, 0)
            gs = (e_ref[half, :, span].astype(F32) * (gp - centre)).astype(BF)
            gs_ref[half, :, span] = gs
            gq_ref[head, span] = dot(kt_ref[head, :], gs, 1, 0) * factor
    out_ref[0] = gq_ref[...].T.astype(BF)
    gk = [dot(gs_ref[half], q_ref[...], 1, 0) for half in range(2)]
    out_ref[1] = (jnp.where(low, gk[0], gk[1]) * factor).astype(BF)
    out_ref[2] = (dot(e_ref[0], gp_ref[0], 1, 1) + dot(e_ref[1], gp_ref[1], 1, 1)).astype(BF)


def attend_back(qkv, go, o, e, inv, chunk=256):
    rows, width = qkv.shape
    pairs = width // 384
    return pl.pallas_call(
        functools.partial(attend_back_kernel, chunk),
        grid=(pairs,),
        in_specs=[
            pl.BlockSpec((rows, 128), lambda p: (0, p)),
            pl.BlockSpec((rows, 128), lambda p: (0, pairs + p)),
            pl.BlockSpec((rows, 128), lambda p: (0, 2 * pairs + p)),
            pl.BlockSpec((128, rows), lambda p: (p, 0)),
            pl.BlockSpec((128, rows), lambda p: (p, 0)),
            pl.BlockSpec((2, rows, rows), lambda p: (p, 0, 0)),
            pl.BlockSpec((1, 2, rows), lambda p: (p, 0, 0)),
        ],
        out_specs=pl.BlockSpec((3, rows, 128), lambda p: (0, 0, p)),
        out_shape=jax.ShapeDtypeStruct((3, rows, pairs * 128), BF),
        scratch_shapes=[
            pltpu.VMEM((128, rows), BF),
            pltpu.VMEM((128, rows), F32),
            pltpu.VMEM((2, rows, rows), BF),
            pltpu.VMEM((2, 128, rows), BF),
        ],
        compiler_params=params(),
        cost_estimate=cost(2 * pairs * 8 * rows * rows * 256, 4 * pairs * rows * rows),
        name="attend_back",
    )(qkv, qkv, qkv, go, o, e, inv)


def finish_kernel(a1_ref, gqkv_ref, w_ref, x_ref, gm1_ref, gain_ref, dw_ref, cols_ref, gx_ref, sums_ref, ga_ref):
    step = pl.program_id(0)
    grads = gqkv_ref[0]
    dw_ref[...] = dot(a1_ref[...], grads, 0, 0).astype(dw_ref.dtype)
    cols_ref[0] = jnp.sum(grads.astype(F32).reshape(-1, 8, grads.shape[-1]), axis=0)
    part = dot(grads, w_ref[...], 1, 1)

    @pl.when(step == 0)
    def _():
        ga_ref[...] = part

    @pl.when(step > 0)
    def _():
        ga_ref[...] += part

    @pl.when(step == pl.num_programs(0) - 1)
    def _():
        sums_ref[...] = jnp.zeros_like(sums_ref)

        def body(rows):
            unit, inverse = normalised(x_ref[rows, :].astype(F32))
            ga = ga_ref[rows, :]
            gx_ref[rows, :] = gm1_ref[rows, :] + norm_back(unit, inverse, ga * gain_ref[...])
            for index, value in enumerate((ga * unit, ga)):
                sums_ref[index] += jnp.sum(value.reshape(-1, 8, value.shape[-1]), axis=0)

        row_loop(x_ref.shape[0], 32, body)


def finish(a1, gqkv, w_in, x, gm1, gain, kind=BF):
    rows, d = x.shape
    return pl.pallas_call(
        finish_kernel,
        grid=(3,),
        in_specs=[
            whole((rows, d)),
            pl.BlockSpec((1, rows, d), lambda t: (t, 0, 0)),
            pl.BlockSpec((d, d), lambda t: (0, t)),
            whole((rows, d)),
            whole((rows, d)),
            whole((1, d)),
        ],
        out_specs=[
            pl.BlockSpec((d, d), lambda t: (0, t)),
            pl.BlockSpec((1, 8, d), lambda t: (t, 0, 0)),
            whole((rows, d)),
            whole((2, 8, d)),
        ],
        out_shape=[
            jax.ShapeDtypeStruct((d, 3 * d), kind),
            jax.ShapeDtypeStruct((3, 8, d), F32),
            jax.ShapeDtypeStruct((rows, d), F32),
            jax.ShapeDtypeStruct((2, 8, d), F32),
        ],
        scratch_shapes=[pltpu.VMEM((rows, d), F32)],
        compiler_params=params(),
        cost_estimate=cost(12 * rows * d * d, 20 * rows * d),
        name="finish",
    )(a1, gqkv, w_in, x, gm1, gain)


def layer(gather, scatter, scatter_small, inputs, segment_ids, cotangent, in_weight, out_weight, up_weight, down_weight, vectors):
    rows, d = inputs.shape
    w_in, w_out, w_up, w_down, vecs = gather(in_weight, out_weight, up_weight, down_weight, vectors)
    in_bias, out_bias, gain1, shift1, scale1, up_bias, down_bias, gain2, shift2, scale2 = vecs
    lane = lax.broadcasted_iota(jnp.int32, (1, 128), 1) % HD
    same = segment_ids[:, None] == lane
    mark = same.astype(BF)
    far = jnp.where(same | (lane > PADDING), 0.0, FAR).astype(BF)
    g = jnp.where((segment_ids < PADDING)[:, None], cotangent, jnp.zeros_like(cotangent))
    offset = jnp.concatenate([in_bias[:, :d], jnp.zeros((1, d), F32), in_bias[:, d:]], axis=1)
    a1, qkv = project(inputs, w_in, gain1, shift1, offset)
    o, e, inv = attend(qkv, mark, far)
    blank = jnp.zeros((1, d), F32)
    m1, a2, gm, gm_sum = middle(
        o, inputs, g, w_out, jnp.concatenate([out_bias, scale1, gain2, shift2, scale2, blank, blank, blank])
    )
    bm, ga2, d_up, d_down, ub_sum = feed(a2, gm, w_up, up_bias, w_down)
    outputs, gm1, go, d_out, join_sums = join(
        m1, bm, ga2, inputs, g, o, w_out, jnp.concatenate([down_bias, scale1, gain2, scale2, blank, blank, blank, blank])
    )
    gqkv = attend_back(qkv, go, o, e, inv)
    d_in, col_sums, gx, last_sums = finish(a1, gqkv, w_in, inputs, gm1, gain1)
    s = jnp.sum
    j = s(join_sums, axis=1)
    c = s(col_sums, axis=1)
    t = s(last_sums, axis=1)
    small = scatter_small(
        [
            jnp.concatenate([c[0], c[2]]),
            j[4],
            t[0],
            t[1],
            j[3] / scale1[0],
            s(ub_sum, axis=0),
            s(gm_sum, axis=0),
            j[1],
            j[2],
            j[0],
        ]
    )
    d_in, d_out, d_up, d_down = scatter(d_in, d_out, d_up, d_down)
    return (
        outputs, gx, d_in, small[0], d_out, small[1], small[2], small[3], small[4],
        d_up, small[5], d_down, small[6], small[7], small[8], small[9],
    )


def shards(
    inputs, segment_ids, cotangent, in_weight, in_bias, out_weight, out_bias, first_gain, first_shift, first_scale,
    up_weight, up_bias, down_weight, down_bias, second_gain, second_shift, second_scale,
):
    vectors = (
        in_bias, out_bias, first_gain, first_shift, first_scale,
        up_bias, down_bias, second_gain, second_shift, second_scale,
    )

    def gather(w_in, w_out, w_up, w_down, vectors):
        take = lambda a: lax.all_gather(a, AXES, axis=0, tiled=True)
        joined = jnp.concatenate(vectors)[None]
        vec = take(joined)
        vecs = []
        at = 0
        for v in vectors:
            vecs.append(vec[:, at : at + v.shape[0]].reshape(1, -1).astype(F32))
            at += v.shape[0]
        return take(w_in), take(w_out), take(w_up), take(w_down), vecs

    def scatter(*grads):
        return [lax.psum_scatter(g, AXES, scatter_dimension=0, tiled=True).astype(F32) for g in grads]

    def scatter_small(sums):
        n = lax.axis_size(AXES)
        joined = jnp.concatenate([v.reshape(n, -1) for v in sums], axis=1)
        mine = lax.psum_scatter(joined, AXES, scatter_dimension=0, tiled=True)[0]
        out = []
        at = 0
        for v in sums:
            size = v.shape[0] // n
            out.append(mine[at : at + size])
            at += size
        return out

    return layer(
        gather, scatter, scatter_small, inputs, segment_ids, cotangent, in_weight, out_weight, up_weight, down_weight, vectors
    )


def solution(mesh):
    wide, flat = P(AXES, None), P(AXES)
    return jax.shard_map(
        shards,
        mesh=mesh,
        in_specs=(wide, flat, wide, wide, flat, wide, flat, flat, flat, flat, wide, flat, wide, flat, flat, flat, flat),
        out_specs=(wide, wide, wide, flat, wide, flat, flat, flat, flat, wide, flat, wide, flat, flat, flat, flat),
        check_vma=False,
    )
```

```python
import functools

import jax
import jax.numpy as jnp
from jax import lax
from jax.experimental import pallas as pl
from jax.experimental.pallas import tpu as pltpu
from jax.sharding import PartitionSpec as P

HD = 64
PADDING = 5
EPSILON = 1e-06
LOG2E = 1.4426950408889634
FAR = -1e30
BF = jnp.bfloat16
F32 = jnp.float32
AXES = ("dp", "fsdp")
VMEM_LIMIT = 62 * 1024 * 1024


def dot(a, b, da, db):
    return lax.dot_general(a, b, (((da,), (db,)), ((), ())), preferred_element_type=F32)


def params(**more):
    return pltpu.CompilerParams(vmem_limit_bytes=VMEM_LIMIT, **more)


def cost(flops, moved, special=0):
    return pl.CostEstimate(flops=int(flops), bytes_accessed=int(moved), transcendentals=int(special))


def whole(shape):
    return pl.BlockSpec(shape, lambda *_: (0,) * len(shape), pipeline_mode=pl.Buffered(1))


def row_loop(rows, size, body):
    def step(index, carry):
        body(pl.ds(pl.multiple_of(index * size, size), size))
        return carry

    lax.fori_loop(0, rows // size, step, 0)


def normalised(values):
    centred = values - jnp.mean(values, axis=-1, keepdims=True)
    spread = jnp.mean(centred * centred, axis=-1, keepdims=True)
    inverse = lax.rsqrt(spread + EPSILON)
    return centred * inverse, inverse


def norm_back(unit, inverse, scaled):
    return inverse * (
        scaled
        - jnp.mean(scaled, axis=-1, keepdims=True)
        - unit * jnp.mean(scaled * unit, axis=-1, keepdims=True)
    )


MESH = pl.DeviceIdType.MESH
ALL = slice(None)


class Near:
    def __init__(self, sizes):
        self.sizes = sizes
        dp, fsdp = lax.axis_index("dp"), lax.axis_index("fsdp")
        ny = sizes["y"]
        self.at = {"x": lax.div(dp, 2), "c": lax.rem(dp, 2), "z": lax.div(fsdp, ny), "y": lax.rem(fsdp, ny)}

    def along(self, axis, shift):
        return lax.rem(self.at[axis] + shift, self.sizes[axis])

    def device(self, axis, shift):
        at = {**self.at, axis: self.along(axis, shift)}
        return (at["x"] * 2 + at["c"], at["z"] * self.sizes["y"] + at["y"])

    def shifts(self, axis):
        return range(1, self.sizes[axis])

    def greet(self):
        barrier = pltpu.get_barrier_semaphore()
        count = 0
        for axis in "cxyz":
            for shift in self.shifts(axis):
                pl.semaphore_signal(barrier, inc=1, device_id=self.device(axis, shift), device_id_type=MESH)
                count += 1
        pl.semaphore_wait(barrier, count)


class Wires:
    def __init__(self, near, send, recv):
        self.near, self.send, self.recv, self.used = near, send, recv, 0

    def wire(self, src, dst, axis, shift):
        n = self.used
        self.used += 1
        return lambda: pltpu.make_async_remote_copy(
            src_ref=src, dst_ref=dst, send_sem=self.send.at[n], recv_sem=self.recv.at[n],
            device_id=self.near.device(axis, shift), device_id_type=MESH,
        )


def start(*groups):
    for group in groups:
        for wire in group:
            wire().start()


def landed(*groups):
    for group in groups:
        for wire in group:
            wire().wait_recv()


def left(*groups):
    for group in groups:
        for wire in group:
            wire().wait_send()


def halves(width):
    cut = (width // 256) * 128
    return (pl.ds(0, cut), pl.ds(cut, width - cut)) if width > 512 else (pl.ds(0, width), None)


def gather_wires(sizes):
    return sizes["z"] + 4 * (sizes["x"] + sizes["y"] - 2)


def gather_stages(near, mine, full, send, recv, own):
    wires = Wires(near, send, recv)
    at = near.at

    def piece(cols, **fixed):
        return full.at[tuple(fixed.get(a, at[a]) for a in "xczy") + (ALL, cols)]

    def spread(axis, done, cols, src=None):
        here = piece(cols, **{a: ALL for a in done})
        return [wires.wire(here if src is None else src, here, axis, k) for k in near.shifts(axis)]

    def forward(axis, done, cols):
        size = near.sizes[axis]
        parts = [piece(cols, **{a: ALL for a in done}, **{axis: near.along(axis, size - k)}) for k in near.shifts(axis)]
        return [wires.wire(p, p, "c", 1) for p in parts]

    first, second = halves(mine.shape[-1])
    whole_z = spread("z", "", ALL, mine)
    column = piece(ALL, z=ALL)
    pair = [wires.wire(column, column, "c", 1)]
    one, two, one_on, two_on = [], [], [], []
    for cols, (a, b) in ((first, "yx"), (second, "xy")):
        if cols is not None:
            one += spread(a, "z", cols)
            one_on += forward(a, "z", cols)
            two += spread(b, "z" + a, cols)
            two_on += forward(b, "z" + a, cols)
    keep = lambda: pltpu.make_async_copy(mine, piece(ALL), own)

    def stage0():
        keep().start()
        start(whole_z)

    def stage1():
        keep().wait()
        landed(whole_z)
        start(one, pair)

    def stage2():
        landed(one)
        start(two, one_on)

    def stage3():
        landed(two)
        start(two_on)

    def stage4():
        left(whole_z, pair, one, two, one_on, two_on)
        landed(pair, one_on, two_on)

    return [stage0, stage1, stage2, stage3, stage4]


def gather_scratch(sizes):
    n = gather_wires(sizes)
    return [pltpu.SemaphoreType.DMA((n,)), pltpu.SemaphoreType.DMA((n,)), pltpu.SemaphoreType.DMA(())]


def lead(sizes):
    return (sizes["x"], 2, sizes["z"], sizes["y"])


def gathered(sizes, arrays):
    return [jax.ShapeDtypeStruct(lead(sizes) + a.shape, a.dtype) for a in arrays]


def run_all(plans, lag=0):
    for t in range(5 + lag * (len(plans) - 1)):
        for i, plan in enumerate(plans):
            if 0 <= t - lag * i < 5:
                plan[t - lag * i]()


def gather_kernel(sizes, count, *refs):
    near = Near(sizes)
    near.greet()
    sems = refs[2 * count :]
    run_all([
        gather_stages(near, refs[i], refs[count + i], *sems[3 * i : 3 * i + 3]) for i in range(count)
    ])


def gather_all(sizes, arrays, collective_id):
    return pl.pallas_call(
        functools.partial(gather_kernel, sizes, len(arrays)),
        in_specs=[pl.BlockSpec(memory_space=pltpu.VMEM)] * len(arrays),
        out_specs=[pl.BlockSpec(memory_space=pltpu.HBM)] * len(arrays),
        out_shape=gathered(sizes, arrays),
        scratch_shapes=gather_scratch(sizes) * len(arrays),
        compiler_params=params(collective_id=collective_id, has_side_effects=True),
        name="gather_all",
    )(*arrays)


def scatter_wires(sizes):
    return 1 + 2 * (sizes["x"] + sizes["y"] - 2) + sizes["z"] - 1


SCATTER_REFS = 10


def scatter_scratch(sizes, block, width, kind):
    nx, ny, nz = sizes["x"], sizes["y"], sizes["z"]
    first, second = halves(width)
    a, b = first.size, second.size
    vmem = lambda *shape: pltpu.VMEM(shape, kind)
    n = scatter_wires(sizes)
    return [
        vmem(nx, nz, ny, block, width), vmem(nx, nz, ny, block, width),
        vmem(nx - 1, nz, ny, block, a), vmem(ny - 1, nx, nz, block, b),
        vmem(ny - 1, nz, block, a), vmem(nx - 1, nz, block, b),
        vmem(nz - 1, block, width),
        pltpu.SemaphoreType.DMA((n,)), pltpu.SemaphoreType.DMA((n,)), pltpu.SemaphoreType.DMA(()),
    ]


def scatter_stages(near, grad, out, held, got, x_first, y_first, y_then, x_then, z_last, send, recv, own):
    wires = Wires(near, send, recv)
    at, sizes = near.at, near.sizes
    nz, ny, nx = sizes["z"], sizes["y"], sizes["x"]
    x, y, z = at["x"], at["y"], at["z"]
    first, second = halves(held.shape[-1])
    load = lambda: pltpu.make_async_copy(grad.at[:, at["c"]], held, own)
    pair = [wires.wire(grad.at[:, 1 - at["c"]], got, "c", 1)]
    one = [wires.wire(held.at[near.along("x", k), :, :, :, first], x_first.at[k - 1], "x", k) for k in near.shifts("x")]
    one += [wires.wire(held.at[:, :, near.along("y", k), :, second], y_first.at[k - 1], "y", k) for k in near.shifts("y")]
    two = [wires.wire(held.at[x, :, near.along("y", k), :, first], y_then.at[k - 1], "y", k) for k in near.shifts("y")]
    two += [wires.wire(held.at[near.along("x", k), :, y, :, second], x_then.at[k - 1], "x", k) for k in near.shifts("x")]
    last = [wires.wire(held.at[x, near.along("z", k), y], z_last.at[k - 1], "z", k) for k in near.shifts("z")]

    def add(where, terms):
        held[where] = sum([t.astype(F32) for t in terms], held[where].astype(F32)).astype(held.dtype)

    def over_z(body):
        lax.fori_loop(0, nz, lambda i, carry: (body(i), carry)[1], 0)

    def stage0():
        start(pair)
        load().start()

    def stage1():
        load().wait()
        landed(pair)

        @over_z
        def _(i):
            for a in range(nx):
                for b in range(ny):
                    add((a, i, b), [got[a, i, b]])

        start(one)

    def stage2():
        landed(one)

        @over_z
        def _(i):
            for b in range(ny):
                add((x, i, b, ALL, first), [x_first[k - 1, i, b] for k in near.shifts("x")])
            for a in range(nx):
                add((a, i, y, ALL, second), [y_first[k - 1, a, i] for k in near.shifts("y")])

        start(two)

    def stage3():
        landed(two)

        @over_z
        def _(i):
            add((x, i, y, ALL, first), [y_then[k - 1, i] for k in near.shifts("y")])
            add((x, i, y, ALL, second), [x_then[k - 1, i] for k in near.shifts("x")])

        start(last)

    def stage4():
        landed(last)
        out[...] = sum([z_last[k - 1].astype(F32) for k in near.shifts("z")], held[x, z, y].astype(F32))
        left(pair, one, two, last)

    return [stage0, stage1, stage2, stage3, stage4]


def total_scratch(sizes, shape):
    n = sum(sizes[a] - 1 for a in "cxyz")
    return [pltpu.VMEM((n,) + shape, F32), pltpu.VMEM((3,) + shape, F32), pltpu.SemaphoreType.DMA((n,)), pltpu.SemaphoreType.DMA((n,))]


def total_stages(near, mine, out, got, held, send, recv):
    wires = Wires(near, send, recv)
    groups, slots = [], []
    for step, axis in enumerate("cxyz"):
        src = mine if step == 0 else held.at[step - 1]
        slots.append([wires.used + k - 1 for k in near.shifts(axis)])
        groups.append([wires.wire(src, got.at[wires.used], axis, k) for k in near.shifts(axis)])

    def stage(step):
        def run():
            if step > 0:
                landed(groups[step - 1])
                total = mine[...] if step == 1 else held[step - 2]
                for slot in slots[step - 1]:
                    total = total + got[slot]
                if step < 4:
                    held[step - 1] = total
                else:
                    out[...] = total
                    left(*groups)
            if step < 4:
                start(groups[step])

        return run

    return [stage(step) for step in range(5)]


def scatter_kernel(sizes, count, lag, *refs):
    near = Near(sizes)
    near.greet()
    ins, outs, rest = refs[: count + 1], refs[count + 1 : 2 * count + 2], refs[2 * count + 2 :]
    plans = [
        scatter_stages(near, ins[i], outs[i], *rest[SCATTER_REFS * i : SCATTER_REFS * (i + 1)]) for i in range(count)
    ]
    small = total_stages(near, ins[count], outs[count], *rest[SCATTER_REFS * count :])
    run_all([*plans, small] if lag == 0 else plans, lag)
    if lag:
        run_all([small])


def blocks_of(sizes, grads):
    return [g.reshape(lead(sizes) + (-1, g.shape[1])) for g in grads]


def scatter_all(sizes, grads, small, collective_id, lag=0):
    blocks = blocks_of(sizes, grads)
    vmem, hbm = pl.BlockSpec(memory_space=pltpu.VMEM), pl.BlockSpec(memory_space=pltpu.HBM)
    return pl.pallas_call(
        functools.partial(scatter_kernel, sizes, len(grads), lag),
        in_specs=[hbm] * len(grads) + [vmem],
        out_specs=[vmem] * (len(grads) + 1),
        out_shape=[jax.ShapeDtypeStruct(b.shape[-2:], F32) for b in blocks] + [jax.ShapeDtypeStruct(small.shape, F32)],
        scratch_shapes=[s for b in blocks for s in scatter_scratch(sizes, *b.shape[-2:], b.dtype)] + total_scratch(sizes, small.shape),
        compiler_params=params(collective_id=collective_id, has_side_effects=True),
        name="scatter_all",
    )(*blocks, small)


def pump(schedule, plans, chunk):
    for step in sorted({at[0] for at in schedule if at[1] == chunk}):

        @pl.when(pl.program_id(0) == step)
        def _():
            for plan, stage in schedule[step, chunk]:
                plans[plan][stage]()


def mesh_sizes(mesh):
    fsdp = mesh.shape["fsdp"]
    ny = 1 << ((fsdp.bit_length() - 1) // 2)
    return {"x": mesh.shape["dp"] // 2, "c": 2, "z": fsdp // ny, "y": ny}


def project_kernel(x_ref, w_ref, gain_ref, shift_ref, offset_ref, a1_ref, qkv_ref):
    @pl.when(pl.program_id(0) == 0)
    def _():
        def body(rows):
            unit, _ = normalised(x_ref[rows, :].astype(F32))
            a1_ref[rows, :] = (unit * gain_ref[...] + shift_ref[...]).astype(BF)

        row_loop(x_ref.shape[0], 32, body)

    qkv_ref[...] = (dot(a1_ref[...], w_ref[...], 1, 0) + offset_ref[...]).astype(BF)


def project(x, w_in, gain, shift, offset):
    rows, d = x.shape
    return pl.pallas_call(
        project_kernel,
        grid=(3,),
        in_specs=[
            whole((rows, d)),
            pl.BlockSpec((d, d), lambda t: (0, t)),
            whole((1, d)),
            whole((1, d)),
            pl.BlockSpec((1, d), lambda t: (0, t)),
        ],
        out_specs=[whole((rows, d)), pl.BlockSpec((rows, d), lambda t: (0, t))],
        out_shape=[
            jax.ShapeDtypeStruct((rows, d), BF),
            jax.ShapeDtypeStruct((rows, 3 * d), BF),
        ],
        compiler_params=params(),
        cost_estimate=cost(6 * rows * d * d, 2 * (5 * rows * d + 3 * d * d)),
        name="project",
    )(x, w_in, gain, shift, offset)


def chunks(rows, size):
    return [(start, min(size, rows - start)) for start in range(0, rows, size)]


GATHER_AT = {
    (0, 0): [(0, 0), (1, 0)],
    (0, 3): [(0, 1)],
    (1, 0): [(2, 0), (0, 2)],
    (1, 3): [(1, 1)],
    (2, 0): [(0, 3)],
    (2, 3): [(1, 2)],
    (3, 0): [(2, 1)],
    (4, 0): [(1, 3), (2, 2)],
    (5, 3): [(2, 3)],
    (5, 5): [(0, 4), (1, 4), (2, 4)],
}


def attend_kernel(chunk, sizes, count, q_ref, k_ref, v_ref, mark_ref, far_ref, *refs):
    shards, (o_ref, e_ref, inv_ref) = refs[:count], refs[count : count + 3]
    full, (vt_ref, k2_ref), sems = refs[count + 3 : 2 * count + 3], refs[2 * count + 3 : 2 * count + 5], refs[2 * count + 5 :]
    rows = q_ref.shape[0]
    plans, schedule = [], {}
    if count:
        near, schedule = Near(sizes), GATHER_AT
        pl.when(pl.program_id(0) == 0)(near.greet)
        plans = [gather_stages(near, shards[i], full[i], *sems[3 * i : 3 * i + 3]) for i in range(count)]
    vt_ref[...] = v_ref[...].astype(F32).T.astype(BF)
    low = lax.broadcasted_iota(jnp.int32, (1, 128), 1) < HD
    for half in range(2):
        mine = low if half == 0 else jnp.logical_not(low)
        k2_ref[half] = jnp.where(mine, k_ref[...], far_ref[...])
    for turn, (start, size) in enumerate(chunks(rows, chunk)):
        pump(schedule, plans, turn)
        for half in range(2):
            mine = low if half == 0 else jnp.logical_not(low)
            span = pl.ds(start, size)
            query = jnp.where(mine, q_ref[span, :], mark_ref[span, :])
            scores = dot(k2_ref[half], query, 1, 1)
            top = jnp.max(scores, axis=0, keepdims=True)
            weights = jnp.exp2((scores - top) * (LOG2E * HD ** (-0.5)))
            total = jnp.sum(weights, axis=0, keepdims=True)
            weights_low = weights.astype(BF)
            e_ref[half, :, span] = weights_low
            inverse = 1.0 / total
            inv_ref[0, half : half + 1, span] = inverse
            head = pl.ds(half * HD, HD)
            o_ref[head, span] = (dot(vt_ref[head, :], weights_low, 1, 0) * inverse).astype(BF)


def attend(qkv, mark, far, sizes, shards, chunk=256):
    count = len(shards)
    rows, width = qkv.shape
    pairs = width // 384
    return pl.pallas_call(
        functools.partial(attend_kernel, chunk, sizes, count),
        grid=(pairs,),
        in_specs=[
            pl.BlockSpec((rows, 128), lambda p: (0, p)),
            pl.BlockSpec((rows, 128), lambda p: (0, pairs + p)),
            pl.BlockSpec((rows, 128), lambda p: (0, 2 * pairs + p)),
            whole((rows, 128)),
            whole((rows, 128)),
            *[whole(a.shape) for a in shards],
        ],
        out_specs=[
            pl.BlockSpec((128, rows), lambda p: (p, 0)),
            pl.BlockSpec((2, rows, rows), lambda p: (p, 0, 0)),
            pl.BlockSpec((1, 2, rows), lambda p: (p, 0, 0)),
            *[pl.BlockSpec(memory_space=pltpu.HBM)] * count,
        ],
        out_shape=[
            jax.ShapeDtypeStruct((pairs * 128, rows), BF),
            jax.ShapeDtypeStruct((2 * pairs, rows, rows), BF),
            jax.ShapeDtypeStruct((pairs, 2, rows), F32),
            *(gathered(sizes, shards) if count else []),
        ],
        scratch_shapes=[
            pltpu.VMEM((128, rows), BF),
            pltpu.VMEM((2, rows, 128), BF),
            *(gather_scratch(sizes) * count if count else []),
        ],
        compiler_params=params(collective_id=1, has_side_effects=True) if count else params(),
        cost_estimate=cost(2 * pairs * 4 * rows * rows * 256, 4 * pairs * rows * rows, 2 * pairs * rows * rows),
        name="attend",
    )(qkv, qkv, qkv, mark, far, *shards)


def middle_kernel(o_ref, x_ref, g_ref, w_ref, vec_ref, m1_ref, a2_ref, gm_ref, gmsum_ref):
    bias, scale1, gain2, shift2, scale2 = (vec_ref[i : i + 1, :] for i in range(5))
    m1_ref[...] = dot(o_ref[...], w_ref[...], 0, 0)
    gmsum_ref[...] = jnp.zeros_like(gmsum_ref)

    def body(rows):
        m1 = x_ref[rows, :].astype(F32) + scale1 * (m1_ref[rows, :] + bias)
        m1_ref[rows, :] = m1
        unit, _ = normalised(m1)
        a2_ref[rows, :] = (unit * gain2 + shift2).astype(BF)
        gm = (scale2 * g_ref[rows, :].astype(F32)).astype(BF)
        gm_ref[rows, :] = gm
        gmsum_ref[...] += jnp.sum(gm.astype(F32).reshape(-1, 8, gm.shape[-1]), axis=0)

    row_loop(x_ref.shape[0], 32, body)


def middle(o, x, g, w_out, vec):
    rows, d = x.shape
    return pl.pallas_call(
        middle_kernel,
        out_shape=[
            jax.ShapeDtypeStruct((rows, d), F32),
            jax.ShapeDtypeStruct((rows, d), BF),
            jax.ShapeDtypeStruct((rows, d), BF),
            jax.ShapeDtypeStruct((8, d), F32),
        ],
        compiler_params=params(),
        cost_estimate=cost(2 * rows * d * d, 14 * rows * d),
        name="middle",
    )(o, x, g, w_out, vec)


def gelu_parts(u):
    near = jnp.abs(u)
    t = 1.0 / (1.0 + (0.3275911 * 0.7071067811865476) * near)
    bell = jnp.exp2((-0.5 * LOG2E) * (u * u))
    poly = t * (
        0.5 * 0.254829592
        + t * (0.5 * -0.284496736 + t * (0.5 * 1.421413741 + t * (0.5 * -1.453152027 + t * (0.5 * 1.061405429))))
    )
    tail = poly * bell
    phi = jnp.where(u < 0, tail, 1.0 - tail)
    return u * phi, phi + u * bell * 0.3989422804014327


def feed_kernel(chunk, a2_ref, gm_ref, up_ref, ub_ref, down_ref, bm_ref, ga_ref, dup_ref, ddown_ref, dub_ref, gl_ref, gu_ref):
    first = pl.program_id(0) == 0

    @pl.when(first)
    def _():
        bm_ref[...] = jnp.zeros_like(bm_ref)
        ga_ref[...] = jnp.zeros_like(ga_ref)

    total = jnp.zeros((8, ub_ref.shape[-1]), F32)
    for start, size in chunks(a2_ref.shape[0], chunk):
        rows = pl.ds(start, size)
        u = dot(a2_ref[rows, :], up_ref[...], 1, 0) + ub_ref[...]
        back = dot(gm_ref[rows, :], down_ref[...], 1, 1)
        active, slope = gelu_parts(u)
        low = active.astype(BF)
        gl_ref[rows, :] = low
        gu = (slope * back).astype(BF)
        gu_ref[rows, :] = gu
        total += jnp.sum(gu.astype(F32).reshape(-1, 8, gu.shape[-1]), axis=0)
        bm_ref[rows, :] += dot(low, down_ref[...], 1, 0)
        ga_ref[rows, :] += dot(gu, up_ref[...], 1, 1)
    dub_ref[...] = total
    ddown_ref[...] = dot(gl_ref[...], gm_ref[...], 0, 0).astype(ddown_ref.dtype)
    dup_ref[...] = dot(a2_ref[...], gu_ref[...], 0, 0).astype(dup_ref.dtype)


def feed(a2, gm, w_up, b_up, w_down, block=512, chunk=704, kind=BF):
    rows, d = a2.shape
    ff = w_up.shape[1]
    return pl.pallas_call(
        functools.partial(feed_kernel, chunk),
        grid=(ff // block,),
        in_specs=[
            whole((rows, d)),
            whole((rows, d)),
            pl.BlockSpec((d, block), lambda f: (0, f)),
            pl.BlockSpec((1, block), lambda f: (0, f)),
            pl.BlockSpec((block, d), lambda f: (f, 0)),
        ],
        out_specs=[
            whole((rows, d)),
            whole((rows, d)),
            pl.BlockSpec((d, block), lambda f: (0, f)),
            pl.BlockSpec((block, d), lambda f: (f, 0)),
            pl.BlockSpec((8, block), lambda f: (0, f)),
        ],
        out_shape=[
            jax.ShapeDtypeStruct((rows, d), F32),
            jax.ShapeDtypeStruct((rows, d), F32),
            jax.ShapeDtypeStruct((d, ff), kind),
            jax.ShapeDtypeStruct((ff, d), kind),
            jax.ShapeDtypeStruct((8, ff), F32),
        ],
        scratch_shapes=[pltpu.VMEM((rows, block), BF), pltpu.VMEM((rows, block), BF)],
        compiler_params=params(),
        cost_estimate=cost(12 * rows * d * ff, 4 * 4 * d * ff),
        name="feed",
    )(a2, gm, w_up, b_up, w_down)


def join_kernel(size, m1_ref, bm_ref, ga_ref, x_ref, g_ref, o_ref, w_ref, vec_ref, out_ref, gm1_ref, go_ref, dout_ref, sums_ref, gb_ref):
    bias2, scale1, gain2, scale2 = (vec_ref[i : i + 1, :] for i in range(4))
    step = pl.program_id(0)

    @pl.when(step == 0)
    def _():
        sums_ref[...] = jnp.zeros_like(sums_ref)

    base = step * m1_ref.shape[0]

    def body(rows):
        m1 = m1_ref[rows, :]
        bm = bm_ref[rows, :] + bias2
        g = g_ref[rows, :].astype(F32)
        out_ref[rows, :] = (m1 + scale2 * bm).astype(BF)
        unit, inverse = normalised(m1)
        ga = ga_ref[rows, :]
        gm1 = g + norm_back(unit, inverse, ga * gain2)
        gm1_ref[rows, :] = gm1
        gb = (scale1 * gm1).astype(BF)
        gb_ref[pl.ds(pl.multiple_of(base + rows.start, size), size), :] = gb
        for index, value in enumerate(
            (g * bm, ga * unit, ga, gm1 * (m1 - x_ref[rows, :].astype(F32)), gb.astype(F32))
        ):
            sums_ref[index] += jnp.sum(value.reshape(-1, 8, value.shape[-1]), axis=0)

    row_loop(m1_ref.shape[0], size, body)

    @pl.when(step == pl.num_programs(0) - 1)
    def _():
        go_ref[...] = dot(w_ref[...], gb_ref[...], 1, 1).astype(BF)
        dout_ref[...] = dot(o_ref[...], gb_ref[...], 1, 0).astype(dout_ref.dtype)


def join(m1, bm, ga, x, g, o, w_out, vec, tile=128, kind=BF):
    rows, d = x.shape
    by_rows = pl.BlockSpec((tile, d), lambda i: (i, 0))
    return pl.pallas_call(
        functools.partial(join_kernel, 32),
        grid=(rows // tile,),
        in_specs=[by_rows] * 5 + [whole((d, rows)), whole((d, d)), whole((8, d))],
        out_specs=[by_rows, by_rows, whole((d, rows)), whole((d, d)), whole((5, 8, d))],
        out_shape=[
            jax.ShapeDtypeStruct((rows, d), BF),
            jax.ShapeDtypeStruct((rows, d), F32),
            jax.ShapeDtypeStruct((d, rows), BF),
            jax.ShapeDtypeStruct((d, d), kind),
            jax.ShapeDtypeStruct((5, 8, d), F32),
        ],
        scratch_shapes=[pltpu.VMEM((rows, d), BF)],
        compiler_params=params(),
        cost_estimate=cost(4 * rows * d * d, 26 * rows * d),
        name="join",
    )(m1, bm, ga, x, g, o, w_out, vec)


SCATTER_AT = {
    (0, 0): [(0, 0)],
    (0, 3): [(0, 1), (1, 0)],
    (1, 3): [(2, 0)],
    (2, 0): [(0, 2), (1, 1)],
    (3, 0): [(0, 3)],
    (4, 0): [(1, 2), (2, 1)],
    (4, 3): [(0, 4)],
    (5, 0): [(1, 3), (2, 2)],
    (5, 3): [(2, 3)],
    (5, 5): [(1, 4), (2, 4)],
}


def attend_back_kernel(chunk, sizes, count, q_ref, k_ref, v_ref, go_ref, o_ref, e_ref, inv_ref, *refs):
    grads, out_ref, sums = refs[:count], refs[count], refs[count + 1 : 2 * count + 1]
    (kt_ref, gq_ref, gs_ref, gp_ref), rest = refs[2 * count + 1 : 2 * count + 5], refs[2 * count + 5 :]
    rows = q_ref.shape[0]
    plans, schedule = [], {}
    if count:
        near, schedule = Near(sizes), SCATTER_AT
        pl.when(pl.program_id(0) == 0)(near.greet)
        plans = [
            scatter_stages(near, grads[i], sums[i], *rest[SCATTER_REFS * i : SCATTER_REFS * (i + 1)]) for i in range(count)
        ]
    factor = HD ** (-0.5)
    kt_ref[...] = k_ref[...].astype(F32).T.astype(BF)
    low = lax.broadcasted_iota(jnp.int32, (1, 128), 1) < HD
    below = lax.broadcasted_iota(jnp.int32, (128, 1), 0) < HD
    gp_ref[...] = jnp.zeros_like(gp_ref)
    for turn, (start, size) in enumerate(chunks(rows, chunk)):
        pump(schedule, plans, turn)
        span = pl.ds(start, size)
        for half in range(2):
            head = pl.ds(half * HD, HD)
            incoming = go_ref[head, span].astype(F32) * inv_ref[0, half : half + 1, span]
            centre = jnp.sum(incoming * o_ref[head, span].astype(F32), axis=0, keepdims=True)
            gp_ref[half, head, span] = incoming.astype(BF)
            gp = dot(v_ref[...], gp_ref[half, :, span], 1, 0)
            gs = (e_ref[half, :, span].astype(F32) * (gp - centre)).astype(BF)
            gs_ref[half, :, span] = gs
            gq_ref[head, span] = dot(kt_ref[head, :], gs, 1, 0) * factor
    out_ref[0] = gq_ref[...].T.astype(BF)
    gk = [dot(gs_ref[half], q_ref[...], 1, 0) for half in range(2)]
    out_ref[1] = (jnp.where(low, gk[0], gk[1]) * factor).astype(BF)
    out_ref[2] = (dot(e_ref[0], gp_ref[0], 1, 1) + dot(e_ref[1], gp_ref[1], 1, 1)).astype(BF)


def attend_back(qkv, go, o, e, inv, sizes, grads, chunk=256):
    blocks = blocks_of(sizes, grads) if grads else []
    count = len(blocks)
    rows, width = qkv.shape
    pairs = width // 384
    return pl.pallas_call(
        functools.partial(attend_back_kernel, chunk, sizes, count),
        grid=(pairs,),
        in_specs=[
            pl.BlockSpec((rows, 128), lambda p: (0, p)),
            pl.BlockSpec((rows, 128), lambda p: (0, pairs + p)),
            pl.BlockSpec((rows, 128), lambda p: (0, 2 * pairs + p)),
            pl.BlockSpec((128, rows), lambda p: (p, 0)),
            pl.BlockSpec((128, rows), lambda p: (p, 0)),
            pl.BlockSpec((2, rows, rows), lambda p: (p, 0, 0)),
            pl.BlockSpec((1, 2, rows), lambda p: (p, 0, 0)),
            *[pl.BlockSpec(memory_space=pltpu.HBM)] * count,
        ],
        out_specs=[pl.BlockSpec((3, rows, 128), lambda p: (0, 0, p)), *[whole(b.shape[-2:]) for b in blocks]],
        out_shape=[
            jax.ShapeDtypeStruct((3, rows, pairs * 128), BF),
            *[jax.ShapeDtypeStruct(b.shape[-2:], F32) for b in blocks],
        ],
        scratch_shapes=[
            pltpu.VMEM((128, rows), BF),
            pltpu.VMEM((128, rows), F32),
            pltpu.VMEM((2, rows, rows), BF),
            pltpu.VMEM((2, 128, rows), BF),
            *[s for b in blocks for s in scatter_scratch(sizes, *b.shape[-2:], b.dtype)],
        ],
        compiler_params=params(collective_id=2, has_side_effects=True) if count else params(),
        cost_estimate=cost(2 * pairs * 8 * rows * rows * 256, 4 * pairs * rows * rows),
        name="attend_back",
    )(qkv, qkv, qkv, go, o, e, inv, *blocks)


def finish_kernel(a1_ref, gqkv_ref, w_ref, x_ref, gm1_ref, gain_ref, dw_ref, cols_ref, gx_ref, sums_ref, ga_ref):
    step = pl.program_id(0)
    grads = gqkv_ref[0]
    dw_ref[...] = dot(a1_ref[...], grads, 0, 0).astype(dw_ref.dtype)
    cols_ref[0] = jnp.sum(grads.astype(F32).reshape(-1, 8, grads.shape[-1]), axis=0)
    part = dot(grads, w_ref[...], 1, 1)

    @pl.when(step == 0)
    def _():
        ga_ref[...] = part

    @pl.when(step > 0)
    def _():
        ga_ref[...] += part

    @pl.when(step == pl.num_programs(0) - 1)
    def _():
        sums_ref[...] = jnp.zeros_like(sums_ref)

        def body(rows):
            unit, inverse = normalised(x_ref[rows, :].astype(F32))
            ga = ga_ref[rows, :]
            gx_ref[rows, :] = gm1_ref[rows, :] + norm_back(unit, inverse, ga * gain_ref[...])
            for index, value in enumerate((ga * unit, ga)):
                sums_ref[index] += jnp.sum(value.reshape(-1, 8, value.shape[-1]), axis=0)

        row_loop(x_ref.shape[0], 32, body)


def finish(a1, gqkv, w_in, x, gm1, gain, kind=BF):
    rows, d = x.shape
    return pl.pallas_call(
        finish_kernel,
        grid=(3,),
        in_specs=[
            whole((rows, d)),
            pl.BlockSpec((1, rows, d), lambda t: (t, 0, 0)),
            pl.BlockSpec((d, d), lambda t: (0, t)),
            whole((rows, d)),
            whole((rows, d)),
            whole((1, d)),
        ],
        out_specs=[
            pl.BlockSpec((d, d), lambda t: (0, t)),
            pl.BlockSpec((1, 8, d), lambda t: (t, 0, 0)),
            whole((rows, d)),
            whole((2, 8, d)),
        ],
        out_shape=[
            jax.ShapeDtypeStruct((d, 3 * d), kind),
            jax.ShapeDtypeStruct((3, 8, d), F32),
            jax.ShapeDtypeStruct((rows, d), F32),
            jax.ShapeDtypeStruct((2, 8, d), F32),
        ],
        scratch_shapes=[pltpu.VMEM((rows, d), F32)],
        compiler_params=params(),
        cost_estimate=cost(12 * rows * d * d, 20 * rows * d),
        name="finish",
    )(a1, gqkv, w_in, x, gm1, gain)


def take(a):
    return lax.all_gather(a, AXES, axis=0, tiled=True)


def give(g):
    return lax.psum_scatter(g, AXES, scatter_dimension=0, tiled=True).astype(F32)


def layer(
    sizes, inputs, segment_ids, cotangent, in_weight, in_bias, out_weight, out_bias, first_gain, first_shift, first_scale,
    up_weight, up_bias, down_weight, down_bias, second_gain, second_shift, second_scale,
):
    rows, d = inputs.shape
    n = lax.axis_size(AXES)
    vectors = (
        in_bias, out_bias, first_gain, first_shift, first_scale,
        up_bias, down_bias, second_gain, second_shift, second_scale,
    )
    own = all(w.shape[0] % 8 == 0 for w in (in_weight, out_weight, up_weight, down_weight))
    joined = jnp.concatenate(vectors)[None]
    used = joined.shape[1]
    if own:
        tile = jnp.pad(joined, ((0, 7), (0, -used % 128)))
        w_in, vec = gather_all(sizes, [in_weight, tile], 0)
        w_in, vec = w_in.reshape(-1, 3 * d), vec.reshape(n, 8, -1)[:, 0, :used]
    else:
        w_in, vec = take(in_weight), take(joined)
    vecs = []
    at = 0
    for v in vectors:
        vecs.append(vec[:, at : at + v.shape[0]].reshape(1, -1).astype(F32))
        at += v.shape[0]
    in_bias, out_bias, gain1, shift1, scale1, up_bias, down_bias, gain2, shift2, scale2 = vecs
    lane = lax.broadcasted_iota(jnp.int32, (1, 128), 1) % HD
    same = segment_ids[:, None] == lane
    mark = same.astype(BF)
    far = jnp.where(same | (lane > PADDING), 0.0, FAR).astype(BF)
    g = jnp.where((segment_ids < PADDING)[:, None], cotangent, jnp.zeros_like(cotangent))
    offset = jnp.concatenate([in_bias[:, :d], jnp.zeros((1, d), F32), in_bias[:, d:]], axis=1)
    a1, qkv = project(inputs, w_in, gain1, shift1, offset)
    o, e, inv, *full = attend(qkv, mark, far, sizes, [out_weight, up_weight, down_weight] if own else [])
    w_out, w_up, w_down = (
        (f.reshape(-1, f.shape[-1]) for f in full) if own else (take(w) for w in (out_weight, up_weight, down_weight))
    )
    blank = jnp.zeros((1, d), F32)
    m1, a2, gm, gm_sum = middle(
        o, inputs, g, w_out, jnp.concatenate([out_bias, scale1, gain2, shift2, scale2, blank, blank, blank])
    )
    bm, ga2, d_up, d_down, ub_sum = feed(a2, gm, w_up, up_bias, w_down)
    outputs, gm1, go, d_out, join_sums = join(
        m1, bm, ga2, inputs, g, o, w_out, jnp.concatenate([down_bias, scale1, gain2, scale2, blank, blank, blank, blank])
    )
    gqkv, *done = attend_back(qkv, go, o, e, inv, sizes, [d_up, d_down, d_out] if own else [])
    d_up, d_down, d_out = done if own else (give(v) for v in (d_up, d_down, d_out))
    d_in, col_sums, gx, last_sums = finish(a1, gqkv, w_in, inputs, gm1, gain1)
    s = jnp.sum
    j = s(join_sums, axis=1)
    c = s(col_sums, axis=1)
    t = s(last_sums, axis=1)
    sums = [
        jnp.concatenate([c[0], c[2]]), j[4], t[0], t[1], j[3] / scale1[0],
        s(ub_sum, axis=0), s(gm_sum, axis=0), j[1], j[2], j[0],
    ]
    small = jnp.concatenate(sums).reshape(-1, d)
    small = jnp.pad(small, ((0, -small.shape[0] % 8), (0, 0)))
    if own:
        d_in, small = scatter_all(sizes, [d_in], small, 3)
    else:
        d_in, small = give(d_in), lax.psum(small, AXES)
    small = small.reshape(-1)
    here = lax.axis_index(AXES)
    out = []
    at = 0
    for v in sums:
        size = v.shape[0] // n
        out.append(lax.dynamic_slice(small, (at + here * size,), (size,)))
        at += v.shape[0]
    return (
        outputs, gx, d_in, out[0], d_out, out[1], out[2], out[3], out[4],
        d_up, out[5], d_down, out[6], out[7], out[8], out[9],
    )


def solution(mesh):
    wide, flat = P(AXES, None), P(AXES)
    return jax.shard_map(
        functools.partial(layer, mesh_sizes(mesh)),
        mesh=mesh,
        in_specs=(wide, flat, wide, wide, flat, wide, flat, flat, flat, flat, wide, flat, wide, flat, flat, flat, flat),
        out_specs=(wide, wide, wide, flat, wide, flat, flat, flat, flat, wide, flat, wide, flat, flat, flat, flat),
        check_vma=False,
    )
```

```python
import functools

import jax
import jax.numpy as jnp
from jax import lax
from jax.experimental import pallas as pl
from jax.experimental.pallas import tpu as pltpu
from jax.sharding import PartitionSpec as P

HD = 64
PADDING = 5
EPSILON = 1e-06
LOG2E = 1.4426950408889634
FAR = -1e30
BF = jnp.bfloat16
F32 = jnp.float32
AXES = ("dp", "fsdp")
VMEM_LIMIT = 62 * 1024 * 1024


def dot(a, b, da, db):
    return lax.dot_general(a, b, (((da,), (db,)), ((), ())), preferred_element_type=F32)


def params(**more):
    return pltpu.CompilerParams(vmem_limit_bytes=VMEM_LIMIT, **more)


def cost(flops, moved, special=0):
    return pl.CostEstimate(flops=int(flops), bytes_accessed=int(moved), transcendentals=int(special))


def whole(shape):
    return pl.BlockSpec(shape, lambda *_: (0,) * len(shape), pipeline_mode=pl.Buffered(1))


def row_loop(rows, size, body):
    def step(index, carry):
        body(pl.ds(pl.multiple_of(index * size, size), size))
        return carry

    lax.fori_loop(0, rows // size, step, 0)


def normalised(values):
    centred = values - jnp.mean(values, axis=-1, keepdims=True)
    spread = jnp.mean(centred * centred, axis=-1, keepdims=True)
    inverse = lax.rsqrt(spread + EPSILON)
    return centred * inverse, inverse


def norm_back(unit, inverse, scaled):
    return inverse * (
        scaled
        - jnp.mean(scaled, axis=-1, keepdims=True)
        - unit * jnp.mean(scaled * unit, axis=-1, keepdims=True)
    )


MESH = pl.DeviceIdType.MESH
ALL = slice(None)


class Near:
    def __init__(self, sizes):
        self.sizes = sizes
        dp, fsdp = lax.axis_index("dp"), lax.axis_index("fsdp")
        ny = sizes["y"]
        self.at = {"x": lax.div(dp, 2), "c": lax.rem(dp, 2), "z": lax.div(fsdp, ny), "y": lax.rem(fsdp, ny)}

    def along(self, axis, shift):
        return lax.rem(self.at[axis] + shift, self.sizes[axis])

    def device(self, axis, shift):
        at = {**self.at, axis: self.along(axis, shift)}
        return (at["x"] * 2 + at["c"], at["z"] * self.sizes["y"] + at["y"])

    def shifts(self, axis):
        return range(1, self.sizes[axis])

    def greet(self):
        barrier = pltpu.get_barrier_semaphore()
        count = 0
        for axis in "cxyz":
            for shift in self.shifts(axis):
                pl.semaphore_signal(barrier, inc=1, device_id=self.device(axis, shift), device_id_type=MESH)
                count += 1
        pl.semaphore_wait(barrier, count)


class Wires:
    def __init__(self, near, send, recv):
        self.near, self.send, self.recv, self.used = near, send, recv, 0

    def wire(self, src, dst, axis, shift):
        n = self.used
        self.used += 1
        return lambda: pltpu.make_async_remote_copy(
            src_ref=src, dst_ref=dst, send_sem=self.send.at[n], recv_sem=self.recv.at[n],
            device_id=self.near.device(axis, shift), device_id_type=MESH,
        )


def start(*groups):
    for group in groups:
        for wire in group:
            wire().start()


def landed(*groups):
    for group in groups:
        for wire in group:
            wire().wait_recv()


def left(*groups):
    for group in groups:
        for wire in group:
            wire().wait_send()


def halves(width, base=0):
    cut = (width // 256) * 128
    return pl.ds(base, cut), pl.ds(base + cut, width - cut)


def gather_wires(sizes):
    return sizes["z"] + 4 * (sizes["x"] + sizes["y"] - 2)


def gather_stages(near, mine, full, send, recv, own, base=0, width=None):
    wires = Wires(near, send, recv)
    at = near.at
    width = mine.shape[-1] if width is None else width
    every = pl.ds(base, width)
    mine = mine.at[:, every]

    def piece(cols, **fixed):
        return full.at[tuple(fixed.get(a, at[a]) for a in "xczy") + (ALL, cols)]

    def spread(axis, done, cols, src=None):
        here = piece(cols, **{a: ALL for a in done})
        return [wires.wire(here if src is None else src, here, axis, k) for k in near.shifts(axis)]

    def forward(axis, done, cols):
        size = near.sizes[axis]
        parts = [piece(cols, **{a: ALL for a in done}, **{axis: near.along(axis, size - k)}) for k in near.shifts(axis)]
        return [wires.wire(p, p, "c", 1) for p in parts]

    first, second = halves(width, base)
    whole_z = spread("z", "", every, mine)
    column = piece(every, z=ALL)
    pair = [wires.wire(column, column, "c", 1)]
    one, two, one_on, two_on = [], [], [], []
    for cols, (a, b) in ((first, "yx"), (second, "xy")):
        one += spread(a, "z", cols)
        one_on += forward(a, "z", cols)
        two += spread(b, "z" + a, cols)
        two_on += forward(b, "z" + a, cols)
    keep = lambda: pltpu.make_async_copy(mine, piece(every), own)

    def stage0():
        keep().start()
        start(whole_z)

    def stage1():
        keep().wait()
        landed(whole_z)
        start(one, pair)

    def stage2():
        landed(one)
        start(two, one_on)

    def stage3():
        landed(two)
        start(two_on)

    def stage4():
        left(whole_z, pair, one, two, one_on, two_on)
        landed(pair, one_on, two_on)

    return [stage0, stage1, stage2, stage3, stage4]


def gather_scratch(sizes):
    n = gather_wires(sizes)
    return [pltpu.SemaphoreType.DMA((n,)), pltpu.SemaphoreType.DMA((n,)), pltpu.SemaphoreType.DMA(())]


def lead(sizes):
    return (sizes["x"], 2, sizes["z"], sizes["y"])


def gathered(sizes, arrays):
    return [jax.ShapeDtypeStruct(lead(sizes) + a.shape, a.dtype) for a in arrays]


def scatter_wires(sizes):
    return 1 + 2 * (sizes["x"] + sizes["y"] - 2) + sizes["z"] - 1


SCATTER_REFS = 10


def scatter_scratch(sizes, block, width, kind):
    nx, ny, nz = sizes["x"], sizes["y"], sizes["z"]
    first, second = halves(width)
    a, b = first.size, second.size
    vmem = lambda *shape: pltpu.VMEM(shape, kind)
    n = scatter_wires(sizes)
    return [
        vmem(nx, nz, ny, block, width), vmem(nx, nz, ny, block, width),
        vmem(nx - 1, nz, ny, block, a), vmem(ny - 1, nx, nz, block, b),
        vmem(ny - 1, nz, block, a), vmem(nx - 1, nz, block, b),
        vmem(nz - 1, block, width),
        pltpu.SemaphoreType.DMA((n,)), pltpu.SemaphoreType.DMA((n,)), pltpu.SemaphoreType.DMA(()),
    ]


def scatter_stages(near, grad, out, held, got, x_first, y_first, y_then, x_then, z_last, send, recv, own):
    wires = Wires(near, send, recv)
    at, sizes = near.at, near.sizes
    nz, ny, nx = sizes["z"], sizes["y"], sizes["x"]
    x, y, z = at["x"], at["y"], at["z"]
    first, second = halves(held.shape[-1])
    loads = [] if own is None else [lambda: pltpu.make_async_copy(grad.at[:, at["c"]], held, own)]
    pair = [wires.wire(grad.at[:, 1 - at["c"]], got, "c", 1)]
    one = [wires.wire(held.at[near.along("x", k), :, :, :, first], x_first.at[k - 1], "x", k) for k in near.shifts("x")]
    one += [wires.wire(held.at[:, :, near.along("y", k), :, second], y_first.at[k - 1], "y", k) for k in near.shifts("y")]
    two = [wires.wire(held.at[x, :, near.along("y", k), :, first], y_then.at[k - 1], "y", k) for k in near.shifts("y")]
    two += [wires.wire(held.at[near.along("x", k), :, y, :, second], x_then.at[k - 1], "x", k) for k in near.shifts("x")]
    last = [wires.wire(held.at[x, near.along("z", k), y], z_last.at[k - 1], "z", k) for k in near.shifts("z")]

    def add(where, terms):
        held[where] = sum([t.astype(F32) for t in terms], held[where].astype(F32)).astype(held.dtype)

    def over_z(body):
        lax.fori_loop(0, nz, lambda i, carry: (body(i), carry)[1], 0)

    def stage0():
        start(pair, loads)

    def stage1():
        for load in loads:
            load().wait()
        landed(pair)

        @over_z
        def _(i):
            for a in range(nx):
                for b in range(ny):
                    if own is None:
                        held[a, i, b] = (grad[a, at["c"], i, b].astype(F32) + got[a, i, b].astype(F32)).astype(held.dtype)
                    else:
                        add((a, i, b), [got[a, i, b]])

        start(one)

    def stage2():
        landed(one)

        @over_z
        def _(i):
            for b in range(ny):
                add((x, i, b, ALL, first), [x_first[k - 1, i, b] for k in near.shifts("x")])
            for a in range(nx):
                add((a, i, y, ALL, second), [y_first[k - 1, a, i] for k in near.shifts("y")])

        start(two)

    def stage3():
        landed(two)

        @over_z
        def _(i):
            add((x, i, y, ALL, first), [y_then[k - 1, i] for k in near.shifts("y")])
            add((x, i, y, ALL, second), [x_then[k - 1, i] for k in near.shifts("x")])

        start(last)

    def stage4():
        landed(last)
        out[...] = sum([z_last[k - 1].astype(F32) for k in near.shifts("z")], held[x, z, y].astype(F32))
        left(pair, one, two, last)

    return [stage0, stage1, stage2, stage3, stage4]


def total_scratch(sizes, shape):
    n = sum(sizes[a] - 1 for a in "cxyz")
    return [pltpu.VMEM((n,) + shape, F32), pltpu.VMEM((3,) + shape, F32), pltpu.SemaphoreType.DMA((n,)), pltpu.SemaphoreType.DMA((n,))]


def total_stages(near, mine, out, got, held, send, recv):
    wires = Wires(near, send, recv)
    groups, slots = [], []
    for step, axis in enumerate("cxyz"):
        src = mine if step == 0 else held.at[step - 1]
        slots.append([wires.used + k - 1 for k in near.shifts(axis)])
        groups.append([wires.wire(src, got.at[wires.used], axis, k) for k in near.shifts(axis)])

    def stage(step):
        def run():
            if step > 0:
                landed(groups[step - 1])
                total = mine[...] if step == 1 else held[step - 2]
                for slot in slots[step - 1]:
                    total = total + got[slot]
                if step < 4:
                    held[step - 1] = total
                else:
                    out[...] = total
                    left(*groups)
            if step < 4:
                start(groups[step])

        return run

    return [stage(step) for step in range(5)]


def blocks_of(sizes, grads):
    return [g.reshape(lead(sizes) + (-1, g.shape[1])) for g in grads]


def pump(schedule, plans, chunk):
    for step in sorted({at[0] for at in schedule if at[1] == chunk}):

        @pl.when(pl.program_id(0) == step)
        def _():
            for plan, stage in schedule[step, chunk]:
                plans[plan][stage]()


def mesh_sizes(mesh):
    fsdp = mesh.shape["fsdp"]
    ny = 1 << ((fsdp.bit_length() - 1) // 2)
    return {"x": mesh.shape["dp"] // 2, "c": 2, "z": fsdp // ny, "y": ny}


def project_kernel(x_ref, w_ref, gain_ref, shift_ref, offset_ref, a1_ref, qkv_ref):
    @pl.when(pl.program_id(0) == 0)
    def _():
        def body(rows):
            unit, _ = normalised(x_ref[rows, :].astype(F32))
            a1_ref[rows, :] = (unit * gain_ref[...] + shift_ref[...]).astype(BF)

        row_loop(x_ref.shape[0], 352, body)

    qkv_ref[...] = (dot(a1_ref[...], w_ref[...], 1, 0) + offset_ref[...]).astype(BF)


def project(x, w_in, gain, shift, offset):
    rows, d = x.shape
    return pl.pallas_call(
        project_kernel,
        grid=(3,),
        in_specs=[
            whole((rows, d)),
            pl.BlockSpec((d, d), lambda t: (0, t)),
            whole((1, d)),
            whole((1, d)),
            pl.BlockSpec((1, d), lambda t: (0, t)),
        ],
        out_specs=[whole((rows, d)), pl.BlockSpec((rows, d), lambda t: (0, t))],
        out_shape=[
            jax.ShapeDtypeStruct((rows, d), BF),
            jax.ShapeDtypeStruct((rows, 3 * d), BF),
        ],
        compiler_params=params(),
        cost_estimate=cost(6 * rows * d * d, 2 * (5 * rows * d + 3 * d * d)),
        name="project",
    )(x, w_in, gain, shift, offset)


VEC_ROWS = 16
UP_ROW = 10


def placed(value, width, device):
    size = value.shape[-1]
    row = lax.broadcasted_iota(jnp.int32, (size, width), 0)
    column = lax.broadcasted_iota(jnp.int32, (size, width), 1)
    return dot(value, (column == row + device * size).astype(BF), 1, 0)


def enter_kernel(sizes, tile, x_ref, w_ref, *refs):
    vec_refs, (a1_out, qkv_out, w_out, vecs_ref) = refs[:10], refs[10:14]
    a1_ref, qkv_ref, w_full, unit_ref, mine_ref = refs[14:19]
    small_refs, gather_refs, out_sems = refs[19:23], refs[23:32], refs[32]
    rows, d = x_ref.shape
    near = Near(sizes)
    near.greet()
    device = lax.axis_index(AXES)
    mine_ref[...] = jnp.zeros_like(mine_ref)
    in_bias, *plain = vec_refs
    up_bias = plain.pop(4)
    for i, ref in enumerate(plain):
        mine_ref[i : i + 1, :] = placed(ref[...], d, device)
    both = placed(in_bias[...], 2 * d, device)
    mine_ref[8:9, :] = both[:, :d]
    mine_ref[9:10, :] = both[:, d:]
    up = placed(up_bias[...], 6 * 512, device)
    for i in range(6):
        mine_ref[UP_ROW + i : UP_ROW + i + 1, :512] = up[:, 512 * i : 512 * (i + 1)]
    plans = [
        gather_stages(near, w_ref, w_full, *gather_refs[3 * t : 3 * t + 3], base=d * t, width=d) for t in range(3)
    ]
    small = total_stages(near, mine_ref, vecs_ref, *small_refs)
    for plan in plans:
        plan[0]()

    def body(index, carry):
        span = pl.ds(pl.multiple_of(index * tile, tile), tile)
        unit_ref[span, :], _ = normalised(x_ref[span, :].astype(F32))
        for step in range(3):
            pl.when(index == step)(small[step])
        return carry

    lax.fori_loop(0, rows // tile, body, 0)
    plans[0][1]()
    small[3]()
    plans[1][1]()
    plans[0][2]()
    plans[2][1]()
    plans[1][2]()
    small[4]()

    def shifted(span):
        a1_ref[span, :] = (unit_ref[span, :] * vecs_ref[1:2, :] + vecs_ref[2:3, :]).astype(BF)

    row_loop(rows, tile, shifted)
    sends = [pltpu.make_async_copy(a1_ref, a1_out, out_sems.at[0])]
    sends[0].start()

    def third(t):
        cols = slice(d * t, d * (t + 1))
        w = w_full[:, :, :, :, :, cols].astype(F32).reshape(d, d).astype(BF)
        value = dot(a1_ref[...], w, 1, 0)
        if t != 1:
            value = value + vecs_ref[8 + t // 2 : 9 + t // 2, :]
        qkv_ref[:, cols] = value.astype(BF)

    def store(t):
        cols = pl.ds(d * t, d)
        sends.append(pltpu.make_async_copy(qkv_ref.at[:, cols], qkv_out.at[:, cols], out_sems.at[1 + t]))
        sends[-1].start()

    plans[0][3]()
    plans[2][2]()
    plans[0][4]()
    third(0)
    plans[1][3]()
    store(0)
    plans[1][4]()
    plans[2][3]()
    third(1)
    store(1)
    plans[2][4]()
    sends.append(pltpu.make_async_copy(w_full, w_out, out_sems.at[4]))
    sends[-1].start()
    third(2)
    store(2)
    for copy in sends:
        copy.wait()


def enter(sizes, x, w_in, vectors, tile=352):
    rows, d = x.shape
    vmem, hbm = pl.BlockSpec(memory_space=pltpu.VMEM), pl.BlockSpec(memory_space=pltpu.HBM)
    full = lead(sizes) + w_in.shape
    return pl.pallas_call(
        functools.partial(enter_kernel, sizes, tile),
        in_specs=[vmem] * 12,
        out_specs=[hbm, hbm, hbm, vmem],
        out_shape=[
            jax.ShapeDtypeStruct((rows, d), BF),
            jax.ShapeDtypeStruct((rows, 3 * d), BF),
            jax.ShapeDtypeStruct(full, BF),
            jax.ShapeDtypeStruct((VEC_ROWS, d), F32),
        ],
        scratch_shapes=[
            pltpu.VMEM((rows, d), BF),
            pltpu.VMEM((rows, 3 * d), BF),
            pltpu.VMEM(full, BF),
            pltpu.VMEM((rows, d), F32),
            pltpu.VMEM((VEC_ROWS, d), F32),
            *total_scratch(sizes, (VEC_ROWS, d)),
            *gather_scratch(sizes) * 3,
            pltpu.SemaphoreType.DMA((5,)),
        ],
        compiler_params=params(collective_id=0, has_side_effects=True),
        name="enter",
    )(x, w_in, *[v[None] for v in vectors])


def chunks(rows, size):
    return [(start, min(size, rows - start)) for start in range(0, rows, size)]


GATHER_AT = {
    (0, 0): [(0, 0), (1, 0)],
    (1, 0): [(0, 1), (2, 0)],
    (2, 0): [(1, 1), (0, 2)],
    (3, 0): [(2, 1), (1, 2), (0, 3)],
    (4, 0): [(2, 2)],
    (5, 0): [(1, 3)],
    (5, -1): [(2, 3), (0, 4), (1, 4), (2, 4)],
}


def attend_kernel(chunk, sizes, count, q_ref, k_ref, v_ref, mark_ref, far_ref, *refs):
    shards, (o_ref, e_ref, inv_ref) = refs[:count], refs[count : count + 3]
    full, (vt_ref, k2_ref), sems = refs[count + 3 : 2 * count + 3], refs[2 * count + 3 : 2 * count + 5], refs[2 * count + 5 :]
    rows = q_ref.shape[0]
    plans, schedule = [], {}
    if count:
        near, schedule = Near(sizes), GATHER_AT
        pl.when(pl.program_id(0) == 0)(near.greet)
        plans = [gather_stages(near, shards[i], full[i], *sems[3 * i : 3 * i + 3]) for i in range(count)]
    vt_ref[...] = v_ref[...].astype(F32).T.astype(BF)
    low = lax.broadcasted_iota(jnp.int32, (1, 128), 1) < HD
    for half in range(2):
        mine = low if half == 0 else jnp.logical_not(low)
        k2_ref[half] = jnp.where(mine, k_ref[...], far_ref[...])
    for turn, (start, size) in enumerate(chunks(rows, chunk)):
        pump(schedule, plans, turn)
        for half in range(2):
            mine = low if half == 0 else jnp.logical_not(low)
            span = pl.ds(start, size)
            query = jnp.where(mine, q_ref[span, :], mark_ref[span, :])
            scores = dot(k2_ref[half], query, 1, 1)
            top = jnp.max(scores, axis=0, keepdims=True)
            weights = jnp.exp2((scores - top) * (LOG2E * HD ** (-0.5)))
            total = jnp.sum(weights, axis=0, keepdims=True)
            weights_low = weights.astype(BF)
            e_ref[half, :, span] = weights_low
            inverse = 1.0 / total
            inv_ref[0, half : half + 1, span] = inverse
            head = pl.ds(half * HD, HD)
            o_ref[head, span] = (dot(vt_ref[head, :], weights_low, 1, 0) * inverse).astype(BF)
    pump(schedule, plans, -1)


def attend(qkv, mark, far, sizes, shards, chunk=256):
    count = len(shards)
    rows, width = qkv.shape
    pairs = width // 384
    return pl.pallas_call(
        functools.partial(attend_kernel, chunk, sizes, count),
        grid=(pairs,),
        in_specs=[
            pl.BlockSpec((rows, 128), lambda p: (0, p)),
            pl.BlockSpec((rows, 128), lambda p: (0, pairs + p)),
            pl.BlockSpec((rows, 128), lambda p: (0, 2 * pairs + p)),
            whole((rows, 128)),
            whole((rows, 128)),
            *[whole(a.shape) for a in shards],
        ],
        out_specs=[
            pl.BlockSpec((128, rows), lambda p: (p, 0)),
            pl.BlockSpec((2, rows, rows), lambda p: (p, 0, 0)),
            pl.BlockSpec((1, 2, rows), lambda p: (p, 0, 0)),
            *[pl.BlockSpec(memory_space=pltpu.HBM)] * count,
        ],
        out_shape=[
            jax.ShapeDtypeStruct((pairs * 128, rows), BF),
            jax.ShapeDtypeStruct((2 * pairs, rows, rows), BF),
            jax.ShapeDtypeStruct((pairs, 2, rows), F32),
            *(gathered(sizes, shards) if count else []),
        ],
        scratch_shapes=[
            pltpu.VMEM((128, rows), BF),
            pltpu.VMEM((2, rows, 128), BF),
            *(gather_scratch(sizes) * count if count else []),
        ],
        compiler_params=params(collective_id=1, has_side_effects=True) if count else params(),
        cost_estimate=cost(2 * pairs * 4 * rows * rows * 256, 4 * pairs * rows * rows, 2 * pairs * rows * rows),
        name="attend",
    )(qkv, qkv, qkv, mark, far, *shards)


def middle_kernel(o_ref, x_ref, g_ref, w_ref, vec_ref, m1_ref, a2_ref, gm_ref, gmsum_ref):
    bias, scale1, gain2, shift2, scale2 = (vec_ref[i : i + 1, :] for i in (0, 3, 5, 6, 7))
    m1_ref[...] = dot(o_ref[...], w_ref[...], 0, 0)
    gmsum_ref[...] = jnp.zeros_like(gmsum_ref)

    def body(rows):
        m1 = x_ref[rows, :].astype(F32) + scale1 * (m1_ref[rows, :] + bias)
        m1_ref[rows, :] = m1
        unit, _ = normalised(m1)
        a2_ref[rows, :] = (unit * gain2 + shift2).astype(BF)
        gm = (scale2 * g_ref[rows, :].astype(F32)).astype(BF)
        gm_ref[rows, :] = gm
        gmsum_ref[...] += jnp.sum(gm.astype(F32).reshape(-1, 8, gm.shape[-1]), axis=0)

    row_loop(x_ref.shape[0], 352, body)


def middle(o, x, g, w_out, vec):
    rows, d = x.shape
    return pl.pallas_call(
        middle_kernel,
        out_shape=[
            jax.ShapeDtypeStruct((rows, d), F32),
            jax.ShapeDtypeStruct((rows, d), BF),
            jax.ShapeDtypeStruct((rows, d), BF),
            jax.ShapeDtypeStruct((8, d), F32),
        ],
        compiler_params=params(),
        cost_estimate=cost(2 * rows * d * d, 14 * rows * d),
        name="middle",
    )(o, x, g, w_out, vec)


def gelu_parts(u):
    near = jnp.abs(u)
    t = 1.0 / (1.0 + (0.3275911 * 0.7071067811865476) * near)
    bell = jnp.exp2((-0.5 * LOG2E) * (u * u))
    poly = t * (
        0.5 * 0.254829592
        + t * (0.5 * -0.284496736 + t * (0.5 * 1.421413741 + t * (0.5 * -1.453152027 + t * (0.5 * 1.061405429))))
    )
    tail = poly * bell
    phi = jnp.where(u < 0, tail, 1.0 - tail)
    return u * phi, phi + u * bell * 0.3989422804014327


def feed_kernel(chunk, a2_ref, gm_ref, up_ref, vec_ref, down_ref, bm_ref, ga_ref, dup_ref, ddown_ref, dub_ref, gl_ref, gu_ref):
    first = pl.program_id(0) == 0

    @pl.when(first)
    def _():
        bm_ref[...] = jnp.zeros_like(bm_ref)
        ga_ref[...] = jnp.zeros_like(ga_ref)

    bias = vec_ref[pl.ds(UP_ROW + pl.program_id(0), 1), : up_ref.shape[-1]]
    total = jnp.zeros((8, up_ref.shape[-1]), F32)
    for start, size in chunks(a2_ref.shape[0], chunk):
        rows = pl.ds(start, size)
        u = dot(a2_ref[rows, :], up_ref[...], 1, 0) + bias
        back = dot(gm_ref[rows, :], down_ref[...], 1, 1)
        active, slope = gelu_parts(u)
        low = active.astype(BF)
        gl_ref[rows, :] = low
        gu = (slope * back).astype(BF)
        gu_ref[rows, :] = gu
        total += jnp.sum(gu.astype(F32).reshape(-1, 8, gu.shape[-1]), axis=0)
        bm_ref[rows, :] += dot(low, down_ref[...], 1, 0)
        ga_ref[rows, :] += dot(gu, up_ref[...], 1, 1)
    dub_ref[...] = total
    ddown_ref[...] = dot(gl_ref[...], gm_ref[...], 0, 0).astype(ddown_ref.dtype)
    dup_ref[...] = dot(a2_ref[...], gu_ref[...], 0, 0).astype(dup_ref.dtype)


def feed(a2, gm, w_up, vecs, w_down, block=512, chunk=704, kind=BF):
    rows, d = a2.shape
    ff = w_up.shape[1]
    return pl.pallas_call(
        functools.partial(feed_kernel, chunk),
        grid=(ff // block,),
        in_specs=[
            whole((rows, d)),
            whole((rows, d)),
            pl.BlockSpec((d, block), lambda f: (0, f)),
            whole((VEC_ROWS, d)),
            pl.BlockSpec((block, d), lambda f: (f, 0)),
        ],
        out_specs=[
            whole((rows, d)),
            whole((rows, d)),
            pl.BlockSpec((d, block), lambda f: (0, f)),
            pl.BlockSpec((block, d), lambda f: (f, 0)),
            pl.BlockSpec((8, block), lambda f: (0, f)),
        ],
        out_shape=[
            jax.ShapeDtypeStruct((rows, d), F32),
            jax.ShapeDtypeStruct((rows, d), F32),
            jax.ShapeDtypeStruct((d, ff), kind),
            jax.ShapeDtypeStruct((ff, d), kind),
            jax.ShapeDtypeStruct((8, ff), F32),
        ],
        scratch_shapes=[pltpu.VMEM((rows, block), BF), pltpu.VMEM((rows, block), BF)],
        compiler_params=params(),
        cost_estimate=cost(12 * rows * d * ff, 4 * 4 * d * ff),
        name="feed",
    )(a2, gm, w_up, vecs, w_down)


def join_kernel(size, m1_ref, bm_ref, ga_ref, x_ref, g_ref, o_ref, w_ref, vec_ref, out_ref, gm1_ref, go_ref, dout_ref, sums_ref, gb_ref):
    bias2, scale1, gain2, scale2 = (vec_ref[i : i + 1, :] for i in (4, 3, 5, 7))
    step = pl.program_id(0)

    @pl.when(step == 0)
    def _():
        sums_ref[...] = jnp.zeros_like(sums_ref)

    base = step * m1_ref.shape[0]

    def body(rows):
        m1 = m1_ref[rows, :]
        bm = bm_ref[rows, :] + bias2
        g = g_ref[rows, :].astype(F32)
        out_ref[rows, :] = (m1 + scale2 * bm).astype(BF)
        unit, inverse = normalised(m1)
        ga = ga_ref[rows, :]
        gm1 = g + norm_back(unit, inverse, ga * gain2)
        gm1_ref[rows, :] = gm1
        gb = (scale1 * gm1).astype(BF)
        gb_ref[pl.ds(pl.multiple_of(base + rows.start, size), size), :] = gb
        for index, value in enumerate(
            (g * bm, ga * unit, ga, gm1 * (m1 - x_ref[rows, :].astype(F32)), gb.astype(F32))
        ):
            sums_ref[index] += jnp.sum(value.reshape(-1, 8, value.shape[-1]), axis=0)

    row_loop(m1_ref.shape[0], size, body)

    @pl.when(step == pl.num_programs(0) - 1)
    def _():
        go_ref[...] = dot(w_ref[...], gb_ref[...], 1, 1).astype(BF)
        dout_ref[...] = dot(o_ref[...], gb_ref[...], 1, 0).astype(dout_ref.dtype)


def join(m1, bm, ga, x, g, o, w_out, vec, tile=352, kind=BF):
    rows, d = x.shape
    by_rows = pl.BlockSpec((tile, d), lambda i: (i, 0))
    return pl.pallas_call(
        functools.partial(join_kernel, 352),
        grid=(rows // tile,),
        in_specs=[by_rows] * 5 + [whole((d, rows)), whole((d, d)), whole((VEC_ROWS, d))],
        out_specs=[by_rows, by_rows, whole((d, rows)), whole((d, d)), whole((5, 8, d))],
        out_shape=[
            jax.ShapeDtypeStruct((rows, d), BF),
            jax.ShapeDtypeStruct((rows, d), F32),
            jax.ShapeDtypeStruct((d, rows), BF),
            jax.ShapeDtypeStruct((d, d), kind),
            jax.ShapeDtypeStruct((5, 8, d), F32),
        ],
        scratch_shapes=[pltpu.VMEM((rows, d), BF)],
        compiler_params=params(),
        cost_estimate=cost(4 * rows * d * d, 26 * rows * d),
        name="join",
    )(m1, bm, ga, x, g, o, w_out, vec)


SCATTER_AT = {
    (0, 0): [(0, 0), (1, 0)],
    (1, 0): [(0, 1), (2, 0)],
    (2, 0): [(0, 2), (1, 1)],
    (3, 0): [(0, 3), (2, 1)],
    (4, 0): [(1, 2), (2, 2)],
    (5, 0): [(1, 3), (2, 3), (0, 4)],
    (5, -1): [(1, 4), (2, 4)],
}


def attend_back_kernel(chunk, sizes, count, q_ref, k_ref, v_ref, go_ref, o_ref, e_ref, inv_ref, *refs):
    grads, out_ref, sums = refs[:count], refs[count], refs[count + 1 : 2 * count + 1]
    (kt_ref, gq_ref, gs_ref, gp_ref), rest = refs[2 * count + 1 : 2 * count + 5], refs[2 * count + 5 :]
    rows = q_ref.shape[0]
    plans, schedule = [], {}
    if count:
        near, schedule = Near(sizes), SCATTER_AT
        pl.when(pl.program_id(0) == 0)(near.greet)
        plans = [
            scatter_stages(near, grads[i], sums[i], *rest[SCATTER_REFS * i : SCATTER_REFS * (i + 1)]) for i in range(count)
        ]
    factor = HD ** (-0.5)
    kt_ref[...] = k_ref[...].astype(F32).T.astype(BF)
    low = lax.broadcasted_iota(jnp.int32, (1, 128), 1) < HD
    below = lax.broadcasted_iota(jnp.int32, (128, 1), 0) < HD
    gp_ref[...] = jnp.zeros_like(gp_ref)
    for turn, (start, size) in enumerate(chunks(rows, chunk)):
        pump(schedule, plans, turn)
        span = pl.ds(start, size)
        for half in range(2):
            head = pl.ds(half * HD, HD)
            incoming = go_ref[head, span].astype(F32) * inv_ref[0, half : half + 1, span]
            centre = jnp.sum(incoming * o_ref[head, span].astype(F32), axis=0, keepdims=True)
            gp_ref[half, head, span] = incoming.astype(BF)
            gp = dot(v_ref[...], gp_ref[half, :, span], 1, 0)
            gs = (e_ref[half, :, span].astype(F32) * (gp - centre)).astype(BF)
            gs_ref[half, :, span] = gs
            gq_ref[head, span] = dot(kt_ref[head, :], gs, 1, 0) * factor
    out_ref[0] = gq_ref[...].T.astype(BF)
    gk = [dot(gs_ref[half], q_ref[...], 1, 0) for half in range(2)]
    out_ref[1] = (jnp.where(low, gk[0], gk[1]) * factor).astype(BF)
    out_ref[2] = (dot(e_ref[0], gp_ref[0], 1, 1) + dot(e_ref[1], gp_ref[1], 1, 1)).astype(BF)
    pump(schedule, plans, -1)


def attend_back(qkv, go, o, e, inv, sizes, grads, chunk=256):
    blocks = blocks_of(sizes, grads) if grads else []
    count = len(blocks)
    rows, width = qkv.shape
    pairs = width // 384
    return pl.pallas_call(
        functools.partial(attend_back_kernel, chunk, sizes, count),
        grid=(pairs,),
        in_specs=[
            pl.BlockSpec((rows, 128), lambda p: (0, p)),
            pl.BlockSpec((rows, 128), lambda p: (0, pairs + p)),
            pl.BlockSpec((rows, 128), lambda p: (0, 2 * pairs + p)),
            pl.BlockSpec((128, rows), lambda p: (p, 0)),
            pl.BlockSpec((128, rows), lambda p: (p, 0)),
            pl.BlockSpec((2, rows, rows), lambda p: (p, 0, 0)),
            pl.BlockSpec((1, 2, rows), lambda p: (p, 0, 0)),
            *[pl.BlockSpec(memory_space=pltpu.HBM)] * count,
        ],
        out_specs=[pl.BlockSpec((3, rows, 128), lambda p: (0, 0, p)), *[whole(b.shape[-2:]) for b in blocks]],
        out_shape=[
            jax.ShapeDtypeStruct((3, rows, pairs * 128), BF),
            *[jax.ShapeDtypeStruct(b.shape[-2:], F32) for b in blocks],
        ],
        scratch_shapes=[
            pltpu.VMEM((128, rows), BF),
            pltpu.VMEM((128, rows), F32),
            pltpu.VMEM((2, rows, rows), BF),
            pltpu.VMEM((2, 128, rows), BF),
            *[s for b in blocks for s in scatter_scratch(sizes, *b.shape[-2:], b.dtype)],
        ],
        compiler_params=params(collective_id=2, has_side_effects=True) if count else params(),
        cost_estimate=cost(2 * pairs * 8 * rows * rows * 256, 4 * pairs * rows * rows),
        name="attend_back",
    )(qkv, qkv, qkv, go, o, e, inv, *blocks)


def finish_kernel(a1_ref, gqkv_ref, w_ref, x_ref, gm1_ref, gain_ref, dw_ref, cols_ref, gx_ref, sums_ref, ga_ref):
    step = pl.program_id(0)
    grads = gqkv_ref[0]
    dw_ref[...] = dot(a1_ref[...], grads, 0, 0).astype(dw_ref.dtype)
    cols_ref[0] = jnp.sum(grads.astype(F32).reshape(-1, 8, grads.shape[-1]), axis=0)
    part = dot(grads, w_ref[...], 1, 1)

    @pl.when(step == 0)
    def _():
        ga_ref[...] = part

    @pl.when(step > 0)
    def _():
        ga_ref[...] += part

    @pl.when(step == pl.num_programs(0) - 1)
    def _():
        sums_ref[...] = jnp.zeros_like(sums_ref)

        def body(rows):
            unit, inverse = normalised(x_ref[rows, :].astype(F32))
            ga = ga_ref[rows, :]
            gx_ref[rows, :] = gm1_ref[rows, :] + norm_back(unit, inverse, ga * gain_ref[...])
            for index, value in enumerate((ga * unit, ga)):
                sums_ref[index] += jnp.sum(value.reshape(-1, 8, value.shape[-1]), axis=0)

        row_loop(x_ref.shape[0], 352, body)


def finish(a1, gqkv, w_in, x, gm1, gain, kind=BF):
    rows, d = x.shape
    return pl.pallas_call(
        finish_kernel,
        grid=(3,),
        in_specs=[
            whole((rows, d)),
            pl.BlockSpec((1, rows, d), lambda t: (t, 0, 0)),
            pl.BlockSpec((d, d), lambda t: (0, t)),
            whole((rows, d)),
            whole((rows, d)),
            whole((1, d)),
        ],
        out_specs=[
            pl.BlockSpec((d, d), lambda t: (0, t)),
            pl.BlockSpec((1, 8, d), lambda t: (t, 0, 0)),
            whole((rows, d)),
            whole((2, 8, d)),
        ],
        out_shape=[
            jax.ShapeDtypeStruct((d, 3 * d), kind),
            jax.ShapeDtypeStruct((3, 8, d), F32),
            jax.ShapeDtypeStruct((rows, d), F32),
            jax.ShapeDtypeStruct((2, 8, d), F32),
        ],
        scratch_shapes=[pltpu.VMEM((rows, d), F32)],
        compiler_params=params(),
        cost_estimate=cost(12 * rows * d * d, 20 * rows * d),
        name="finish",
    )(a1, gqkv, w_in, x, gm1, gain)


def leave_kernel(sizes, tile, a1_in, gqkv_in, w_in, x_in, gm1_in, vec_ref, join_ref, ub_ref, gmsum_ref, gx_out, dw_ref, early_ref, late_ref, *refs):
    a1_ref, gqkv_ref, w_ref, x_ref, gm1_ref, gx_ref, ga_ref, sums_ref, mine_ref, last_ref = refs[:10]
    grad_refs, refs = refs[10:13], refs[13:]
    scatter_refs, refs = [refs[9 * t : 9 * t + 9] for t in range(3)], refs[27:]
    early_refs, late_refs, in_sems, out_sems = refs[:4], refs[4:8], refs[8], refs[9]
    rows, d = x_in.shape
    count = rows // tile
    moves = [(a1_in, a1_ref), *[(gqkv_in.at[t], gqkv_ref.at[t]) for t in range(3)], (w_in, w_ref), (x_in, x_ref), (gm1_in, gm1_ref)]
    fetch = [pltpu.make_async_copy(src, dst, in_sems.at[n]) for n, (src, dst) in enumerate(moves)]
    for copy in fetch:
        copy.start()
    near = Near(sizes)
    near.greet()
    row = lambda value: jnp.sum(value, axis=0, keepdims=True)
    mine_ref[...] = jnp.zeros_like(mine_ref)
    for i, value in enumerate(
        (row(join_ref[4]), row(join_ref[3]) / vec_ref[3:4, :], row(gmsum_ref[...]), row(join_ref[1]), row(join_ref[2]), row(join_ref[0]))
    ):
        mine_ref[i : i + 1, :] = value
    for i in range(4):
        mine_ref[8 + i : 9 + i, :] = row(ub_ref[:, d * i : d * (i + 1)])
    plans = [
        scatter_stages(near, grad_refs[t], dw_ref.at[:, pl.ds(d * t, d)], *scatter_refs[t], None) for t in range(3)
    ]
    early = total_stages(near, mine_ref, early_ref, *early_refs)
    late = total_stages(near, last_ref, late_ref, *late_refs)
    last_ref[...] = jnp.zeros_like(last_ref)

    def weight(t):
        fetch[1 + t].wait()
        value = dot(a1_ref[...], gqkv_ref[t], 0, 0)
        grad_refs[t][...] = value.reshape(grad_refs[t].shape).astype(BF)

    def back(t):
        part = dot(gqkv_ref[t], w_ref[:, d * t : d * (t + 1)], 1, 1)
        if t == 0:
            ga_ref[...] = part
        else:
            ga_ref[...] += part
        if t != 1:
            total = jnp.zeros((1, d), F32)
            for start_row, size in chunks(rows, tile):
                total += row(gqkv_ref[t, pl.ds(start_row, size), :].astype(F32))
            last_ref[2 + t // 2 : 3 + t // 2, :] = total

    fetch[0].wait()
    weight(0)
    early[0]()
    plans[0][0]()
    weight(1)
    plans[0][1]()
    plans[1][0]()
    early[1]()
    weight(2)
    plans[1][1]()
    plans[2][0]()
    fetch[4].wait()
    back(0)
    plans[0][2]()
    plans[2][1]()
    early[2]()
    back(1)
    plans[1][2]()
    back(2)
    plans[0][3]()
    early[3]()
    fetch[5].wait()
    fetch[6].wait()
    sums_ref[...] = jnp.zeros_like(sums_ref)

    def send(index):
        span = pl.ds(pl.multiple_of(index * tile, tile), tile)
        return pltpu.make_async_copy(gx_ref.at[span], gx_out.at[span], out_sems.at[index])

    between = [[], [plans[2][2], plans[1][3]], []]

    def body(index, carry):
        span = pl.ds(pl.multiple_of(index * tile, tile), tile)
        unit, inverse = normalised(x_ref[span, :].astype(F32))
        ga = ga_ref[span, :]
        gx_ref[span, :] = gm1_ref[span, :] + norm_back(unit, inverse, ga * vec_ref[1:2, :])
        for n, value in enumerate((ga * unit, ga)):
            sums_ref[n] += jnp.sum(value.reshape(-1, 8, d), axis=0)
        for n, stages in enumerate(between):

            @pl.when(index == n)
            def _():
                for stage in stages:
                    stage()

        pl.when(index > 0)(lambda: send(index - 1).start())
        return carry

    lax.fori_loop(0, count, body, 0)
    for n in range(2):
        last_ref[n : n + 1, :] = row(sums_ref[n])
    late[0]()
    send(count - 1).start()
    early[4]()
    plans[2][3]()
    late[1]()
    plans[0][4]()
    late[2]()
    plans[1][4]()
    late[3]()
    plans[2][4]()
    late[4]()
    for index in range(count):
        send(index).wait()


def leave(sizes, a1, gqkv, w_in, x, gm1, vecs, join_sums, ub_sum, gm_sum, tile=352):
    rows, d = x.shape
    vmem, hbm = pl.BlockSpec(memory_space=pltpu.VMEM), pl.BlockSpec(memory_space=pltpu.HBM)
    block = d // (sizes["x"] * 2 * sizes["z"] * sizes["y"])
    return pl.pallas_call(
        functools.partial(leave_kernel, sizes, tile),
        in_specs=[hbm] * 5 + [vmem] * 4,
        out_specs=[hbm, vmem, vmem, vmem],
        out_shape=[
            jax.ShapeDtypeStruct((rows, d), F32),
            jax.ShapeDtypeStruct((block, 3 * d), F32),
            jax.ShapeDtypeStruct((16, d), F32),
            jax.ShapeDtypeStruct((8, d), F32),
        ],
        scratch_shapes=[
            pltpu.VMEM((rows, d), BF),
            pltpu.VMEM((3, rows, d), BF),
            pltpu.VMEM((d, 3 * d), BF),
            pltpu.VMEM((rows, d), BF),
            pltpu.VMEM((rows, d), F32),
            pltpu.VMEM((rows, d), F32),
            pltpu.VMEM((rows, d), F32),
            pltpu.VMEM((2, 8, d), F32),
            pltpu.VMEM((16, d), F32),
            pltpu.VMEM((8, d), F32),
            *[pltpu.VMEM(lead(sizes) + (block, d), BF)] * 3,
            *scatter_scratch(sizes, block, d, BF)[:-1] * 3,
            *total_scratch(sizes, (16, d)),
            *total_scratch(sizes, (8, d)),
            pltpu.SemaphoreType.DMA((7,)),
            pltpu.SemaphoreType.DMA((rows // tile,)),
        ],
        compiler_params=params(collective_id=3, has_side_effects=True),
        name="leave",
    )(a1, gqkv, w_in, x, gm1, vecs, join_sums, ub_sum, gm_sum)


def share_kernel(early_ref, late_ref, *refs):
    grads, outs, vec_outs = refs[:4], refs[4:8], refs[8:]
    for src, dst in zip(grads, outs):
        dst[...] = src[...]
    device = lax.axis_index(AXES)
    d = early_ref.shape[-1]

    def entries(ref, first_row, size):
        at = device * size
        line = ref[pl.ds(first_row + lax.div(at, d), 1), :]
        return pltpu.roll(jnp.broadcast_to(line, (8, d)), lax.rem(d - lax.rem(at, d), d), 1)[:1, :size]

    spots = [
        (late_ref, 2), (early_ref, 0), (late_ref, 0), (late_ref, 1), (early_ref, 1),
        (early_ref, 8), (early_ref, 2), (early_ref, 3), (early_ref, 4), (early_ref, 5),
    ]
    for (ref, first_row), out in zip(spots, vec_outs):
        out[...] = entries(ref, first_row, out.shape[-1])


def share(early, late, grads, sizes):
    vmem = pl.BlockSpec(memory_space=pltpu.VMEM)
    return pl.pallas_call(
        share_kernel,
        in_specs=[vmem] * 6,
        out_specs=[vmem] * 14,
        out_shape=[jax.ShapeDtypeStruct(g.shape, F32) for g in grads] + [jax.ShapeDtypeStruct((1, n), F32) for n in sizes],
        compiler_params=params(),
        name="share",
    )(early, late, *grads)


def take(a):
    return lax.all_gather(a, AXES, axis=0, tiled=True)


def give(g):
    return lax.psum_scatter(g, AXES, scatter_dimension=0, tiled=True).astype(F32)


def layer(
    sizes, inputs, segment_ids, cotangent, in_weight, in_bias, out_weight, out_bias, first_gain, first_shift, first_scale,
    up_weight, up_bias, down_weight, down_bias, second_gain, second_shift, second_scale,
):
    rows, d = inputs.shape
    vectors = (
        in_bias, out_bias, first_gain, first_shift, first_scale,
        up_bias, down_bias, second_gain, second_shift, second_scale,
    )
    own = all(w.shape[0] % 8 == 0 for w in (in_weight, out_weight, up_weight, down_weight))
    if own:
        a1, qkv, w_in, vecs = enter(sizes, inputs, in_weight, vectors)
        w_in = w_in.reshape(d, 3 * d)
    else:
        w_in = take(in_weight)
        row = lambda v: take(v).astype(F32).reshape(-1, d)
        vecs = jnp.concatenate(
            [row(v) for v in (out_bias, first_gain, first_shift, first_scale, down_bias, second_gain, second_shift, second_scale, in_bias)]
            + [jnp.pad(take(up_bias).astype(F32).reshape(6, 512), ((0, 0), (0, d - 512)))]
        )
        offset = jnp.concatenate([vecs[8:9], jnp.zeros((1, d), F32), vecs[9:10]], axis=1)
        a1, qkv = project(inputs, w_in, vecs[1:2], vecs[2:3], offset)
    lane = lax.broadcasted_iota(jnp.int32, (1, 128), 1) % HD
    same = segment_ids[:, None] == lane
    mark = same.astype(BF)
    far = jnp.where(same | (lane > PADDING), 0.0, FAR).astype(BF)
    g = jnp.where((segment_ids < PADDING)[:, None], cotangent, jnp.zeros_like(cotangent))
    o, e, inv, *full = attend(qkv, mark, far, sizes, [out_weight, up_weight, down_weight] if own else [])
    w_out, w_up, w_down = (
        (f.reshape(-1, f.shape[-1]) for f in full) if own else (take(w) for w in (out_weight, up_weight, down_weight))
    )
    m1, a2, gm, gm_sum = middle(o, inputs, g, w_out, vecs)
    bm, ga2, d_up, d_down, ub_sum = feed(a2, gm, w_up, vecs, w_down)
    outputs, gm1, go, d_out, join_sums = join(m1, bm, ga2, inputs, g, o, w_out, vecs)
    gqkv, *done = attend_back(qkv, go, o, e, inv, sizes, [d_up, d_down, d_out] if own else [])
    if own:
        gx, d_in, early, late = leave(sizes, a1, gqkv, w_in, inputs, gm1, vecs, join_sums, ub_sum, gm_sum)
        d_up, d_down, d_out, d_in, *out = share(early, late, [*done, d_in], [v.shape[0] for v in vectors])
        out = [v.reshape(-1) for v in out]
    else:
        d_in, col_sums, gx, last_sums = finish(a1, gqkv, w_in, inputs, gm1, vecs[1:2])
        d_in, d_up, d_down, d_out = (give(v) for v in (d_in, d_up, d_down, d_out))
        s = jnp.sum
        j, c, t = (s(v, axis=1) for v in (join_sums, col_sums, last_sums))
        sums = (
            jnp.concatenate([c[0], c[2]]), j[4], t[0], t[1], j[3] / vecs[3], s(ub_sum, axis=0), s(gm_sum, axis=0), j[1], j[2], j[0],
        )
        out = [give(v) for v in sums]
    return (
        outputs, gx, d_in, out[0], d_out, out[1], out[2], out[3], out[4],
        d_up, out[5], d_down, out[6], out[7], out[8], out[9],
    )


def solution(mesh):
    wide, flat = P(AXES, None), P(AXES)
    return jax.shard_map(
        functools.partial(layer, mesh_sizes(mesh)),
        mesh=mesh,
        in_specs=(wide, flat, wide, wide, flat, wide, flat, flat, flat, flat, wide, flat, wide, flat, flat, flat, flat),
        out_specs=(wide, wide, wide, flat, wide, flat, flat, flat, flat, wide, flat, wide, flat, flat, flat, flat),
        check_vma=False,
    )
```

```python
import functools

import jax
import jax.numpy as jnp
from jax import lax
from jax.experimental import pallas as pl
from jax.experimental.pallas import tpu as pltpu
from jax.sharding import PartitionSpec as P

HD = 64
PADDING = 5
EPSILON = 1e-06
LOG2E = 1.4426950408889634
FAR = -1e30
BF = jnp.bfloat16
F32 = jnp.float32
AXES = ("dp", "fsdp")
VMEM_LIMIT = 62 * 1024 * 1024


def dot(a, b, da, db):
    return lax.dot_general(a, b, (((da,), (db,)), ((), ())), preferred_element_type=F32)


def params(**more):
    return pltpu.CompilerParams(vmem_limit_bytes=VMEM_LIMIT, **more)


def cost(flops, moved, special=0):
    return pl.CostEstimate(flops=int(flops), bytes_accessed=int(moved), transcendentals=int(special))


def whole(shape):
    return pl.BlockSpec(shape, lambda *_: (0,) * len(shape), pipeline_mode=pl.Buffered(1))


def row_loop(rows, size, body):
    def step(index, carry):
        body(pl.ds(pl.multiple_of(index * size, size), size))
        return carry

    lax.fori_loop(0, rows // size, step, 0)


def normalised(values):
    centred = values - jnp.mean(values, axis=-1, keepdims=True)
    spread = jnp.mean(centred * centred, axis=-1, keepdims=True)
    inverse = lax.rsqrt(spread + EPSILON)
    return centred * inverse, inverse


def norm_back(unit, inverse, scaled):
    return inverse * (
        scaled
        - jnp.mean(scaled, axis=-1, keepdims=True)
        - unit * jnp.mean(scaled * unit, axis=-1, keepdims=True)
    )


MESH = pl.DeviceIdType.MESH
ALL = slice(None)


class Near:
    def __init__(self, sizes):
        self.sizes = sizes
        dp, fsdp = lax.axis_index("dp"), lax.axis_index("fsdp")
        ny = sizes["y"]
        self.at = {"x": lax.div(dp, 2), "c": lax.rem(dp, 2), "z": lax.div(fsdp, ny), "y": lax.rem(fsdp, ny)}

    def along(self, axis, shift):
        return lax.rem(self.at[axis] + shift, self.sizes[axis])

    def device(self, axis, shift):
        at = {**self.at, axis: self.along(axis, shift)}
        return (at["x"] * 2 + at["c"], at["z"] * self.sizes["y"] + at["y"])

    def shifts(self, axis):
        return range(1, self.sizes[axis])

    def greet(self):
        barrier = pltpu.get_barrier_semaphore()
        count = 0
        for axis in "cxyz":
            for shift in self.shifts(axis):
                pl.semaphore_signal(barrier, inc=1, device_id=self.device(axis, shift), device_id_type=MESH)
                count += 1
        pl.semaphore_wait(barrier, count)


class Wires:
    def __init__(self, near, send, recv):
        self.near, self.send, self.recv, self.used = near, send, recv, 0

    def wire(self, src, dst, axis, shift):
        n = self.used
        self.used += 1
        return lambda: pltpu.make_async_remote_copy(
            src_ref=src, dst_ref=dst, send_sem=self.send.at[n], recv_sem=self.recv.at[n],
            device_id=self.near.device(axis, shift), device_id_type=MESH,
        )


def start(*groups):
    for group in groups:
        for wire in group:
            wire().start()


def landed(*groups):
    for group in groups:
        for wire in group:
            wire().wait_recv()


def left(*groups):
    for group in groups:
        for wire in group:
            wire().wait_send()


def halves(width, base=0):
    cut = (width // 256) * 128
    return pl.ds(base, cut), pl.ds(base + cut, width - cut)


def gather_wires(sizes):
    return sizes["z"] + 4 * (sizes["x"] + sizes["y"] - 2)


def gather_stages(near, mine, full, send, recv, own, base=0, width=None, part="all"):
    wires = Wires(near, send, recv)
    at = near.at
    width = full.shape[-1] if width is None else width
    every = pl.ds(base, width)
    if part != "rest":
        mine = mine.at[:, every]

    def piece(cols, **fixed):
        return full.at[tuple(fixed.get(a, at[a]) for a in "xczy") + (ALL, cols)]

    def spread(axis, done, cols, src=None):
        here = piece(cols, **{a: ALL for a in done})
        return [wires.wire(here if src is None else src, here, axis, k) for k in near.shifts(axis)]

    def forward(axis, done, cols):
        size = near.sizes[axis]
        parts = [piece(cols, **{a: ALL for a in done}, **{axis: near.along(axis, size - k)}) for k in near.shifts(axis)]
        return [wires.wire(p, p, "c", 1) for p in parts]

    first, second = halves(width, base)
    whole_z = [] if part == "rest" else spread("z", "", every, mine)
    column = piece(every, z=ALL)
    pair = [wires.wire(column, column, "c", 1)]
    one, two, one_on, two_on = [], [], [], []
    for cols, (a, b) in ((first, "yx"), (second, "xy")):
        one += spread(a, "z", cols)
        one_on += forward(a, "z", cols)
        two += spread(b, "z" + a, cols)
        two_on += forward(b, "z" + a, cols)
    keep = lambda: pltpu.make_async_copy(mine, piece(every), own)

    def stage0():
        keep().start()
        start(whole_z)

    def arrive():
        keep().wait()
        landed(whole_z)
        left(whole_z)

    def stage1():
        if part != "rest":
            arrive()
        start(one, pair)

    def stage2():
        landed(one)
        start(two, one_on)

    def stage3():
        landed(two)
        start(two_on)

    def stage4():
        left(pair, one, two, one_on, two_on)
        landed(pair, one_on, two_on)

    return [stage0, arrive] if part == "first" else [stage0, stage1, stage2, stage3, stage4]


def gather_scratch(sizes):
    n = gather_wires(sizes)
    return [pltpu.SemaphoreType.DMA((n,)), pltpu.SemaphoreType.DMA((n,)), pltpu.SemaphoreType.DMA(())]


def lead(sizes):
    return (sizes["x"], 2, sizes["z"], sizes["y"])


def gathered(sizes, arrays):
    return [jax.ShapeDtypeStruct(lead(sizes) + a.shape, a.dtype) for a in arrays]


def scatter_wires(sizes):
    return 1 + 2 * (sizes["x"] + sizes["y"] - 2) + sizes["z"] - 1


SCATTER_REFS = 10


def scatter_scratch(sizes, block, width, kind):
    nx, ny, nz = sizes["x"], sizes["y"], sizes["z"]
    first, second = halves(width)
    a, b = first.size, second.size
    vmem = lambda *shape: pltpu.VMEM(shape, kind)
    n = scatter_wires(sizes)
    return [
        vmem(nx, nz, ny, block, width), vmem(nx, nz, ny, block, width),
        vmem(nx - 1, nz, ny, block, a), vmem(ny - 1, nx, nz, block, b),
        vmem(ny - 1, nz, block, a), vmem(nx - 1, nz, block, b),
        vmem(nz - 1, block, width),
        pltpu.SemaphoreType.DMA((n,)), pltpu.SemaphoreType.DMA((n,)), pltpu.SemaphoreType.DMA(()),
    ]


def scatter_stages(near, grad, out, held, got, x_first, y_first, y_then, x_then, z_last, send, recv, own, early=False):
    wires = Wires(near, send, recv)
    at, sizes = near.at, near.sizes
    nz, ny, nx = sizes["z"], sizes["y"], sizes["x"]
    x, y, z = at["x"], at["y"], at["z"]
    first, second = halves(held.shape[-1])
    loads = [] if own is None else [lambda: pltpu.make_async_copy(grad.at[:, at["c"]], held, own)]
    pair = [wires.wire(grad.at[:, 1 - at["c"]], got, "c", 1)]
    one = [wires.wire(held.at[near.along("x", k), :, :, :, first], x_first.at[k - 1], "x", k) for k in near.shifts("x")]
    one += [wires.wire(held.at[:, :, near.along("y", k), :, second], y_first.at[k - 1], "y", k) for k in near.shifts("y")]
    two = [wires.wire(held.at[x, :, near.along("y", k), :, first], y_then.at[k - 1], "y", k) for k in near.shifts("y")]
    two += [wires.wire(held.at[near.along("x", k), :, y, :, second], x_then.at[k - 1], "x", k) for k in near.shifts("x")]
    last = [wires.wire(held.at[x, near.along("z", k), y], z_last.at[k - 1], "z", k) for k in near.shifts("z")]

    def add(where, terms):
        held[where] = sum([t.astype(F32) for t in terms], held[where].astype(F32)).astype(held.dtype)

    def over_z(body):
        lax.fori_loop(0, nz, lambda i, carry: (body(i), carry)[1], 0)

    def stage0():
        start(pair, loads)

    def stage1():
        for load in loads:
            load().wait()
        landed(pair)

        @over_z
        def _(i):
            for a in range(nx):
                for b in range(ny):
                    if own is None:
                        held[a, i, b] = (grad[a, at["c"], i, b].astype(F32) + got[a, i, b].astype(F32)).astype(held.dtype)
                    else:
                        add((a, i, b), [got[a, i, b]])

        start(one)

    def stage2():
        landed(one)

        @over_z
        def _(i):
            for b in range(ny):
                add((x, i, b, ALL, first), [x_first[k - 1, i, b] for k in near.shifts("x")])
            for a in range(nx):
                add((a, i, y, ALL, second), [y_first[k - 1, a, i] for k in near.shifts("y")])

        start(two)

    def stage3():
        landed(two)

        @over_z
        def _(i):
            add((x, i, y, ALL, first), [y_then[k - 1, i] for k in near.shifts("y")])
            add((x, i, y, ALL, second), [x_then[k - 1, i] for k in near.shifts("x")])
            if early:
                out[i] = held[x, i, y]

        if early:
            left(pair, one, two)
        else:
            start(last)

    def stage4():
        landed(last)
        out[...] = sum([z_last[k - 1].astype(F32) for k in near.shifts("z")], held[x, z, y].astype(F32))
        left(pair, one, two, last)

    return [stage0, stage1, stage2, stage3] if early else [stage0, stage1, stage2, stage3, stage4]


def column_stages(near, column, out, z_last, send, recv):
    wires = Wires(near, send, recv)
    last = [wires.wire(column.at[near.along("z", k)], z_last.at[k - 1], "z", k) for k in near.shifts("z")]

    def finish():
        landed(last)
        out[...] = sum([z_last[k - 1].astype(F32) for k in near.shifts("z")], column[near.at["z"]].astype(F32))
        left(last)

    return [lambda: start(last), finish]


def total_scratch(sizes, shape):
    n = sum(sizes[a] - 1 for a in "cxyz")
    return [pltpu.VMEM((n,) + shape, F32), pltpu.VMEM((3,) + shape, F32), pltpu.SemaphoreType.DMA((n,)), pltpu.SemaphoreType.DMA((n,))]


def total_stages(near, mine, out, got, held, send, recv):
    wires = Wires(near, send, recv)
    groups, slots = [], []
    for step, axis in enumerate("cxyz"):
        src = mine if step == 0 else held.at[step - 1]
        slots.append([wires.used + k - 1 for k in near.shifts(axis)])
        groups.append([wires.wire(src, got.at[wires.used], axis, k) for k in near.shifts(axis)])

    def stage(step):
        def run():
            if step > 0:
                landed(groups[step - 1])
                total = mine[...] if step == 1 else held[step - 2]
                for slot in slots[step - 1]:
                    total = total + got[slot]
                if step < 4:
                    held[step - 1] = total
                else:
                    out[...] = total
                    left(*groups)
            if step < 4:
                start(groups[step])

        return run

    return [stage(step) for step in range(5)]


def blocks_of(sizes, grads):
    return [g.reshape(lead(sizes) + (-1, g.shape[1])) for g in grads]


def pump(schedule, plans, chunk):
    for step in sorted({at[0] for at in schedule if at[1] == chunk}):

        @pl.when(pl.program_id(0) == step)
        def _():
            for plan, stage in schedule[step, chunk]:
                plans[plan][stage]()


def mesh_sizes(mesh):
    fsdp = mesh.shape["fsdp"]
    ny = 1 << ((fsdp.bit_length() - 1) // 2)
    return {"x": mesh.shape["dp"] // 2, "c": 2, "z": fsdp // ny, "y": ny}


def project_kernel(x_ref, w_ref, gain_ref, shift_ref, offset_ref, a1_ref, qkv_ref):
    @pl.when(pl.program_id(0) == 0)
    def _():
        def body(rows):
            unit, _ = normalised(x_ref[rows, :].astype(F32))
            a1_ref[rows, :] = (unit * gain_ref[...] + shift_ref[...]).astype(BF)

        row_loop(x_ref.shape[0], 352, body)

    qkv_ref[...] = (dot(a1_ref[...], w_ref[...], 1, 0) + offset_ref[...]).astype(BF)


def project(x, w_in, gain, shift, offset):
    rows, d = x.shape
    return pl.pallas_call(
        project_kernel,
        grid=(3,),
        in_specs=[
            whole((rows, d)),
            pl.BlockSpec((d, d), lambda t: (0, t)),
            whole((1, d)),
            whole((1, d)),
            pl.BlockSpec((1, d), lambda t: (0, t)),
        ],
        out_specs=[whole((rows, d)), pl.BlockSpec((rows, d), lambda t: (0, t))],
        out_shape=[
            jax.ShapeDtypeStruct((rows, d), BF),
            jax.ShapeDtypeStruct((rows, 3 * d), BF),
        ],
        compiler_params=params(),
        cost_estimate=cost(6 * rows * d * d, 2 * (5 * rows * d + 3 * d * d)),
        name="project",
    )(x, w_in, gain, shift, offset)


VEC_ROWS = 16
UP_ROW = 10


def placed(value, width, device):
    size = value.shape[-1]
    row = lax.broadcasted_iota(jnp.int32, (size, width), 0)
    column = lax.broadcasted_iota(jnp.int32, (size, width), 1)
    return dot(value, (column == row + device * size).astype(BF), 1, 0)


def enter_kernel(sizes, tile, x_ref, w_ref, seg_ref, wo_ref, wu_ref, *refs):
    vec_refs, (a1_out, qkv_out, w_out, vecs_ref, mark_ref, far_ref, wo_full, wu_full) = refs[:10], refs[10:18]
    a1_ref, qkv_ref, w_full, unit_ref, mine_ref, third_ref = refs[18:24]
    small_refs, gather_refs, ahead_refs, out_sems = refs[24:28], refs[28:37], refs[37:43], refs[43]
    rows, d = x_ref.shape
    near = Near(sizes)
    near.greet()
    device = lax.axis_index(AXES)
    mine_ref[...] = jnp.zeros_like(mine_ref)
    in_bias, *plain = vec_refs
    up_bias = plain.pop(4)
    for i, ref in enumerate(plain):
        mine_ref[i : i + 1, :] = placed(ref[...], d, device)
    both = placed(in_bias[...], 2 * d, device)
    mine_ref[8:9, :] = both[:, :d]
    mine_ref[9:10, :] = both[:, d:]
    up = placed(up_bias[...], 4 * d, device)
    for i in range(4):
        mine_ref[UP_ROW + i : UP_ROW + i + 1, :] = up[:, d * i : d * (i + 1)]
    plans = [
        gather_stages(near, w_ref, w_full, *gather_refs[3 * t : 3 * t + 3], base=d * t, width=d) for t in range(3)
    ]
    ahead = [
        gather_stages(near, wo_ref, wo_full, *ahead_refs[:3], part="first"),
        gather_stages(near, wu_ref, wu_full, *ahead_refs[3:], part="first"),
    ]
    small = total_stages(near, mine_ref, vecs_ref, *small_refs)
    for plan in plans:
        plan[0]()

    def body(index, carry):
        span = pl.ds(pl.multiple_of(index * tile, tile), tile)
        unit_ref[span, :], _ = normalised(x_ref[span, :].astype(F32))
        for step in range(3):
            pl.when(index == step)(small[step])
        return carry

    lax.fori_loop(0, rows // tile, body, 0)
    plans[0][1]()
    small[3]()
    for plan in ahead:
        plan[0]()
    image = lax.broadcasted_iota(jnp.int32, (128, rows), 0) % HD
    same = seg_ref[...] == image
    mark_ref[...] = same.astype(F32).T.astype(BF)
    far_ref[...] = jnp.where(same | (image > PADDING), 0.0, FAR).T.astype(BF)
    plans[1][1]()
    plans[0][2]()
    plans[2][1]()
    plans[1][2]()
    small[4]()

    def shifted(span):
        a1_ref[span, :] = (unit_ref[span, :] * vecs_ref[1:2, :] + vecs_ref[2:3, :]).astype(BF)

    row_loop(rows, tile, shifted)
    sends = [pltpu.make_async_copy(a1_ref, a1_out, out_sems.at[0])]
    sends[0].start()

    def third(t):
        cols = slice(d * t, d * (t + 1))
        third_ref[...] = w_full[:, :, :, :, :, cols].astype(F32).reshape(d, d).astype(BF)

        def body(span):
            value = dot(a1_ref[span, :], third_ref[...], 1, 0)
            if t != 1:
                value = value + vecs_ref[8 + t // 2 : 9 + t // 2, :]
            qkv_ref[span, cols] = value.astype(BF)

        row_loop(rows, rows // 2, body)

    def store(t):
        cols = pl.ds(d * t, d)
        sends.append(pltpu.make_async_copy(qkv_ref.at[:, cols], qkv_out.at[:, cols], out_sems.at[1 + t]))
        sends[-1].start()

    plans[0][3]()
    plans[2][2]()
    plans[0][4]()
    third(0)
    plans[1][3]()
    store(0)
    plans[1][4]()
    plans[2][3]()
    third(1)
    store(1)
    plans[2][4]()
    sends.append(pltpu.make_async_copy(w_full, w_out, out_sems.at[4]))
    sends[-1].start()
    third(2)
    store(2)
    for plan in ahead:
        plan[1]()
    for copy in sends:
        copy.wait()


def enter(sizes, x, w_in, segment_ids, w_out, w_up, vectors, tile=352):
    rows, d = x.shape
    vmem, hbm = pl.BlockSpec(memory_space=pltpu.VMEM), pl.BlockSpec(memory_space=pltpu.HBM)
    full = lead(sizes) + w_in.shape
    return pl.pallas_call(
        functools.partial(enter_kernel, sizes, tile),
        in_specs=[vmem] * 15,
        out_specs=[hbm, hbm, hbm, vmem, vmem, vmem, hbm, hbm],
        out_shape=[
            jax.ShapeDtypeStruct((rows, d), BF),
            jax.ShapeDtypeStruct((rows, 3 * d), BF),
            jax.ShapeDtypeStruct(full, BF),
            jax.ShapeDtypeStruct((VEC_ROWS, d), F32),
            jax.ShapeDtypeStruct((rows, 128), BF),
            jax.ShapeDtypeStruct((rows, 128), BF),
            *gathered(sizes, [w_out, w_up]),
        ],
        scratch_shapes=[
            pltpu.VMEM((rows, d), BF),
            pltpu.VMEM((rows, 3 * d), BF),
            pltpu.VMEM(full, BF),
            pltpu.VMEM((rows, d), F32),
            pltpu.VMEM((VEC_ROWS, d), F32),
            pltpu.VMEM((d, d), BF),
            *total_scratch(sizes, (VEC_ROWS, d)),
            *gather_scratch(sizes) * 5,
            pltpu.SemaphoreType.DMA((5,)),
        ],
        compiler_params=params(collective_id=0, has_side_effects=True),
        name="enter",
    )(x, w_in, segment_ids[None], w_out, w_up, *[v[None] for v in vectors])


def chunks(rows, size):
    return [(start, min(size, rows - start)) for start in range(0, rows, size)]


GATHER_AT = {
    (0, 0): [(2, 0), (0, 1), (1, 1)],
    (1, 0): [(0, 2), (1, 2)],
    (2, 0): [(2, 1), (0, 3)],
    (3, 0): [(2, 2), (1, 3)],
    (5, 0): [(2, 3)],
    (5, -1): [(0, 4), (1, 4), (2, 4)],
}


def attend_kernel(chunk, sizes, count, q_ref, k_ref, v_ref, mark_ref, far_ref, *refs):
    shards, (o_ref, e_ref, inv_ref) = refs[:count][::-1], refs[count : count + 3]
    full, (vt_ref, k2_ref), sems = refs[count + 3 : 2 * count + 3], refs[2 * count + 3 : 2 * count + 5], refs[2 * count + 5 :]
    rows = q_ref.shape[0]
    plans, schedule = [], {}
    if count:
        near, schedule = Near(sizes), GATHER_AT
        pl.when(pl.program_id(0) == 0)(near.greet)
        plans = [
            gather_stages(near, shards[i], full[i], *sems[3 * i : 3 * i + 3], part="all" if i == 2 else "rest") for i in range(count)
        ]
    vt_ref[...] = v_ref[...].astype(F32).T.astype(BF)
    low = lax.broadcasted_iota(jnp.int32, (1, 128), 1) < HD
    for half in range(2):
        mine = low if half == 0 else jnp.logical_not(low)
        k2_ref[half] = jnp.where(mine, k_ref[...], far_ref[...])
    for turn, (start, size) in enumerate(chunks(rows, chunk)):
        pump(schedule, plans, turn)
        for half in range(2):
            mine = low if half == 0 else jnp.logical_not(low)
            span = pl.ds(start, size)
            query = jnp.where(mine, q_ref[span, :], mark_ref[span, :])
            scores = dot(k2_ref[half], query, 1, 1)
            top = jnp.max(scores, axis=0, keepdims=True)
            weights = jnp.exp2((scores - top) * (LOG2E * HD ** (-0.5)))
            total = jnp.sum(weights, axis=0, keepdims=True)
            weights_low = weights.astype(BF)
            e_ref[half, :, span] = weights_low
            inverse = 1.0 / total
            inv_ref[0, half : half + 1, span] = inverse
            head = pl.ds(half * HD, HD)
            o_ref[head, span] = (dot(vt_ref[head, :], weights_low, 1, 0) * inverse).astype(BF)
    pump(schedule, plans, -1)


def attend(qkv, mark, far, sizes, shards, chunk=256):
    count = len(shards)
    hbm = pl.BlockSpec(memory_space=pltpu.HBM)
    rows, width = qkv.shape
    pairs = width // 384
    return pl.pallas_call(
        functools.partial(attend_kernel, chunk, sizes, count),
        grid=(pairs,),
        in_specs=[
            pl.BlockSpec((rows, 128), lambda p: (0, p)),
            pl.BlockSpec((rows, 128), lambda p: (0, pairs + p)),
            pl.BlockSpec((rows, 128), lambda p: (0, 2 * pairs + p)),
            whole((rows, 128)),
            whole((rows, 128)),
            *([whole(shards[2].shape), hbm, hbm] if count else []),
        ],
        out_specs=[
            pl.BlockSpec((128, rows), lambda p: (p, 0)),
            pl.BlockSpec((2, rows, rows), lambda p: (p, 0, 0)),
            pl.BlockSpec((1, 2, rows), lambda p: (p, 0, 0)),
            *[hbm] * count,
        ],
        out_shape=[
            jax.ShapeDtypeStruct((pairs * 128, rows), BF),
            jax.ShapeDtypeStruct((2 * pairs, rows, rows), BF),
            jax.ShapeDtypeStruct((pairs, 2, rows), F32),
            *([*shards[:2], *gathered(sizes, shards[2:])] if count else []),
        ],
        scratch_shapes=[
            pltpu.VMEM((128, rows), BF),
            pltpu.VMEM((2, rows, 128), BF),
            *(gather_scratch(sizes) * count if count else []),
        ],
        compiler_params=params(collective_id=1, has_side_effects=True) if count else params(),
        cost_estimate=cost(2 * pairs * 4 * rows * rows * 256, 4 * pairs * rows * rows, 2 * pairs * rows * rows),
        input_output_aliases={7: 3, 6: 4} if count else {},
        name="attend",
    )(qkv, qkv, qkv, mark, far, *shards[::-1])


def masked(g_ref, mark_ref, rows):
    padding = mark_ref[rows, PADDING : PADDING + 1].astype(F32)
    return jnp.where(padding > 0, 0.0, g_ref[rows, :].astype(F32))


def middle_kernel(o_ref, x_ref, g_ref, mark_ref, w_ref, vec_ref, m1_ref, a2_ref, gm_ref, gmsum_ref):
    bias, scale1, gain2, shift2, scale2 = (vec_ref[i : i + 1, :] for i in (0, 3, 5, 6, 7))
    m1_ref[...] = dot(o_ref[...], w_ref[...], 0, 0)
    gmsum_ref[...] = jnp.zeros_like(gmsum_ref)

    def body(rows):
        m1 = x_ref[rows, :].astype(F32) + scale1 * (m1_ref[rows, :] + bias)
        m1_ref[rows, :] = m1
        unit, _ = normalised(m1)
        a2_ref[rows, :] = (unit * gain2 + shift2).astype(BF)
        gm = (scale2 * masked(g_ref, mark_ref, rows)).astype(BF)
        gm_ref[rows, :] = gm
        gmsum_ref[...] += jnp.sum(gm.astype(F32).reshape(-1, 8, gm.shape[-1]), axis=0)

    row_loop(x_ref.shape[0], 352, body)


def middle(o, x, g, mark, w_out, vec):
    rows, d = x.shape
    return pl.pallas_call(
        middle_kernel,
        out_shape=[
            jax.ShapeDtypeStruct((rows, d), F32),
            jax.ShapeDtypeStruct((rows, d), BF),
            jax.ShapeDtypeStruct((rows, d), BF),
            jax.ShapeDtypeStruct((8, d), F32),
        ],
        compiler_params=params(),
        cost_estimate=cost(2 * rows * d * d, 14 * rows * d),
        name="middle",
    )(o, x, g, mark, w_out, vec)


def gelu_parts(u):
    near = jnp.abs(u)
    t = 1.0 / (1.0 + (0.3275911 * 0.7071067811865476) * near)
    bell = jnp.exp2((-0.5 * LOG2E) * (u * u))
    poly = t * (
        0.5 * 0.254829592
        + t * (0.5 * -0.284496736 + t * (0.5 * 1.421413741 + t * (0.5 * -1.453152027 + t * (0.5 * 1.061405429))))
    )
    tail = poly * bell
    phi = jnp.where(u < 0, tail, 1.0 - tail)
    return u * phi, phi + u * bell * 0.3989422804014327


def feed_kernel(chunk, a2_ref, gm_ref, up_ref, vec_ref, down_ref, bm_ref, ga_ref, dup_ref, ddown_ref, dub_ref, gl_ref, gu_ref):
    first = pl.program_id(0) == 0

    @pl.when(first)
    def _():
        bm_ref[...] = jnp.zeros_like(bm_ref)
        ga_ref[...] = jnp.zeros_like(ga_ref)

    d = vec_ref.shape[-1]
    spread = up_ref.shape[-1] // d
    bias = jnp.concatenate([vec_ref[pl.ds(UP_ROW + pl.program_id(0) * spread + i, 1), :] for i in range(spread)], axis=1)
    total = jnp.zeros((8, up_ref.shape[-1]), F32)
    for start, size in chunks(a2_ref.shape[0], chunk):
        rows = pl.ds(start, size)
        u = dot(a2_ref[rows, :], up_ref[...], 1, 0) + bias
        back = dot(gm_ref[rows, :], down_ref[...], 1, 1)
        active, slope = gelu_parts(u)
        low = active.astype(BF)
        gl_ref[rows, :] = low
        gu = (slope * back).astype(BF)
        gu_ref[rows, :] = gu
        total += jnp.sum(gu.astype(F32).reshape(-1, 8, gu.shape[-1]), axis=0)
        bm_ref[rows, :] += dot(low, down_ref[...], 1, 0)
        ga_ref[rows, :] += dot(gu, up_ref[...], 1, 1)
    dub_ref[...] = total
    ddown_ref[...] = dot(gl_ref[...], gm_ref[...], 0, 0).astype(ddown_ref.dtype)
    dup_ref[...] = dot(a2_ref[...], gu_ref[...], 0, 0).astype(dup_ref.dtype)


def feed(a2, gm, w_up, vecs, w_down, block=768, chunk=704, kind=BF):
    rows, d = a2.shape
    ff = w_up.shape[1]
    return pl.pallas_call(
        functools.partial(feed_kernel, chunk),
        grid=(ff // block,),
        in_specs=[
            whole((rows, d)),
            whole((rows, d)),
            pl.BlockSpec((d, block), lambda f: (0, f)),
            whole((VEC_ROWS, d)),
            pl.BlockSpec((block, d), lambda f: (f, 0)),
        ],
        out_specs=[
            whole((rows, d)),
            whole((rows, d)),
            pl.BlockSpec((d, block), lambda f: (0, f)),
            pl.BlockSpec((block, d), lambda f: (f, 0)),
            pl.BlockSpec((8, block), lambda f: (0, f)),
        ],
        out_shape=[
            jax.ShapeDtypeStruct((rows, d), F32),
            jax.ShapeDtypeStruct((rows, d), F32),
            jax.ShapeDtypeStruct((d, ff), kind),
            jax.ShapeDtypeStruct((ff, d), kind),
            jax.ShapeDtypeStruct((8, ff), F32),
        ],
        scratch_shapes=[pltpu.VMEM((rows, block), BF), pltpu.VMEM((rows, block), BF)],
        compiler_params=params(),
        cost_estimate=cost(12 * rows * d * ff, 4 * 4 * d * ff),
        name="feed",
    )(a2, gm, w_up, vecs, w_down)


def join_kernel(size, m1_ref, bm_ref, ga_ref, x_ref, g_ref, mark_ref, o_ref, w_ref, vec_ref, out_ref, gm1_ref, go_ref, dout_ref, sums_ref, gb_ref):
    bias2, scale1, gain2, scale2 = (vec_ref[i : i + 1, :] for i in (4, 3, 5, 7))
    step = pl.program_id(0)

    @pl.when(step == 0)
    def _():
        sums_ref[...] = jnp.zeros_like(sums_ref)

    base = step * m1_ref.shape[0]

    def body(rows):
        m1 = m1_ref[rows, :]
        bm = bm_ref[rows, :] + bias2
        g = masked(g_ref, mark_ref, rows)
        out_ref[rows, :] = (m1 + scale2 * bm).astype(BF)
        unit, inverse = normalised(m1)
        ga = ga_ref[rows, :]
        gm1 = g + norm_back(unit, inverse, ga * gain2)
        gm1_ref[rows, :] = gm1
        gb = (scale1 * gm1).astype(BF)
        gb_ref[pl.ds(pl.multiple_of(base + rows.start, size), size), :] = gb
        for index, value in enumerate(
            (g * bm, ga * unit, ga, gm1 * (m1 - x_ref[rows, :].astype(F32)), gb.astype(F32))
        ):
            sums_ref[index] += jnp.sum(value.reshape(-1, 8, value.shape[-1]), axis=0)

    row_loop(m1_ref.shape[0], size, body)

    @pl.when(step == pl.num_programs(0) - 1)
    def _():
        go_ref[...] = dot(w_ref[...], gb_ref[...], 1, 1).astype(BF)
        dout_ref[...] = dot(o_ref[...], gb_ref[...], 1, 0).astype(dout_ref.dtype)


def join(m1, bm, ga, x, g, mark, o, w_out, vec, tile=352, kind=BF):
    rows, d = x.shape
    by_rows = pl.BlockSpec((tile, d), lambda i: (i, 0))
    return pl.pallas_call(
        functools.partial(join_kernel, 352),
        grid=(rows // tile,),
        in_specs=[by_rows] * 5 + [pl.BlockSpec((tile, 128), lambda i: (i, 0)), whole((d, rows)), whole((d, d)), whole((VEC_ROWS, d))],
        out_specs=[by_rows, by_rows, whole((d, rows)), whole((d, d)), whole((5, 8, d))],
        out_shape=[
            jax.ShapeDtypeStruct((rows, d), BF),
            jax.ShapeDtypeStruct((rows, d), F32),
            jax.ShapeDtypeStruct((d, rows), BF),
            jax.ShapeDtypeStruct((d, d), kind),
            jax.ShapeDtypeStruct((5, 8, d), F32),
        ],
        scratch_shapes=[pltpu.VMEM((rows, d), BF)],
        compiler_params=params(),
        cost_estimate=cost(4 * rows * d * d, 26 * rows * d),
        name="join",
    )(m1, bm, ga, x, g, mark, o, w_out, vec)


SCATTER_AT = {
    (0, 0): [(2, 0), (0, 0), (1, 0)],
    (1, 0): [(0, 1), (2, 1)],
    (2, 0): [(1, 1)],
    (3, 0): [(0, 2), (2, 2)],
    (4, 0): [(1, 2), (0, 3)],
    (5, 0): [(2, 3), (1, 3)],
    (5, -1): [(0, 4), (2, 4)],
}


def attend_back_kernel(chunk, sizes, count, q_ref, k_ref, v_ref, go_ref, o_ref, e_ref, inv_ref, *refs):
    grads, out_ref, sums = refs[:count], refs[count], refs[count + 1 : 2 * count + 1]
    (kt_ref, gq_ref, gs_ref, gp_ref), rest = refs[2 * count + 1 : 2 * count + 5], refs[2 * count + 5 :]
    rows = q_ref.shape[0]
    plans, schedule = [], {}
    if count:
        near, schedule = Near(sizes), SCATTER_AT
        pl.when(pl.program_id(0) == 0)(near.greet)
        plans = [
            scatter_stages(near, grads[i], sums[i], *rest[SCATTER_REFS * i : SCATTER_REFS * (i + 1)], early=i == 1)
            for i in range(count)
        ]
    factor = HD ** (-0.5)
    kt_ref[...] = k_ref[...].astype(F32).T.astype(BF)
    low = lax.broadcasted_iota(jnp.int32, (1, 128), 1) < HD
    below = lax.broadcasted_iota(jnp.int32, (128, 1), 0) < HD
    gp_ref[...] = jnp.zeros_like(gp_ref)
    for turn, (start, size) in enumerate(chunks(rows, chunk)):
        pump(schedule, plans, turn)
        span = pl.ds(start, size)
        for half in range(2):
            head = pl.ds(half * HD, HD)
            incoming = go_ref[head, span].astype(F32) * inv_ref[0, half : half + 1, span]
            centre = jnp.sum(incoming * o_ref[head, span].astype(F32), axis=0, keepdims=True)
            gp_ref[half, head, span] = incoming.astype(BF)
            gp = dot(v_ref[...], gp_ref[half, :, span], 1, 0)
            gs = (e_ref[half, :, span].astype(F32) * (gp - centre)).astype(BF)
            gs_ref[half, :, span] = gs
            gq_ref[head, span] = dot(kt_ref[head, :], gs, 1, 0) * factor
    out_ref[0] = gq_ref[...].T.astype(BF)
    gk = [dot(gs_ref[half], q_ref[...], 1, 0) for half in range(2)]
    out_ref[1] = (jnp.where(low, gk[0], gk[1]) * factor).astype(BF)
    out_ref[2] = (dot(e_ref[0], gp_ref[0], 1, 1) + dot(e_ref[1], gp_ref[1], 1, 1)).astype(BF)
    pump(schedule, plans, -1)


def attend_back(qkv, go, o, e, inv, sizes, grads, chunk=256):
    blocks = blocks_of(sizes, grads) if grads else []
    count = len(blocks)
    sums = [jax.ShapeDtypeStruct(b.shape[-2:], F32) for b in blocks]
    if count:
        sums[1] = jax.ShapeDtypeStruct((sizes["z"],) + sums[1].shape, BF)
    rows, width = qkv.shape
    pairs = width // 384
    return pl.pallas_call(
        functools.partial(attend_back_kernel, chunk, sizes, count),
        grid=(pairs,),
        in_specs=[
            pl.BlockSpec((rows, 128), lambda p: (0, p)),
            pl.BlockSpec((rows, 128), lambda p: (0, pairs + p)),
            pl.BlockSpec((rows, 128), lambda p: (0, 2 * pairs + p)),
            pl.BlockSpec((128, rows), lambda p: (p, 0)),
            pl.BlockSpec((128, rows), lambda p: (p, 0)),
            pl.BlockSpec((2, rows, rows), lambda p: (p, 0, 0)),
            pl.BlockSpec((1, 2, rows), lambda p: (p, 0, 0)),
            *[pl.BlockSpec(memory_space=pltpu.HBM)] * count,
        ],
        out_specs=[pl.BlockSpec((3, rows, 128), lambda p: (0, 0, p)), *[whole(v.shape) for v in sums]],
        out_shape=[
            jax.ShapeDtypeStruct((3, rows, pairs * 128), BF),
            *sums,
        ],
        scratch_shapes=[
            pltpu.VMEM((128, rows), BF),
            pltpu.VMEM((128, rows), F32),
            pltpu.VMEM((2, rows, rows), BF),
            pltpu.VMEM((2, 128, rows), BF),
            *[s for b in blocks for s in scatter_scratch(sizes, *b.shape[-2:], b.dtype)],
        ],
        compiler_params=params(collective_id=2, has_side_effects=True) if count else params(),
        cost_estimate=cost(2 * pairs * 8 * rows * rows * 256, 4 * pairs * rows * rows),
        name="attend_back",
    )(qkv, qkv, qkv, go, o, e, inv, *blocks)


def finish_kernel(a1_ref, gqkv_ref, w_ref, x_ref, gm1_ref, gain_ref, dw_ref, cols_ref, gx_ref, sums_ref, ga_ref):
    step = pl.program_id(0)
    grads = gqkv_ref[0]
    dw_ref[...] = dot(a1_ref[...], grads, 0, 0).astype(dw_ref.dtype)
    cols_ref[0] = jnp.sum(grads.astype(F32).reshape(-1, 8, grads.shape[-1]), axis=0)
    part = dot(grads, w_ref[...], 1, 1)

    @pl.when(step == 0)
    def _():
        ga_ref[...] = part

    @pl.when(step > 0)
    def _():
        ga_ref[...] += part

    @pl.when(step == pl.num_programs(0) - 1)
    def _():
        sums_ref[...] = jnp.zeros_like(sums_ref)

        def body(rows):
            unit, inverse = normalised(x_ref[rows, :].astype(F32))
            ga = ga_ref[rows, :]
            gx_ref[rows, :] = gm1_ref[rows, :] + norm_back(unit, inverse, ga * gain_ref[...])
            for index, value in enumerate((ga * unit, ga)):
                sums_ref[index] += jnp.sum(value.reshape(-1, 8, value.shape[-1]), axis=0)

        row_loop(x_ref.shape[0], 352, body)


def finish(a1, gqkv, w_in, x, gm1, gain, kind=BF):
    rows, d = x.shape
    return pl.pallas_call(
        finish_kernel,
        grid=(3,),
        in_specs=[
            whole((rows, d)),
            pl.BlockSpec((1, rows, d), lambda t: (t, 0, 0)),
            pl.BlockSpec((d, d), lambda t: (0, t)),
            whole((rows, d)),
            whole((rows, d)),
            whole((1, d)),
        ],
        out_specs=[
            pl.BlockSpec((d, d), lambda t: (0, t)),
            pl.BlockSpec((1, 8, d), lambda t: (t, 0, 0)),
            whole((rows, d)),
            whole((2, 8, d)),
        ],
        out_shape=[
            jax.ShapeDtypeStruct((d, 3 * d), kind),
            jax.ShapeDtypeStruct((3, 8, d), F32),
            jax.ShapeDtypeStruct((rows, d), F32),
            jax.ShapeDtypeStruct((2, 8, d), F32),
        ],
        scratch_shapes=[pltpu.VMEM((rows, d), F32)],
        compiler_params=params(),
        cost_estimate=cost(12 * rows * d * d, 20 * rows * d),
        name="finish",
    )(a1, gqkv, w_in, x, gm1, gain)


def leave_kernel(sizes, tile, a1_in, gqkv_in, w_in, x_in, gm1_in, vec_ref, join_ref, ub_ref, gmsum_ref, column_ref, gx_out, dw_ref, early_ref, late_ref, ddown_ref, *refs):
    a1_ref, gqkv_ref, w_ref, x_ref, gm1_ref, gx_ref, ga_ref, sums_ref, mine_ref, last_ref = refs[:10]
    grad_refs, refs = refs[10:13], refs[13:]
    scatter_refs, refs = [refs[9 * t : 9 * t + 9] for t in range(3)], refs[27:]
    early_refs, late_refs, column_refs, in_sems, out_sems = refs[:4], refs[4:8], refs[8:11], refs[11], refs[12]
    rows, d = x_in.shape
    count = rows // tile
    moves = [(a1_in, a1_ref), *[(gqkv_in.at[t], gqkv_ref.at[t]) for t in range(3)], (w_in, w_ref), (x_in, x_ref), (gm1_in, gm1_ref)]
    fetch = [pltpu.make_async_copy(src, dst, in_sems.at[n]) for n, (src, dst) in enumerate(moves)]
    for copy in fetch:
        copy.start()
    near = Near(sizes)
    near.greet()
    row = lambda value: jnp.sum(value, axis=0, keepdims=True)
    mine_ref[...] = jnp.zeros_like(mine_ref)
    for i, value in enumerate(
        (row(join_ref[4]), row(join_ref[3]) / vec_ref[3:4, :], row(gmsum_ref[...]), row(join_ref[1]), row(join_ref[2]), row(join_ref[0]))
    ):
        mine_ref[i : i + 1, :] = value
    for i in range(4):
        mine_ref[8 + i : 9 + i, :] = row(ub_ref[:, d * i : d * (i + 1)])
    plans = [
        scatter_stages(near, grad_refs[t], dw_ref.at[:, pl.ds(d * t, d)], *scatter_refs[t], None) for t in range(3)
    ]
    early = total_stages(near, mine_ref, early_ref, *early_refs)
    late = total_stages(near, last_ref, late_ref, *late_refs)
    column = column_stages(near, column_ref, ddown_ref, *column_refs)
    column[0]()
    last_ref[...] = jnp.zeros_like(last_ref)

    def weight(t):
        fetch[1 + t].wait()
        value = dot(a1_ref[...], gqkv_ref[t], 0, 0)
        grad_refs[t][...] = value.reshape(grad_refs[t].shape).astype(BF)

    def back(t):
        def body(span):
            part = dot(gqkv_ref[t, span, :], w_ref[:, d * t : d * (t + 1)], 1, 1)
            ga_ref[span, :] = part if t == 0 else ga_ref[span, :] + part

        row_loop(rows, rows // 2, body)
        if t != 1:
            total = jnp.zeros((1, d), F32)
            for start_row, size in chunks(rows, tile):
                total += row(gqkv_ref[t, pl.ds(start_row, size), :].astype(F32))
            last_ref[2 + t // 2 : 3 + t // 2, :] = total

    fetch[0].wait()
    weight(0)
    early[0]()
    plans[0][0]()
    weight(1)
    plans[0][1]()
    plans[1][0]()
    early[1]()
    weight(2)
    plans[1][1]()
    plans[2][0]()
    fetch[4].wait()
    back(0)
    plans[0][2]()
    plans[2][1]()
    early[2]()
    back(1)
    plans[1][2]()
    back(2)
    plans[0][3]()
    column[1]()
    early[3]()
    fetch[5].wait()
    fetch[6].wait()
    sums_ref[...] = jnp.zeros_like(sums_ref)

    def send(index):
        span = pl.ds(pl.multiple_of(index * tile, tile), tile)
        return pltpu.make_async_copy(gx_ref.at[span], gx_out.at[span], out_sems.at[index])

    between = [[], [plans[2][2], plans[1][3]], []]

    def body(index, carry):
        span = pl.ds(pl.multiple_of(index * tile, tile), tile)
        unit, inverse = normalised(x_ref[span, :].astype(F32))
        ga = ga_ref[span, :]
        gx_ref[span, :] = gm1_ref[span, :] + norm_back(unit, inverse, ga * vec_ref[1:2, :])
        for n, value in enumerate((ga * unit, ga)):
            sums_ref[n] += jnp.sum(value.reshape(-1, 8, d), axis=0)
        for n, stages in enumerate(between):

            @pl.when(index == n)
            def _():
                for stage in stages:
                    stage()

        pl.when(index > 0)(lambda: send(index - 1).start())
        return carry

    lax.fori_loop(0, count, body, 0)
    for n in range(2):
        last_ref[n : n + 1, :] = row(sums_ref[n])
    late[0]()
    send(count - 1).start()
    early[4]()
    plans[2][3]()
    late[1]()
    plans[0][4]()
    late[2]()
    plans[1][4]()
    late[3]()
    plans[2][4]()
    late[4]()
    for index in range(count):
        send(index).wait()


def leave(sizes, a1, gqkv, w_in, x, gm1, vecs, join_sums, ub_sum, gm_sum, column, tile=352):
    rows, d = x.shape
    vmem, hbm = pl.BlockSpec(memory_space=pltpu.VMEM), pl.BlockSpec(memory_space=pltpu.HBM)
    block = d // (sizes["x"] * 2 * sizes["z"] * sizes["y"])
    return pl.pallas_call(
        functools.partial(leave_kernel, sizes, tile),
        in_specs=[hbm] * 5 + [vmem] * 5,
        out_specs=[hbm, vmem, vmem, vmem, vmem],
        out_shape=[
            jax.ShapeDtypeStruct((rows, d), F32),
            jax.ShapeDtypeStruct((block, 3 * d), F32),
            jax.ShapeDtypeStruct((16, d), F32),
            jax.ShapeDtypeStruct((8, d), F32),
            jax.ShapeDtypeStruct(column.shape[1:], F32),
        ],
        scratch_shapes=[
            pltpu.VMEM((rows, d), BF),
            pltpu.VMEM((3, rows, d), BF),
            pltpu.VMEM((d, 3 * d), BF),
            pltpu.VMEM((rows, d), BF),
            pltpu.VMEM((rows, d), F32),
            pltpu.VMEM((rows, d), F32),
            pltpu.VMEM((rows, d), F32),
            pltpu.VMEM((2, 8, d), F32),
            pltpu.VMEM((16, d), F32),
            pltpu.VMEM((8, d), F32),
            *[pltpu.VMEM(lead(sizes) + (block, d), BF)] * 3,
            *scatter_scratch(sizes, block, d, BF)[:-1] * 3,
            *total_scratch(sizes, (16, d)),
            *total_scratch(sizes, (8, d)),
            pltpu.VMEM((sizes["z"] - 1,) + column.shape[1:], BF),
            pltpu.SemaphoreType.DMA((sizes["z"] - 1,)),
            pltpu.SemaphoreType.DMA((sizes["z"] - 1,)),
            pltpu.SemaphoreType.DMA((7,)),
            pltpu.SemaphoreType.DMA((rows // tile,)),
        ],
        compiler_params=params(collective_id=3, has_side_effects=True),
        name="leave",
    )(a1, gqkv, w_in, x, gm1, vecs, join_sums, ub_sum, gm_sum, column)


def share_kernel(early_ref, late_ref, *refs):
    grads, outs, vec_outs = refs[:4], refs[4:8], refs[8:]
    for src, dst in zip(grads, outs):
        dst[...] = src[...]
    device = lax.axis_index(AXES)
    d = early_ref.shape[-1]

    def entries(ref, first_row, size):
        at = device * size
        line = ref[pl.ds(first_row + lax.div(at, d), 1), :]
        return pltpu.roll(jnp.broadcast_to(line, (8, d)), lax.rem(d - lax.rem(at, d), d), 1)[:1, :size]

    spots = [
        (late_ref, 2), (early_ref, 0), (late_ref, 0), (late_ref, 1), (early_ref, 1),
        (early_ref, 8), (early_ref, 2), (early_ref, 3), (early_ref, 4), (early_ref, 5),
    ]
    for (ref, first_row), out in zip(spots, vec_outs):
        out[...] = entries(ref, first_row, out.shape[-1])


def share(early, late, grads, sizes):
    vmem = pl.BlockSpec(memory_space=pltpu.VMEM)
    return pl.pallas_call(
        share_kernel,
        in_specs=[vmem] * 6,
        out_specs=[vmem] * 14,
        out_shape=[jax.ShapeDtypeStruct(g.shape, F32) for g in grads] + [jax.ShapeDtypeStruct((1, n), F32) for n in sizes],
        compiler_params=params(),
        name="share",
    )(early, late, *grads)


def take(a):
    return lax.all_gather(a, AXES, axis=0, tiled=True)


def give(g):
    return lax.psum_scatter(g, AXES, scatter_dimension=0, tiled=True).astype(F32)


def layer(
    sizes, inputs, segment_ids, cotangent, in_weight, in_bias, out_weight, out_bias, first_gain, first_shift, first_scale,
    up_weight, up_bias, down_weight, down_bias, second_gain, second_shift, second_scale,
):
    rows, d = inputs.shape
    vectors = (
        in_bias, out_bias, first_gain, first_shift, first_scale,
        up_bias, down_bias, second_gain, second_shift, second_scale,
    )
    own = all(w.shape[0] % 8 == 0 for w in (in_weight, out_weight, up_weight, down_weight))
    if own:
        a1, qkv, w_in, vecs, mark, far, *begun = enter(
            sizes, inputs, in_weight, segment_ids, out_weight, up_weight, vectors
        )
        w_in = w_in.reshape(d, 3 * d)
    else:
        w_in = take(in_weight)
        row = lambda v: take(v).astype(F32).reshape(-1, d)
        vecs = jnp.concatenate(
            [row(v) for v in (out_bias, first_gain, first_shift, first_scale, down_bias, second_gain, second_shift, second_scale, in_bias)]
            + [row(up_bias), jnp.zeros((VEC_ROWS - 14, d), F32)]
        )
        offset = jnp.concatenate([vecs[8:9], jnp.zeros((1, d), F32), vecs[9:10]], axis=1)
        a1, qkv = project(inputs, w_in, vecs[1:2], vecs[2:3], offset)
        lane = lax.broadcasted_iota(jnp.int32, (1, 128), 1) % HD
        same = segment_ids[:, None] == lane
        mark = same.astype(BF)
        far = jnp.where(same | (lane > PADDING), 0.0, FAR).astype(BF)
    o, e, inv, *full = attend(qkv, mark, far, sizes, [*begun, down_weight] if own else [])
    w_out, w_up, w_down = (
        (f.reshape(-1, f.shape[-1]) for f in full) if own else (take(w) for w in (out_weight, up_weight, down_weight))
    )
    m1, a2, gm, gm_sum = middle(o, inputs, cotangent, mark, w_out, vecs)
    bm, ga2, d_up, d_down, ub_sum = feed(a2, gm, w_up, vecs, w_down)
    outputs, gm1, go, d_out, join_sums = join(m1, bm, ga2, inputs, cotangent, mark, o, w_out, vecs)
    gqkv, *done = attend_back(qkv, go, o, e, inv, sizes, [d_up, d_down, d_out] if own else [])
    if own:
        d_up, column, d_out = done
        gx, d_in, early, late, d_down = leave(sizes, a1, gqkv, w_in, inputs, gm1, vecs, join_sums, ub_sum, gm_sum, column)
        d_up, d_down, d_out, d_in, *out = share(early, late, [d_up, d_down, d_out, d_in], [v.shape[0] for v in vectors])
        out = [v.reshape(-1) for v in out]
    else:
        d_in, col_sums, gx, last_sums = finish(a1, gqkv, w_in, inputs, gm1, vecs[1:2])
        d_in, d_up, d_down, d_out = (give(v) for v in (d_in, d_up, d_down, d_out))
        s = jnp.sum
        j, c, t = (s(v, axis=1) for v in (join_sums, col_sums, last_sums))
        sums = (
            jnp.concatenate([c[0], c[2]]), j[4], t[0], t[1], j[3] / vecs[3], s(ub_sum, axis=0), s(gm_sum, axis=0), j[1], j[2], j[0],
        )
        out = [give(v) for v in sums]
    return (
        outputs, gx, d_in, out[0], d_out, out[1], out[2], out[3], out[4],
        d_up, out[5], d_down, out[6], out[7], out[8], out[9],
    )


def solution(mesh):
    wide, flat = P(AXES, None), P(AXES)
    return jax.shard_map(
        functools.partial(layer, mesh_sizes(mesh)),
        mesh=mesh,
        in_specs=(wide, flat, wide, wide, flat, wide, flat, flat, flat, flat, wide, flat, wide, flat, flat, flat, flat),
        out_specs=(wide, wide, wide, flat, wide, flat, flat, flat, flat, wide, flat, wide, flat, flat, flat, flat),
        check_vma=False,
    )
```

```python
import functools

import jax
import jax.numpy as jnp
from jax import lax
from jax.experimental import pallas as pl
from jax.experimental.pallas import tpu as pltpu
from jax.sharding import PartitionSpec as P

HD = 64
PADDING = 5
EPSILON = 1e-06
LOG2E = 1.4426950408889634
FAR = -1e30
BF = jnp.bfloat16
F32 = jnp.float32
AXES = ("dp", "fsdp")
VMEM_LIMIT = 62 * 1024 * 1024


def dot(a, b, da, db):
    return lax.dot_general(a, b, (((da,), (db,)), ((), ())), preferred_element_type=F32)


def params(**more):
    return pltpu.CompilerParams(vmem_limit_bytes=VMEM_LIMIT, **more)


def cost(flops, moved, special=0):
    return pl.CostEstimate(flops=int(flops), bytes_accessed=int(moved), transcendentals=int(special))


def whole(shape):
    return pl.BlockSpec(shape, lambda *_: (0,) * len(shape), pipeline_mode=pl.Buffered(1))


def row_loop(rows, size, body):
    def step(index, carry):
        body(pl.ds(pl.multiple_of(index * size, size), size))
        return carry

    lax.fori_loop(0, rows // size, step, 0)


def normalised(values):
    centred = values - jnp.mean(values, axis=-1, keepdims=True)
    spread = jnp.mean(centred * centred, axis=-1, keepdims=True)
    inverse = lax.rsqrt(spread + EPSILON)
    return centred * inverse, inverse


def norm_back(unit, inverse, scaled):
    return inverse * (
        scaled
        - jnp.mean(scaled, axis=-1, keepdims=True)
        - unit * jnp.mean(scaled * unit, axis=-1, keepdims=True)
    )


MESH = pl.DeviceIdType.MESH
ALL = slice(None)


class Near:
    def __init__(self, sizes):
        self.sizes = sizes
        dp, fsdp = lax.axis_index("dp"), lax.axis_index("fsdp")
        ny = sizes["y"]
        self.at = {"x": lax.div(dp, 2), "c": lax.rem(dp, 2), "z": lax.div(fsdp, ny), "y": lax.rem(fsdp, ny)}

    def along(self, axis, shift):
        return lax.rem(self.at[axis] + shift, self.sizes[axis])

    def device(self, axis, shift):
        at = {**self.at, axis: self.along(axis, shift)}
        return (at["x"] * 2 + at["c"], at["z"] * self.sizes["y"] + at["y"])

    def shifts(self, axis):
        return range(1, self.sizes[axis])

    def greet(self):
        barrier = pltpu.get_barrier_semaphore()
        count = 0
        for axis in "cxyz":
            for shift in self.shifts(axis):
                pl.semaphore_signal(barrier, inc=1, device_id=self.device(axis, shift), device_id_type=MESH)
                count += 1
        pl.semaphore_wait(barrier, count)


class Wires:
    def __init__(self, near, send, recv):
        self.near, self.send, self.recv, self.used = near, send, recv, 0

    def wire(self, src, dst, axis, shift):
        n = self.used
        self.used += 1
        return lambda: pltpu.make_async_remote_copy(
            src_ref=src, dst_ref=dst, send_sem=self.send.at[n], recv_sem=self.recv.at[n],
            device_id=self.near.device(axis, shift), device_id_type=MESH,
        )


def start(*groups):
    for group in groups:
        for wire in group:
            wire().start()


def landed(*groups):
    for group in groups:
        for wire in group:
            wire().wait_recv()


def left(*groups):
    for group in groups:
        for wire in group:
            wire().wait_send()


def halves(width, base=0):
    cut = (width // 256) * 128
    return pl.ds(base, cut), pl.ds(base + cut, width - cut)


def gather_wires(sizes):
    return sizes["z"] + 4 * (sizes["x"] + sizes["y"] - 2)


def gather_stages(near, mine, full, send, recv, own, base=0, width=None, part="all"):
    wires = Wires(near, send, recv)
    at = near.at
    width = full.shape[-1] if width is None else width
    every = pl.ds(base, width)
    if part != "rest":
        mine = mine.at[:, every]

    def piece(cols, **fixed):
        return full.at[tuple(fixed.get(a, at[a]) for a in "xczy") + (ALL, cols)]

    def spread(axis, done, cols, src=None):
        here = piece(cols, **{a: ALL for a in done})
        return [wires.wire(here if src is None else src, here, axis, k) for k in near.shifts(axis)]

    def forward(axis, done, cols):
        size = near.sizes[axis]
        parts = [piece(cols, **{a: ALL for a in done}, **{axis: near.along(axis, size - k)}) for k in near.shifts(axis)]
        return [wires.wire(p, p, "c", 1) for p in parts]

    first, second = halves(width, base)
    whole_z = [] if part == "rest" else spread("z", "", every, mine)
    column = piece(every, z=ALL)
    pair = [wires.wire(column, column, "c", 1)]
    one, two, one_on, two_on = [], [], [], []
    for cols, (a, b) in ((first, "yx"), (second, "xy")):
        one += spread(a, "z", cols)
        one_on += forward(a, "z", cols)
        two += spread(b, "z" + a, cols)
        two_on += forward(b, "z" + a, cols)
    keep = lambda: pltpu.make_async_copy(mine, piece(every), own)

    def stage0():
        keep().start()
        start(whole_z)

    def arrive():
        keep().wait()
        landed(whole_z)
        left(whole_z)

    def stage1():
        if part != "rest":
            arrive()
        start(one, pair)

    def stage2():
        landed(one)
        start(two, one_on)

    def stage3():
        landed(two)
        start(two_on)

    def stage4():
        left(pair, one, two, one_on, two_on)
        landed(pair, one_on, two_on)

    return [stage0, arrive] if part == "first" else [stage0, stage1, stage2, stage3, stage4]


def gather_scratch(sizes):
    n = gather_wires(sizes)
    return [pltpu.SemaphoreType.DMA((n,)), pltpu.SemaphoreType.DMA((n,)), pltpu.SemaphoreType.DMA(())]


def lead(sizes):
    return (sizes["x"], 2, sizes["z"], sizes["y"])


def gathered(sizes, arrays):
    return [jax.ShapeDtypeStruct(lead(sizes) + a.shape, a.dtype) for a in arrays]


def scatter_wires(sizes):
    return 1 + 2 * (sizes["x"] + sizes["y"] - 2) + sizes["z"] - 1


SCATTER_REFS = 10


def scatter_scratch(sizes, block, width, kind):
    nx, ny, nz = sizes["x"], sizes["y"], sizes["z"]
    first, second = halves(width)
    a, b = first.size, second.size
    vmem = lambda *shape: pltpu.VMEM(shape, kind)
    n = scatter_wires(sizes)
    return [
        vmem(nx, nz, ny, block, width), vmem(nx, nz, ny, block, width),
        vmem(nx - 1, nz, ny, block, a), vmem(ny - 1, nx, nz, block, b),
        vmem(ny - 1, nz, block, a), vmem(nx - 1, nz, block, b),
        vmem(nz - 1, block, width),
        pltpu.SemaphoreType.DMA((n,)), pltpu.SemaphoreType.DMA((n,)), pltpu.SemaphoreType.DMA(()),
    ]


def scatter_stages(near, grad, out, held, got, x_first, y_first, y_then, x_then, z_last, send, recv, own, early=False):
    wires = Wires(near, send, recv)
    at, sizes = near.at, near.sizes
    nz, ny, nx = sizes["z"], sizes["y"], sizes["x"]
    x, y, z = at["x"], at["y"], at["z"]
    first, second = halves(held.shape[-1])
    loads = [] if own is None else [lambda: pltpu.make_async_copy(grad.at[:, at["c"]], held, own)]
    pair = [wires.wire(grad.at[:, 1 - at["c"]], got, "c", 1)]
    one = [wires.wire(held.at[near.along("x", k), :, :, :, first], x_first.at[k - 1], "x", k) for k in near.shifts("x")]
    one += [wires.wire(held.at[:, :, near.along("y", k), :, second], y_first.at[k - 1], "y", k) for k in near.shifts("y")]
    two = [wires.wire(held.at[x, :, near.along("y", k), :, first], y_then.at[k - 1], "y", k) for k in near.shifts("y")]
    two += [wires.wire(held.at[near.along("x", k), :, y, :, second], x_then.at[k - 1], "x", k) for k in near.shifts("x")]
    last = [wires.wire(held.at[x, near.along("z", k), y], z_last.at[k - 1], "z", k) for k in near.shifts("z")]

    def add(where, terms):
        held[where] = sum([t.astype(F32) for t in terms], held[where].astype(F32)).astype(held.dtype)

    def over_z(body):
        lax.fori_loop(0, nz, lambda i, carry: (body(i), carry)[1], 0)

    def stage0():
        start(pair, loads)

    def stage1():
        for load in loads:
            load().wait()
        landed(pair)

        @over_z
        def _(i):
            for a in range(nx):
                for b in range(ny):
                    if own is None:
                        held[a, i, b] = (grad[a, at["c"], i, b].astype(F32) + got[a, i, b].astype(F32)).astype(held.dtype)
                    else:
                        add((a, i, b), [got[a, i, b]])

        start(one)

    def stage2():
        landed(one)

        @over_z
        def _(i):
            for b in range(ny):
                add((x, i, b, ALL, first), [x_first[k - 1, i, b] for k in near.shifts("x")])
            for a in range(nx):
                add((a, i, y, ALL, second), [y_first[k - 1, a, i] for k in near.shifts("y")])

        start(two)

    def stage3():
        landed(two)

        @over_z
        def _(i):
            add((x, i, y, ALL, first), [y_then[k - 1, i] for k in near.shifts("y")])
            add((x, i, y, ALL, second), [x_then[k - 1, i] for k in near.shifts("x")])
            if early:
                out[i] = held[x, i, y]

        if early:
            left(pair, one, two)
        else:
            start(last)

    def stage4():
        landed(last)
        out[...] = sum([z_last[k - 1].astype(F32) for k in near.shifts("z")], held[x, z, y].astype(F32))
        left(pair, one, two, last)

    return [stage0, stage1, stage2, stage3] if early else [stage0, stage1, stage2, stage3, stage4]


def column_stages(near, column, out, z_last, send, recv):
    wires = Wires(near, send, recv)
    last = [wires.wire(column.at[near.along("z", k)], z_last.at[k - 1], "z", k) for k in near.shifts("z")]

    def finish():
        landed(last)
        out[...] = sum([z_last[k - 1].astype(F32) for k in near.shifts("z")], column[near.at["z"]].astype(F32))
        left(last)

    return [lambda: start(last), finish]


def total_scratch(sizes, shape):
    n = sum(sizes[a] - 1 for a in "cxyz")
    return [pltpu.VMEM((n,) + shape, F32), pltpu.VMEM((3,) + shape, F32), pltpu.SemaphoreType.DMA((n,)), pltpu.SemaphoreType.DMA((n,))]


def total_stages(near, mine, out, got, held, send, recv):
    wires = Wires(near, send, recv)
    groups, slots = [], []
    for step, axis in enumerate("cxyz"):
        src = mine if step == 0 else held.at[step - 1]
        slots.append([wires.used + k - 1 for k in near.shifts(axis)])
        groups.append([wires.wire(src, got.at[wires.used], axis, k) for k in near.shifts(axis)])

    def stage(step):
        def run():
            if step > 0:
                landed(groups[step - 1])
                total = mine[...] if step == 1 else held[step - 2]
                for slot in slots[step - 1]:
                    total = total + got[slot]
                if step < 4:
                    held[step - 1] = total
                else:
                    out[...] = total
                    left(*groups)
            if step < 4:
                start(groups[step])

        return run

    return [stage(step) for step in range(5)]


def blocks_of(sizes, grads):
    return [g.reshape(lead(sizes) + (-1, g.shape[1])) for g in grads]


def pump(schedule, plans, chunk):
    for step in sorted({at[0] for at in schedule if at[1] == chunk}):

        @pl.when(pl.program_id(0) == step)
        def _():
            for plan, stage in schedule[step, chunk]:
                plans[plan][stage]()


def mesh_sizes(mesh):
    fsdp = mesh.shape["fsdp"]
    ny = 1 << ((fsdp.bit_length() - 1) // 2)
    return {"x": mesh.shape["dp"] // 2, "c": 2, "z": fsdp // ny, "y": ny}


def project_kernel(x_ref, w_ref, gain_ref, shift_ref, offset_ref, a1_ref, qkv_ref):
    @pl.when(pl.program_id(0) == 0)
    def _():
        def body(rows):
            unit, _ = normalised(x_ref[rows, :].astype(F32))
            a1_ref[rows, :] = (unit * gain_ref[...] + shift_ref[...]).astype(BF)

        row_loop(x_ref.shape[0], 352, body)

    qkv_ref[...] = (dot(a1_ref[...], w_ref[...], 1, 0) + offset_ref[...]).astype(BF)


def project(x, w_in, gain, shift, offset):
    rows, d = x.shape
    return pl.pallas_call(
        project_kernel,
        grid=(3,),
        in_specs=[
            whole((rows, d)),
            pl.BlockSpec((d, d), lambda t: (0, t)),
            whole((1, d)),
            whole((1, d)),
            pl.BlockSpec((1, d), lambda t: (0, t)),
        ],
        out_specs=[whole((rows, d)), pl.BlockSpec((rows, d), lambda t: (0, t))],
        out_shape=[
            jax.ShapeDtypeStruct((rows, d), BF),
            jax.ShapeDtypeStruct((rows, 3 * d), BF),
        ],
        compiler_params=params(),
        cost_estimate=cost(6 * rows * d * d, 2 * (5 * rows * d + 3 * d * d)),
        name="project",
    )(x, w_in, gain, shift, offset)


VEC_ROWS = 16
UP_ROW = 10


def placed(value, width, device):
    size = value.shape[-1]
    row = lax.broadcasted_iota(jnp.int32, (size, width), 0)
    column = lax.broadcasted_iota(jnp.int32, (size, width), 1)
    return dot(value, (column == row + device * size).astype(BF), 1, 0)


def enter_kernel(sizes, tile, x_ref, w_ref, seg_ref, wo_ref, wu_ref, *refs):
    vec_refs, (a1_out, qkv_out, w_out, vecs_ref, mark_ref, far_ref, wo_full, wu_full) = refs[:10], refs[10:18]
    a1_ref, qkv_ref, w_full, unit_ref, mine_ref, third_ref = refs[18:24]
    small_refs, gather_refs, ahead_refs, out_sems = refs[24:28], refs[28:37], refs[37:43], refs[43]
    rows, d = x_ref.shape
    near = Near(sizes)
    near.greet()
    device = lax.axis_index(AXES)
    mine_ref[...] = jnp.zeros_like(mine_ref)
    in_bias, *plain = vec_refs
    up_bias = plain.pop(4)
    for i, ref in enumerate(plain):
        mine_ref[i : i + 1, :] = placed(ref[...], d, device)
    both = placed(in_bias[...], 2 * d, device)
    mine_ref[8:9, :] = both[:, :d]
    mine_ref[9:10, :] = both[:, d:]
    up = placed(up_bias[...], 4 * d, device)
    for i in range(4):
        mine_ref[UP_ROW + i : UP_ROW + i + 1, :] = up[:, d * i : d * (i + 1)]
    plans = [
        gather_stages(near, w_ref, w_full, *gather_refs[3 * t : 3 * t + 3], base=d * t, width=d) for t in range(3)
    ]
    ahead = [
        gather_stages(near, wo_ref, wo_full, *ahead_refs[:3], part="first"),
        gather_stages(near, wu_ref, wu_full, *ahead_refs[3:], part="first"),
    ]
    small = total_stages(near, mine_ref, vecs_ref, *small_refs)
    for plan in plans:
        plan[0]()

    def body(index, carry):
        span = pl.ds(pl.multiple_of(index * tile, tile), tile)
        unit_ref[span, :], _ = normalised(x_ref[span, :].astype(F32))
        for step in range(3):
            pl.when(index == step)(small[step])
        return carry

    lax.fori_loop(0, rows // tile, body, 0)
    plans[0][1]()
    small[3]()
    for plan in ahead:
        plan[0]()
    image = lax.broadcasted_iota(jnp.int32, (128, rows), 0) % HD
    same = seg_ref[...] == image
    mark_ref[...] = same.astype(F32).T.astype(BF)
    far_ref[...] = jnp.where(same | (image > PADDING), 0.0, FAR).T.astype(BF)
    plans[1][1]()
    plans[0][2]()
    plans[2][1]()
    plans[1][2]()
    small[4]()

    def shifted(span):
        a1_ref[span, :] = (unit_ref[span, :] * vecs_ref[1:2, :] + vecs_ref[2:3, :]).astype(BF)

    row_loop(rows, tile, shifted)
    sends = [pltpu.make_async_copy(a1_ref, a1_out, out_sems.at[0])]
    sends[0].start()

    def third(t):
        cols = slice(d * t, d * (t + 1))
        third_ref[...] = w_full[:, :, :, :, :, cols].astype(F32).reshape(d, d).astype(BF)

        def body(span):
            value = dot(a1_ref[span, :], third_ref[...], 1, 0)
            if t != 1:
                value = value + vecs_ref[8 + t // 2 : 9 + t // 2, :]
            qkv_ref[span, cols] = value.astype(BF)

        row_loop(rows, rows // 2, body)

    def store(t):
        cols = pl.ds(d * t, d)
        sends.append(pltpu.make_async_copy(qkv_ref.at[:, cols], qkv_out.at[:, cols], out_sems.at[1 + t]))
        sends[-1].start()

    plans[0][3]()
    plans[2][2]()
    plans[0][4]()
    third(0)
    plans[1][3]()
    store(0)
    plans[1][4]()
    plans[2][3]()
    third(1)
    store(1)
    plans[2][4]()
    sends.append(pltpu.make_async_copy(w_full, w_out, out_sems.at[4]))
    sends[-1].start()
    third(2)
    store(2)
    for plan in ahead:
        plan[1]()
    for copy in sends:
        copy.wait()


def enter(sizes, x, w_in, segment_ids, w_out, w_up, vectors, tile=352):
    rows, d = x.shape
    vmem, hbm = pl.BlockSpec(memory_space=pltpu.VMEM), pl.BlockSpec(memory_space=pltpu.HBM)
    full = lead(sizes) + w_in.shape
    return pl.pallas_call(
        functools.partial(enter_kernel, sizes, tile),
        in_specs=[vmem] * 15,
        out_specs=[hbm, hbm, hbm, vmem, vmem, vmem, hbm, hbm],
        out_shape=[
            jax.ShapeDtypeStruct((rows, d), BF),
            jax.ShapeDtypeStruct((rows, 3 * d), BF),
            jax.ShapeDtypeStruct(full, BF),
            jax.ShapeDtypeStruct((VEC_ROWS, d), F32),
            jax.ShapeDtypeStruct((rows, 128), BF),
            jax.ShapeDtypeStruct((rows, 128), BF),
            *gathered(sizes, [w_out, w_up]),
        ],
        scratch_shapes=[
            pltpu.VMEM((rows, d), BF),
            pltpu.VMEM((rows, 3 * d), BF),
            pltpu.VMEM(full, BF),
            pltpu.VMEM((rows, d), F32),
            pltpu.VMEM((VEC_ROWS, d), F32),
            pltpu.VMEM((d, d), BF),
            *total_scratch(sizes, (VEC_ROWS, d)),
            *gather_scratch(sizes) * 5,
            pltpu.SemaphoreType.DMA((5,)),
        ],
        compiler_params=params(collective_id=0, has_side_effects=True),
        name="enter",
    )(x, w_in, segment_ids[None], w_out, w_up, *[v[None] for v in vectors])


def chunks(rows, size):
    return [(start, min(size, rows - start)) for start in range(0, rows, size)]


GATHER_AT = {
    (0, 0): [(2, 0), (1, 1), (0, 1)],
    (1, 0): [(1, 2)],
    (2, 0): [(2, 1)],
    (3, 0): [(0, 2), (1, 3), (2, 2)],
    (4, 0): [(0, 3)],
    (5, 0): [(2, 3), (0, 4)],
    (5, -1): [(1, 4), (2, 4)],
}


def attend_kernel(chunk, sizes, count, q_ref, k_ref, v_ref, mark_ref, far_ref, *refs):
    shards, (o_ref, e_ref, inv_ref) = refs[:count][::-1], refs[count : count + 3]
    full, (vt_ref, k2_ref), sems = refs[count + 3 : 2 * count + 3], refs[2 * count + 3 : 2 * count + 5], refs[2 * count + 5 :]
    rows = q_ref.shape[0]
    plans, schedule = [], {}
    if count:
        near, schedule = Near(sizes), GATHER_AT
        pl.when(pl.program_id(0) == 0)(near.greet)
        plans = [
            gather_stages(near, shards[i], full[i], *sems[3 * i : 3 * i + 3], part="all" if i == 2 else "rest") for i in range(count)
        ]
    vt_ref[...] = v_ref[...].astype(F32).T.astype(BF)
    low = lax.broadcasted_iota(jnp.int32, (1, 128), 1) < HD
    for half in range(2):
        mine = low if half == 0 else jnp.logical_not(low)
        k2_ref[half] = jnp.where(mine, k_ref[...], far_ref[...])
    for turn, (start, size) in enumerate(chunks(rows, chunk)):
        pump(schedule, plans, turn)
        for half in range(2):
            mine = low if half == 0 else jnp.logical_not(low)
            span = pl.ds(start, size)
            query = jnp.where(mine, q_ref[span, :], mark_ref[span, :])
            scores = dot(k2_ref[half], query, 1, 1)
            top = jnp.max(scores, axis=0, keepdims=True)
            weights = jnp.exp2((scores - top) * (LOG2E * HD ** (-0.5)))
            total = jnp.sum(weights, axis=0, keepdims=True)
            weights_low = weights.astype(BF)
            e_ref[half, :, span] = weights_low
            inverse = 1.0 / total
            inv_ref[0, half : half + 1, span] = inverse
            head = pl.ds(half * HD, HD)
            o_ref[head, span] = (dot(vt_ref[head, :], weights_low, 1, 0) * inverse).astype(BF)
    pump(schedule, plans, -1)


def attend(qkv, mark, far, sizes, shards, chunk=704):
    count = len(shards)
    hbm = pl.BlockSpec(memory_space=pltpu.HBM)
    rows, width = qkv.shape
    pairs = width // 384
    return pl.pallas_call(
        functools.partial(attend_kernel, chunk, sizes, count),
        grid=(pairs,),
        in_specs=[
            pl.BlockSpec((rows, 128), lambda p: (0, p)),
            pl.BlockSpec((rows, 128), lambda p: (0, pairs + p)),
            pl.BlockSpec((rows, 128), lambda p: (0, 2 * pairs + p)),
            whole((rows, 128)),
            whole((rows, 128)),
            *([whole(shards[2].shape), hbm, hbm] if count else []),
        ],
        out_specs=[
            pl.BlockSpec((128, rows), lambda p: (p, 0)),
            pl.BlockSpec((2, rows, rows), lambda p: (p, 0, 0)),
            pl.BlockSpec((1, 2, rows), lambda p: (p, 0, 0)),
            *[hbm] * count,
        ],
        out_shape=[
            jax.ShapeDtypeStruct((pairs * 128, rows), BF),
            jax.ShapeDtypeStruct((2 * pairs, rows, rows), BF),
            jax.ShapeDtypeStruct((pairs, 2, rows), F32),
            *([*shards[:2], *gathered(sizes, shards[2:])] if count else []),
        ],
        scratch_shapes=[
            pltpu.VMEM((128, rows), BF),
            pltpu.VMEM((2, rows, 128), BF),
            *(gather_scratch(sizes) * count if count else []),
        ],
        compiler_params=params(collective_id=1, has_side_effects=True) if count else params(),
        cost_estimate=cost(2 * pairs * 4 * rows * rows * 256, 4 * pairs * rows * rows, 2 * pairs * rows * rows),
        input_output_aliases={7: 3, 6: 4} if count else {},
        name="attend",
    )(qkv, qkv, qkv, mark, far, *shards[::-1])


def masked(g_ref, mark_ref, rows):
    padding = mark_ref[rows, PADDING : PADDING + 1].astype(F32)
    return jnp.where(padding > 0, 0.0, g_ref[rows, :].astype(F32))


def middle_kernel(o_ref, x_ref, g_ref, mark_ref, w_ref, vec_ref, m1_ref, a2_ref, gm_ref, gmsum_ref):
    bias, scale1, gain2, shift2, scale2 = (vec_ref[i : i + 1, :] for i in (0, 3, 5, 6, 7))
    m1_ref[...] = dot(o_ref[...], w_ref[...], 0, 0)
    gmsum_ref[...] = jnp.zeros_like(gmsum_ref)

    def body(rows):
        m1 = x_ref[rows, :].astype(F32) + scale1 * (m1_ref[rows, :] + bias)
        m1_ref[rows, :] = m1
        unit, _ = normalised(m1)
        a2_ref[rows, :] = (unit * gain2 + shift2).astype(BF)
        gm = (scale2 * masked(g_ref, mark_ref, rows)).astype(BF)
        gm_ref[rows, :] = gm
        gmsum_ref[...] += jnp.sum(gm.astype(F32).reshape(-1, 8, gm.shape[-1]), axis=0)

    row_loop(x_ref.shape[0], 352, body)


def middle(o, x, g, mark, w_out, vec):
    rows, d = x.shape
    return pl.pallas_call(
        middle_kernel,
        out_shape=[
            jax.ShapeDtypeStruct((rows, d), F32),
            jax.ShapeDtypeStruct((rows, d), BF),
            jax.ShapeDtypeStruct((rows, d), BF),
            jax.ShapeDtypeStruct((8, d), F32),
        ],
        compiler_params=params(),
        cost_estimate=cost(2 * rows * d * d, 14 * rows * d),
        name="middle",
    )(o, x, g, mark, w_out, vec)


def gelu_parts(u):
    near = jnp.abs(u)
    t = 1.0 / (1.0 + (0.3275911 * 0.7071067811865476) * near)
    bell = jnp.exp2((-0.5 * LOG2E) * (u * u))
    poly = t * (
        0.5 * 0.254829592
        + t * (0.5 * -0.284496736 + t * (0.5 * 1.421413741 + t * (0.5 * -1.453152027 + t * (0.5 * 1.061405429))))
    )
    tail = poly * bell
    phi = jnp.where(u < 0, tail, 1.0 - tail)
    return u * phi, phi + u * bell * 0.3989422804014327


def feed_kernel(chunk, a2_ref, gm_ref, up_ref, vec_ref, down_ref, bm_ref, ga_ref, dup_ref, ddown_ref, dub_ref, gl_ref, gu_ref):
    first = pl.program_id(0) == 0

    @pl.when(first)
    def _():
        bm_ref[...] = jnp.zeros_like(bm_ref)
        ga_ref[...] = jnp.zeros_like(ga_ref)

    d = vec_ref.shape[-1]
    spread = up_ref.shape[-1] // d
    bias = jnp.concatenate([vec_ref[pl.ds(UP_ROW + pl.program_id(0) * spread + i, 1), :] for i in range(spread)], axis=1)
    total = jnp.zeros((8, up_ref.shape[-1]), F32)
    for start, size in chunks(a2_ref.shape[0], chunk):
        rows = pl.ds(start, size)
        u = dot(a2_ref[rows, :], up_ref[...], 1, 0) + bias
        back = dot(gm_ref[rows, :], down_ref[...], 1, 1)
        active, slope = gelu_parts(u)
        low = active.astype(BF)
        gl_ref[rows, :] = low
        gu = (slope * back).astype(BF)
        gu_ref[rows, :] = gu
        total += jnp.sum(gu.astype(F32).reshape(-1, 8, gu.shape[-1]), axis=0)
        bm_ref[rows, :] += dot(low, down_ref[...], 1, 0)
        ga_ref[rows, :] += dot(gu, up_ref[...], 1, 1)
    dub_ref[...] = total
    ddown_ref[...] = dot(gl_ref[...], gm_ref[...], 0, 0).astype(ddown_ref.dtype)
    dup_ref[...] = dot(a2_ref[...], gu_ref[...], 0, 0).astype(dup_ref.dtype)


def feed(a2, gm, w_up, vecs, w_down, block=768, chunk=704, kind=BF):
    rows, d = a2.shape
    ff = w_up.shape[1]
    return pl.pallas_call(
        functools.partial(feed_kernel, chunk),
        grid=(ff // block,),
        in_specs=[
            whole((rows, d)),
            whole((rows, d)),
            pl.BlockSpec((d, block), lambda f: (0, f)),
            whole((VEC_ROWS, d)),
            pl.BlockSpec((block, d), lambda f: (f, 0)),
        ],
        out_specs=[
            whole((rows, d)),
            whole((rows, d)),
            pl.BlockSpec((d, block), lambda f: (0, f)),
            pl.BlockSpec((block, d), lambda f: (f, 0)),
            pl.BlockSpec((8, block), lambda f: (0, f)),
        ],
        out_shape=[
            jax.ShapeDtypeStruct((rows, d), F32),
            jax.ShapeDtypeStruct((rows, d), F32),
            jax.ShapeDtypeStruct((d, ff), kind),
            jax.ShapeDtypeStruct((ff, d), kind),
            jax.ShapeDtypeStruct((8, ff), F32),
        ],
        scratch_shapes=[pltpu.VMEM((rows, block), BF), pltpu.VMEM((rows, block), BF)],
        compiler_params=params(),
        cost_estimate=cost(12 * rows * d * ff, 4 * 4 * d * ff),
        name="feed",
    )(a2, gm, w_up, vecs, w_down)


def join_kernel(size, m1_ref, bm_ref, ga_ref, x_ref, g_ref, mark_ref, o_ref, w_ref, vec_ref, out_ref, gm1_ref, go_ref, dout_ref, sums_ref, gb_ref):
    bias2, scale1, gain2, scale2 = (vec_ref[i : i + 1, :] for i in (4, 3, 5, 7))
    step = pl.program_id(0)

    @pl.when(step == 0)
    def _():
        sums_ref[...] = jnp.zeros_like(sums_ref)

    base = step * m1_ref.shape[0]

    def body(rows):
        m1 = m1_ref[rows, :]
        bm = bm_ref[rows, :] + bias2
        g = masked(g_ref, mark_ref, rows)
        out_ref[rows, :] = (m1 + scale2 * bm).astype(BF)
        unit, inverse = normalised(m1)
        ga = ga_ref[rows, :]
        gm1 = g + norm_back(unit, inverse, ga * gain2)
        gm1_ref[rows, :] = gm1
        gb = (scale1 * gm1).astype(BF)
        gb_ref[pl.ds(pl.multiple_of(base + rows.start, size), size), :] = gb
        for index, value in enumerate(
            (g * bm, ga * unit, ga, gm1 * (m1 - x_ref[rows, :].astype(F32)), gb.astype(F32))
        ):
            sums_ref[index] += jnp.sum(value.reshape(-1, 8, value.shape[-1]), axis=0)

    row_loop(m1_ref.shape[0], size, body)

    @pl.when(step == pl.num_programs(0) - 1)
    def _():
        go_ref[...] = dot(w_ref[...], gb_ref[...], 1, 1).astype(BF)
        dout_ref[...] = dot(o_ref[...], gb_ref[...], 1, 0).astype(dout_ref.dtype)


def join(m1, bm, ga, x, g, mark, o, w_out, vec, tile=352, kind=BF):
    rows, d = x.shape
    by_rows = pl.BlockSpec((tile, d), lambda i: (i, 0))
    return pl.pallas_call(
        functools.partial(join_kernel, 352),
        grid=(rows // tile,),
        in_specs=[by_rows] * 5 + [pl.BlockSpec((tile, 128), lambda i: (i, 0)), whole((d, rows)), whole((d, d)), whole((VEC_ROWS, d))],
        out_specs=[by_rows, by_rows, whole((d, rows)), whole((d, d)), whole((5, 8, d))],
        out_shape=[
            jax.ShapeDtypeStruct((rows, d), BF),
            jax.ShapeDtypeStruct((rows, d), F32),
            jax.ShapeDtypeStruct((d, rows), BF),
            jax.ShapeDtypeStruct((d, d), kind),
            jax.ShapeDtypeStruct((5, 8, d), F32),
        ],
        scratch_shapes=[pltpu.VMEM((rows, d), BF)],
        compiler_params=params(),
        cost_estimate=cost(4 * rows * d * d, 26 * rows * d),
        name="join",
    )(m1, bm, ga, x, g, mark, o, w_out, vec)


SCATTER_AT = {
    (0, 0): [(0, 0), (2, 0)],
    (1, 0): [(0, 1)],
    (2, 0): [(1, 0), (2, 1)],
    (3, 0): [(0, 2), (1, 1)],
    (4, 0): [(2, 2), (0, 3)],
    (5, 0): [(1, 2), (2, 3)],
    (5, -1): [(1, 3), (2, 4), (0, 4)],
}


def attend_back_kernel(chunk, sizes, count, q_ref, k_ref, v_ref, go_ref, o_ref, e_ref, inv_ref, *refs):
    grads, out_ref, sums = refs[:count], refs[count], refs[count + 1 : 2 * count + 1]
    (kt_ref, gq_ref, gs_ref, gp_ref), rest = refs[2 * count + 1 : 2 * count + 5], refs[2 * count + 5 :]
    rows = q_ref.shape[0]
    plans, schedule = [], {}
    if count:
        near, schedule = Near(sizes), SCATTER_AT
        pl.when(pl.program_id(0) == 0)(near.greet)
        plans = [
            scatter_stages(near, grads[i], sums[i], *rest[SCATTER_REFS * i : SCATTER_REFS * (i + 1)], early=i == 1)
            for i in range(count)
        ]
    factor = HD ** (-0.5)
    kt_ref[...] = k_ref[...].astype(F32).T.astype(BF)
    low = lax.broadcasted_iota(jnp.int32, (1, 128), 1) < HD
    below = lax.broadcasted_iota(jnp.int32, (128, 1), 0) < HD
    gp_ref[...] = jnp.zeros_like(gp_ref)
    for turn, (start, size) in enumerate(chunks(rows, chunk)):
        pump(schedule, plans, turn)
        span = pl.ds(start, size)
        for half in range(2):
            head = pl.ds(half * HD, HD)
            incoming = go_ref[head, span].astype(F32) * inv_ref[0, half : half + 1, span]
            centre = jnp.sum(incoming * o_ref[head, span].astype(F32), axis=0, keepdims=True)
            gp_ref[half, head, span] = incoming.astype(BF)
            gp = dot(v_ref[...], gp_ref[half, :, span], 1, 0)
            gs = (e_ref[half, :, span].astype(F32) * (gp - centre)).astype(BF)
            gs_ref[half, :, span] = gs
            gq_ref[head, span] = dot(kt_ref[head, :], gs, 1, 0) * factor
    out_ref[0] = gq_ref[...].T.astype(BF)
    gk = [dot(gs_ref[half], q_ref[...], 1, 0) for half in range(2)]
    out_ref[1] = (jnp.where(low, gk[0], gk[1]) * factor).astype(BF)
    out_ref[2] = (dot(e_ref[0], gp_ref[0], 1, 1) + dot(e_ref[1], gp_ref[1], 1, 1)).astype(BF)
    pump(schedule, plans, -1)


def attend_back(qkv, go, o, e, inv, sizes, grads, chunk=512):
    blocks = blocks_of(sizes, grads) if grads else []
    count = len(blocks)
    sums = [jax.ShapeDtypeStruct(b.shape[-2:], F32) for b in blocks]
    if count:
        sums[1] = jax.ShapeDtypeStruct((sizes["z"],) + sums[1].shape, BF)
    rows, width = qkv.shape
    pairs = width // 384
    return pl.pallas_call(
        functools.partial(attend_back_kernel, chunk, sizes, count),
        grid=(pairs,),
        in_specs=[
            pl.BlockSpec((rows, 128), lambda p: (0, p)),
            pl.BlockSpec((rows, 128), lambda p: (0, pairs + p)),
            pl.BlockSpec((rows, 128), lambda p: (0, 2 * pairs + p)),
            pl.BlockSpec((128, rows), lambda p: (p, 0)),
            pl.BlockSpec((128, rows), lambda p: (p, 0)),
            pl.BlockSpec((2, rows, rows), lambda p: (p, 0, 0)),
            pl.BlockSpec((1, 2, rows), lambda p: (p, 0, 0)),
            *[pl.BlockSpec(memory_space=pltpu.HBM)] * count,
        ],
        out_specs=[pl.BlockSpec((3, rows, 128), lambda p: (0, 0, p)), *[whole(v.shape) for v in sums]],
        out_shape=[
            jax.ShapeDtypeStruct((3, rows, pairs * 128), BF),
            *sums,
        ],
        scratch_shapes=[
            pltpu.VMEM((128, rows), BF),
            pltpu.VMEM((128, rows), F32),
            pltpu.VMEM((2, rows, rows), BF),
            pltpu.VMEM((2, 128, rows), BF),
            *[s for b in blocks for s in scatter_scratch(sizes, *b.shape[-2:], b.dtype)],
        ],
        compiler_params=params(collective_id=2, has_side_effects=True) if count else params(),
        cost_estimate=cost(2 * pairs * 8 * rows * rows * 256, 4 * pairs * rows * rows),
        name="attend_back",
    )(qkv, qkv, qkv, go, o, e, inv, *blocks)


def finish_kernel(a1_ref, gqkv_ref, w_ref, x_ref, gm1_ref, gain_ref, dw_ref, cols_ref, gx_ref, sums_ref, ga_ref):
    step = pl.program_id(0)
    grads = gqkv_ref[0]
    dw_ref[...] = dot(a1_ref[...], grads, 0, 0).astype(dw_ref.dtype)
    cols_ref[0] = jnp.sum(grads.astype(F32).reshape(-1, 8, grads.shape[-1]), axis=0)
    part = dot(grads, w_ref[...], 1, 1)

    @pl.when(step == 0)
    def _():
        ga_ref[...] = part

    @pl.when(step > 0)
    def _():
        ga_ref[...] += part

    @pl.when(step == pl.num_programs(0) - 1)
    def _():
        sums_ref[...] = jnp.zeros_like(sums_ref)

        def body(rows):
            unit, inverse = normalised(x_ref[rows, :].astype(F32))
            ga = ga_ref[rows, :]
            gx_ref[rows, :] = gm1_ref[rows, :] + norm_back(unit, inverse, ga * gain_ref[...])
            for index, value in enumerate((ga * unit, ga)):
                sums_ref[index] += jnp.sum(value.reshape(-1, 8, value.shape[-1]), axis=0)

        row_loop(x_ref.shape[0], 352, body)


def finish(a1, gqkv, w_in, x, gm1, gain, kind=BF):
    rows, d = x.shape
    return pl.pallas_call(
        finish_kernel,
        grid=(3,),
        in_specs=[
            whole((rows, d)),
            pl.BlockSpec((1, rows, d), lambda t: (t, 0, 0)),
            pl.BlockSpec((d, d), lambda t: (0, t)),
            whole((rows, d)),
            whole((rows, d)),
            whole((1, d)),
        ],
        out_specs=[
            pl.BlockSpec((d, d), lambda t: (0, t)),
            pl.BlockSpec((1, 8, d), lambda t: (t, 0, 0)),
            whole((rows, d)),
            whole((2, 8, d)),
        ],
        out_shape=[
            jax.ShapeDtypeStruct((d, 3 * d), kind),
            jax.ShapeDtypeStruct((3, 8, d), F32),
            jax.ShapeDtypeStruct((rows, d), F32),
            jax.ShapeDtypeStruct((2, 8, d), F32),
        ],
        scratch_shapes=[pltpu.VMEM((rows, d), F32)],
        compiler_params=params(),
        cost_estimate=cost(12 * rows * d * d, 20 * rows * d),
        name="finish",
    )(a1, gqkv, w_in, x, gm1, gain)


def leave_kernel(sizes, tile, a1_in, gqkv_in, w_in, x_in, gm1_in, vec_ref, join_ref, ub_ref, gmsum_ref, column_ref, gx_out, dw_ref, early_ref, late_ref, ddown_ref, *refs):
    a1_ref, gqkv_ref, w_ref, x_ref, gm1_ref, gx_ref, ga_ref, sums_ref, mine_ref, last_ref = refs[:10]
    grad_refs, refs = refs[10:13], refs[13:]
    scatter_refs, refs = [refs[9 * t : 9 * t + 9] for t in range(3)], refs[27:]
    early_refs, late_refs, column_refs, in_sems, out_sems = refs[:4], refs[4:8], refs[8:11], refs[11], refs[12]
    rows, d = x_in.shape
    count = rows // tile
    moves = [(a1_in, a1_ref), *[(gqkv_in.at[t], gqkv_ref.at[t]) for t in range(3)], (w_in, w_ref), (x_in, x_ref), (gm1_in, gm1_ref)]
    fetch = [pltpu.make_async_copy(src, dst, in_sems.at[n]) for n, (src, dst) in enumerate(moves)]
    for copy in fetch:
        copy.start()
    near = Near(sizes)
    near.greet()
    row = lambda value: jnp.sum(value, axis=0, keepdims=True)
    mine_ref[...] = jnp.zeros_like(mine_ref)
    for i, value in enumerate(
        (row(join_ref[4]), row(join_ref[3]) / vec_ref[3:4, :], row(gmsum_ref[...]), row(join_ref[1]), row(join_ref[2]), row(join_ref[0]))
    ):
        mine_ref[i : i + 1, :] = value
    for i in range(4):
        mine_ref[8 + i : 9 + i, :] = row(ub_ref[:, d * i : d * (i + 1)])
    plans = [
        scatter_stages(near, grad_refs[t], dw_ref.at[:, pl.ds(d * t, d)], *scatter_refs[t], None) for t in range(3)
    ]
    early = total_stages(near, mine_ref, early_ref, *early_refs)
    late = total_stages(near, last_ref, late_ref, *late_refs)
    column = column_stages(near, column_ref, ddown_ref, *column_refs)
    column[0]()
    last_ref[...] = jnp.zeros_like(last_ref)

    def weight(t):
        fetch[1 + t].wait()
        value = dot(a1_ref[...], gqkv_ref[t], 0, 0)
        grad_refs[t][...] = value.reshape(grad_refs[t].shape).astype(BF)

    def back(t):
        def body(span):
            part = dot(gqkv_ref[t, span, :], w_ref[:, d * t : d * (t + 1)], 1, 1)
            ga_ref[span, :] = part if t == 0 else ga_ref[span, :] + part

        row_loop(rows, rows // 2, body)
        if t != 1:
            total = jnp.zeros((1, d), F32)
            for start_row, size in chunks(rows, tile):
                total += row(gqkv_ref[t, pl.ds(start_row, size), :].astype(F32))
            last_ref[2 + t // 2 : 3 + t // 2, :] = total

    fetch[0].wait()
    weight(0)
    early[0]()
    plans[0][0]()
    weight(1)
    plans[0][1]()
    plans[1][0]()
    early[1]()
    weight(2)
    plans[1][1]()
    plans[2][0]()
    fetch[4].wait()
    back(0)
    plans[0][2]()
    plans[2][1]()
    early[2]()
    back(1)
    plans[1][2]()
    back(2)
    plans[0][3]()
    column[1]()
    early[3]()
    fetch[5].wait()
    fetch[6].wait()
    sums_ref[...] = jnp.zeros_like(sums_ref)

    def send(index):
        span = pl.ds(pl.multiple_of(index * tile, tile), tile)
        return pltpu.make_async_copy(gx_ref.at[span], gx_out.at[span], out_sems.at[index])

    between = [[], [plans[2][2], plans[1][3]], []]

    def body(index, carry):
        span = pl.ds(pl.multiple_of(index * tile, tile), tile)
        unit, inverse = normalised(x_ref[span, :].astype(F32))
        ga = ga_ref[span, :]
        gx_ref[span, :] = gm1_ref[span, :] + norm_back(unit, inverse, ga * vec_ref[1:2, :])
        for n, value in enumerate((ga * unit, ga)):
            sums_ref[n] += jnp.sum(value.reshape(-1, 8, d), axis=0)
        for n, stages in enumerate(between):

            @pl.when(index == n)
            def _():
                for stage in stages:
                    stage()

        pl.when(index > 0)(lambda: send(index - 1).start())
        return carry

    lax.fori_loop(0, count, body, 0)
    for n in range(2):
        last_ref[n : n + 1, :] = row(sums_ref[n])
    late[0]()
    send(count - 1).start()
    early[4]()
    plans[2][3]()
    late[1]()
    plans[0][4]()
    late[2]()
    plans[1][4]()
    late[3]()
    plans[2][4]()
    late[4]()
    for index in range(count):
        send(index).wait()


def leave(sizes, a1, gqkv, w_in, x, gm1, vecs, join_sums, ub_sum, gm_sum, column, tile=352):
    rows, d = x.shape
    vmem, hbm = pl.BlockSpec(memory_space=pltpu.VMEM), pl.BlockSpec(memory_space=pltpu.HBM)
    block = d // (sizes["x"] * 2 * sizes["z"] * sizes["y"])
    return pl.pallas_call(
        functools.partial(leave_kernel, sizes, tile),
        in_specs=[hbm] * 5 + [vmem] * 5,
        out_specs=[hbm, vmem, vmem, vmem, vmem],
        out_shape=[
            jax.ShapeDtypeStruct((rows, d), F32),
            jax.ShapeDtypeStruct((block, 3 * d), F32),
            jax.ShapeDtypeStruct((16, d), F32),
            jax.ShapeDtypeStruct((8, d), F32),
            jax.ShapeDtypeStruct(column.shape[1:], F32),
        ],
        scratch_shapes=[
            pltpu.VMEM((rows, d), BF),
            pltpu.VMEM((3, rows, d), BF),
            pltpu.VMEM((d, 3 * d), BF),
            pltpu.VMEM((rows, d), BF),
            pltpu.VMEM((rows, d), F32),
            pltpu.VMEM((rows, d), F32),
            pltpu.VMEM((rows, d), F32),
            pltpu.VMEM((2, 8, d), F32),
            pltpu.VMEM((16, d), F32),
            pltpu.VMEM((8, d), F32),
            *[pltpu.VMEM(lead(sizes) + (block, d), BF)] * 3,
            *scatter_scratch(sizes, block, d, BF)[:-1] * 3,
            *total_scratch(sizes, (16, d)),
            *total_scratch(sizes, (8, d)),
            pltpu.VMEM((sizes["z"] - 1,) + column.shape[1:], BF),
            pltpu.SemaphoreType.DMA((sizes["z"] - 1,)),
            pltpu.SemaphoreType.DMA((sizes["z"] - 1,)),
            pltpu.SemaphoreType.DMA((7,)),
            pltpu.SemaphoreType.DMA((rows // tile,)),
        ],
        compiler_params=params(collective_id=3, has_side_effects=True),
        name="leave",
    )(a1, gqkv, w_in, x, gm1, vecs, join_sums, ub_sum, gm_sum, column)


def share_kernel(early_ref, late_ref, *refs):
    grads, outs, vec_outs = refs[:4], refs[4:8], refs[8:]
    for src, dst in zip(grads, outs):
        dst[...] = src[...]
    device = lax.axis_index(AXES)
    d = early_ref.shape[-1]

    def entries(ref, first_row, size):
        at = device * size
        line = ref[pl.ds(first_row + lax.div(at, d), 1), :]
        return pltpu.roll(jnp.broadcast_to(line, (8, d)), lax.rem(d - lax.rem(at, d), d), 1)[:1, :size]

    spots = [
        (late_ref, 2), (early_ref, 0), (late_ref, 0), (late_ref, 1), (early_ref, 1),
        (early_ref, 8), (early_ref, 2), (early_ref, 3), (early_ref, 4), (early_ref, 5),
    ]
    for (ref, first_row), out in zip(spots, vec_outs):
        out[...] = entries(ref, first_row, out.shape[-1])


def share(early, late, grads, sizes):
    vmem = pl.BlockSpec(memory_space=pltpu.VMEM)
    return pl.pallas_call(
        share_kernel,
        in_specs=[vmem] * 6,
        out_specs=[vmem] * 14,
        out_shape=[jax.ShapeDtypeStruct(g.shape, F32) for g in grads] + [jax.ShapeDtypeStruct((1, n), F32) for n in sizes],
        compiler_params=params(),
        name="share",
    )(early, late, *grads)


def take(a):
    return lax.all_gather(a, AXES, axis=0, tiled=True)


def give(g):
    return lax.psum_scatter(g, AXES, scatter_dimension=0, tiled=True).astype(F32)


def layer(
    sizes, inputs, segment_ids, cotangent, in_weight, in_bias, out_weight, out_bias, first_gain, first_shift, first_scale,
    up_weight, up_bias, down_weight, down_bias, second_gain, second_shift, second_scale,
):
    rows, d = inputs.shape
    vectors = (
        in_bias, out_bias, first_gain, first_shift, first_scale,
        up_bias, down_bias, second_gain, second_shift, second_scale,
    )
    own = all(w.shape[0] % 8 == 0 for w in (in_weight, out_weight, up_weight, down_weight))
    if own:
        a1, qkv, w_in, vecs, mark, far, *begun = enter(
            sizes, inputs, in_weight, segment_ids, out_weight, up_weight, vectors
        )
        w_in = w_in.reshape(d, 3 * d)
    else:
        w_in = take(in_weight)
        row = lambda v: take(v).astype(F32).reshape(-1, d)
        vecs = jnp.concatenate(
            [row(v) for v in (out_bias, first_gain, first_shift, first_scale, down_bias, second_gain, second_shift, second_scale, in_bias)]
            + [row(up_bias), jnp.zeros((VEC_ROWS - 14, d), F32)]
        )
        offset = jnp.concatenate([vecs[8:9], jnp.zeros((1, d), F32), vecs[9:10]], axis=1)
        a1, qkv = project(inputs, w_in, vecs[1:2], vecs[2:3], offset)
        lane = lax.broadcasted_iota(jnp.int32, (1, 128), 1) % HD
        same = segment_ids[:, None] == lane
        mark = same.astype(BF)
        far = jnp.where(same | (lane > PADDING), 0.0, FAR).astype(BF)
    o, e, inv, *full = attend(qkv, mark, far, sizes, [*begun, down_weight] if own else [])
    w_out, w_up, w_down = (
        (f.reshape(-1, f.shape[-1]) for f in full) if own else (take(w) for w in (out_weight, up_weight, down_weight))
    )
    m1, a2, gm, gm_sum = middle(o, inputs, cotangent, mark, w_out, vecs)
    bm, ga2, d_up, d_down, ub_sum = feed(a2, gm, w_up, vecs, w_down)
    outputs, gm1, go, d_out, join_sums = join(m1, bm, ga2, inputs, cotangent, mark, o, w_out, vecs)
    gqkv, *done = attend_back(qkv, go, o, e, inv, sizes, [d_up, d_down, d_out] if own else [])
    if own:
        d_up, column, d_out = done
        gx, d_in, early, late, d_down = leave(sizes, a1, gqkv, w_in, inputs, gm1, vecs, join_sums, ub_sum, gm_sum, column)
        d_up, d_down, d_out, d_in, *out = share(early, late, [d_up, d_down, d_out, d_in], [v.shape[0] for v in vectors])
        out = [v.reshape(-1) for v in out]
    else:
        d_in, col_sums, gx, last_sums = finish(a1, gqkv, w_in, inputs, gm1, vecs[1:2])
        d_in, d_up, d_down, d_out = (give(v) for v in (d_in, d_up, d_down, d_out))
        s = jnp.sum
        j, c, t = (s(v, axis=1) for v in (join_sums, col_sums, last_sums))
        sums = (
            jnp.concatenate([c[0], c[2]]), j[4], t[0], t[1], j[3] / vecs[3], s(ub_sum, axis=0), s(gm_sum, axis=0), j[1], j[2], j[0],
        )
        out = [give(v) for v in sums]
    return (
        outputs, gx, d_in, out[0], d_out, out[1], out[2], out[3], out[4],
        d_up, out[5], d_down, out[6], out[7], out[8], out[9],
    )


def solution(mesh):
    wide, flat = P(AXES, None), P(AXES)
    return jax.shard_map(
        functools.partial(layer, mesh_sizes(mesh)),
        mesh=mesh,
        in_specs=(wide, flat, wide, wide, flat, wide, flat, flat, flat, flat, wide, flat, wide, flat, flat, flat, flat),
        out_specs=(wide, wide, wide, flat, wide, flat, flat, flat, flat, wide, flat, wide, flat, flat, flat, flat),
        check_vma=False,
    )
```

```python
import functools

import jax
import jax.numpy as jnp
from jax import lax
from jax.experimental import pallas as pl
from jax.experimental.pallas import tpu as pltpu
from jax.sharding import PartitionSpec as P

HD = 64
PADDING = 5
EPSILON = 1e-06
LOG2E = 1.4426950408889634
FAR = -1e30
BF = jnp.bfloat16
F32 = jnp.float32
AXES = ("dp", "fsdp")
VMEM_LIMIT = 62 * 1024 * 1024


def dot(a, b, da, db):
    return lax.dot_general(a, b, (((da,), (db,)), ((), ())), preferred_element_type=F32)


def params(**more):
    return pltpu.CompilerParams(vmem_limit_bytes=VMEM_LIMIT, **more)


def cost(flops, moved, special=0):
    return pl.CostEstimate(flops=int(flops), bytes_accessed=int(moved), transcendentals=int(special))


def whole(shape):
    return pl.BlockSpec(shape, lambda *_: (0,) * len(shape), pipeline_mode=pl.Buffered(1))


def row_loop(rows, size, body):
    def step(index, carry):
        body(pl.ds(pl.multiple_of(index * size, size), size))
        return carry

    lax.fori_loop(0, rows // size, step, 0)


def normalised(values):
    centred = values - jnp.mean(values, axis=-1, keepdims=True)
    spread = jnp.mean(centred * centred, axis=-1, keepdims=True)
    inverse = lax.rsqrt(spread + EPSILON)
    return centred * inverse, inverse


def norm_back(unit, inverse, scaled):
    return inverse * (
        scaled
        - jnp.mean(scaled, axis=-1, keepdims=True)
        - unit * jnp.mean(scaled * unit, axis=-1, keepdims=True)
    )


MESH = pl.DeviceIdType.MESH
ALL = slice(None)


class Near:
    def __init__(self, sizes):
        self.sizes = sizes
        dp, fsdp = lax.axis_index("dp"), lax.axis_index("fsdp")
        ny = sizes["y"]
        self.at = {"x": lax.div(dp, 2), "c": lax.rem(dp, 2), "z": lax.div(fsdp, ny), "y": lax.rem(fsdp, ny)}

    def along(self, axis, shift):
        return lax.rem(self.at[axis] + shift, self.sizes[axis])

    def device(self, axis, shift):
        at = {**self.at, axis: self.along(axis, shift)}
        return (at["x"] * 2 + at["c"], at["z"] * self.sizes["y"] + at["y"])

    def shifts(self, axis):
        return range(1, self.sizes[axis])

    def greet(self):
        barrier = pltpu.get_barrier_semaphore()
        count = 0
        for axis in "cxyz":
            for shift in self.shifts(axis):
                pl.semaphore_signal(barrier, inc=1, device_id=self.device(axis, shift), device_id_type=MESH)
                count += 1
        pl.semaphore_wait(barrier, count)


class Wires:
    def __init__(self, near, send, recv):
        self.near, self.send, self.recv, self.used = near, send, recv, 0

    def wire(self, src, dst, axis, shift):
        n = self.used
        self.used += 1
        return lambda: pltpu.make_async_remote_copy(
            src_ref=src, dst_ref=dst, send_sem=self.send.at[n], recv_sem=self.recv.at[n],
            device_id=self.near.device(axis, shift), device_id_type=MESH,
        )


def start(*groups):
    for group in groups:
        for wire in group:
            wire().start()


def landed(*groups):
    for group in groups:
        for wire in group:
            wire().wait_recv()


def left(*groups):
    for group in groups:
        for wire in group:
            wire().wait_send()


def halves(width, base=0):
    cut = (width // 256) * 128
    return pl.ds(base, cut), pl.ds(base + cut, width - cut)


def gather_wires(sizes):
    return sizes["z"] + 4 * (sizes["x"] + sizes["y"] - 2)


def gather_stages(near, mine, full, send, recv, own, base=0, width=None, part="all"):
    wires = Wires(near, send, recv)
    at = near.at
    width = full.shape[-1] if width is None else width
    every = pl.ds(base, width)
    if part != "rest":
        mine = mine.at[:, every]

    def piece(cols, **fixed):
        return full.at[tuple(fixed.get(a, at[a]) for a in "xczy") + (ALL, cols)]

    def spread(axis, done, cols, src=None):
        here = piece(cols, **{a: ALL for a in done})
        return [wires.wire(here if src is None else src, here, axis, k) for k in near.shifts(axis)]

    def forward(axis, done, cols):
        size = near.sizes[axis]
        parts = [piece(cols, **{a: ALL for a in done}, **{axis: near.along(axis, size - k)}) for k in near.shifts(axis)]
        return [wires.wire(p, p, "c", 1) for p in parts]

    first, second = halves(width, base)
    whole_z = [] if part == "rest" else spread("z", "", every, mine)
    column = piece(every, z=ALL)
    pair = [wires.wire(column, column, "c", 1)]
    one, two, one_on, two_on = [], [], [], []
    for cols, (a, b) in ((first, "yx"), (second, "xy")):
        one += spread(a, "z", cols)
        one_on += forward(a, "z", cols)
        two += spread(b, "z" + a, cols)
        two_on += forward(b, "z" + a, cols)
    keep = lambda: pltpu.make_async_copy(mine, piece(every), own)

    def stage0():
        keep().start()
        start(whole_z)

    def arrive():
        keep().wait()
        landed(whole_z)
        left(whole_z)

    def stage1():
        if part != "rest":
            arrive()
        start(one, pair)

    def stage2():
        landed(one)
        start(two, one_on)

    def stage3():
        landed(two)
        start(two_on)

    def stage4():
        left(pair, one, two, one_on, two_on)
        landed(pair, one_on, two_on)

    return [stage0, arrive] if part == "first" else [stage0, stage1, stage2, stage3, stage4]


def gather_scratch(sizes):
    n = gather_wires(sizes)
    return [pltpu.SemaphoreType.DMA((n,)), pltpu.SemaphoreType.DMA((n,)), pltpu.SemaphoreType.DMA(())]


def lead(sizes):
    return (sizes["x"], 2, sizes["z"], sizes["y"])


def gathered(sizes, arrays):
    return [jax.ShapeDtypeStruct(lead(sizes) + a.shape, a.dtype) for a in arrays]


def scatter_wires(sizes):
    return 1 + 2 * (sizes["x"] + sizes["y"] - 2) + sizes["z"] - 1


SCATTER_REFS = 10


def scatter_scratch(sizes, block, width, kind):
    nx, ny, nz = sizes["x"], sizes["y"], sizes["z"]
    first, second = halves(width)
    a, b = first.size, second.size
    vmem = lambda *shape: pltpu.VMEM(shape, kind)
    n = scatter_wires(sizes)
    return [
        vmem(nx, nz, ny, block, width), vmem(nx, nz, ny, block, width),
        vmem(nx - 1, nz, ny, block, a), vmem(ny - 1, nx, nz, block, b),
        vmem(ny - 1, nz, block, a), vmem(nx - 1, nz, block, b),
        vmem(nz - 1, block, width),
        pltpu.SemaphoreType.DMA((n,)), pltpu.SemaphoreType.DMA((n,)), pltpu.SemaphoreType.DMA(()),
    ]


def scatter_stages(near, grad, out, held, got, x_first, y_first, y_then, x_then, z_last, send, recv, own, early=False):
    wires = Wires(near, send, recv)
    at, sizes = near.at, near.sizes
    nz, ny, nx = sizes["z"], sizes["y"], sizes["x"]
    x, y, z = at["x"], at["y"], at["z"]
    first, second = halves(held.shape[-1])
    loads = [] if own is None else [lambda: pltpu.make_async_copy(grad.at[:, at["c"]], held, own)]
    pair = [wires.wire(grad.at[:, 1 - at["c"]], got, "c", 1)]
    one = [wires.wire(held.at[near.along("x", k), :, :, :, first], x_first.at[k - 1], "x", k) for k in near.shifts("x")]
    one += [wires.wire(held.at[:, :, near.along("y", k), :, second], y_first.at[k - 1], "y", k) for k in near.shifts("y")]
    two = [wires.wire(held.at[x, :, near.along("y", k), :, first], y_then.at[k - 1], "y", k) for k in near.shifts("y")]
    two += [wires.wire(held.at[near.along("x", k), :, y, :, second], x_then.at[k - 1], "x", k) for k in near.shifts("x")]
    last = [wires.wire(held.at[x, near.along("z", k), y], z_last.at[k - 1], "z", k) for k in near.shifts("z")]

    def add(where, terms):
        held[where] = sum([t.astype(F32) for t in terms], held[where].astype(F32)).astype(held.dtype)

    def over_z(body):
        lax.fori_loop(0, nz, lambda i, carry: (body(i), carry)[1], 0)

    def stage0():
        start(pair, loads)

    def stage1():
        for load in loads:
            load().wait()
        landed(pair)

        @over_z
        def _(i):
            for a in range(nx):
                for b in range(ny):
                    if own is None:
                        held[a, i, b] = (grad[a, at["c"], i, b].astype(F32) + got[a, i, b].astype(F32)).astype(held.dtype)
                    else:
                        add((a, i, b), [got[a, i, b]])

        start(one)

    def stage2():
        landed(one)

        @over_z
        def _(i):
            for b in range(ny):
                add((x, i, b, ALL, first), [x_first[k - 1, i, b] for k in near.shifts("x")])
            for a in range(nx):
                add((a, i, y, ALL, second), [y_first[k - 1, a, i] for k in near.shifts("y")])

        start(two)

    def stage3():
        landed(two)

        @over_z
        def _(i):
            add((x, i, y, ALL, first), [y_then[k - 1, i] for k in near.shifts("y")])
            add((x, i, y, ALL, second), [x_then[k - 1, i] for k in near.shifts("x")])
            if early:
                out[i] = held[x, i, y]

        if early:
            left(pair, one, two)
        else:
            start(last)

    def stage4():
        landed(last)
        out[...] = sum([z_last[k - 1].astype(F32) for k in near.shifts("z")], held[x, z, y].astype(F32))
        left(pair, one, two, last)

    return [stage0, stage1, stage2, stage3] if early else [stage0, stage1, stage2, stage3, stage4]


def column_stages(near, column, out, z_last, send, recv):
    wires = Wires(near, send, recv)
    last = [wires.wire(column.at[near.along("z", k)], z_last.at[k - 1], "z", k) for k in near.shifts("z")]

    def finish():
        landed(last)
        out[...] = sum([z_last[k - 1].astype(F32) for k in near.shifts("z")], column[near.at["z"]].astype(F32))
        left(last)

    return [lambda: start(last), finish]


def total_scratch(sizes, shape):
    n = sum(sizes[a] - 1 for a in "cxyz")
    return [pltpu.VMEM((n,) + shape, F32), pltpu.VMEM((3,) + shape, F32), pltpu.SemaphoreType.DMA((n,)), pltpu.SemaphoreType.DMA((n,))]


def total_stages(near, mine, out, got, held, send, recv):
    wires = Wires(near, send, recv)
    groups, slots = [], []
    for step, axis in enumerate("cxyz"):
        src = mine if step == 0 else held.at[step - 1]
        slots.append([wires.used + k - 1 for k in near.shifts(axis)])
        groups.append([wires.wire(src, got.at[wires.used], axis, k) for k in near.shifts(axis)])

    def stage(step):
        def run():
            if step > 0:
                landed(groups[step - 1])
                total = mine[...] if step == 1 else held[step - 2]
                for slot in slots[step - 1]:
                    total = total + got[slot]
                if step < 4:
                    held[step - 1] = total
                else:
                    out[...] = total
                    left(*groups)
            if step < 4:
                start(groups[step])

        return run

    return [stage(step) for step in range(5)]


def blocks_of(sizes, grads):
    return [g.reshape(lead(sizes) + (-1, g.shape[1])) for g in grads]


def pump(schedule, plans, chunk):
    for step in sorted({at[0] for at in schedule if at[1] == chunk}):

        @pl.when(pl.program_id(0) == step)
        def _():
            for plan, stage in schedule[step, chunk]:
                plans[plan][stage]()


def mesh_sizes(mesh):
    fsdp = mesh.shape["fsdp"]
    ny = 1 << ((fsdp.bit_length() - 1) // 2)
    return {"x": mesh.shape["dp"] // 2, "c": 2, "z": fsdp // ny, "y": ny}


def project_kernel(x_ref, w_ref, gain_ref, shift_ref, offset_ref, a1_ref, qkv_ref):
    @pl.when(pl.program_id(0) == 0)
    def _():
        def body(rows):
            unit, _ = normalised(x_ref[rows, :].astype(F32))
            a1_ref[rows, :] = (unit * gain_ref[...] + shift_ref[...]).astype(BF)

        row_loop(x_ref.shape[0], 352, body)

    qkv_ref[...] = (dot(a1_ref[...], w_ref[...], 1, 0) + offset_ref[...]).astype(BF)


def project(x, w_in, gain, shift, offset):
    rows, d = x.shape
    return pl.pallas_call(
        project_kernel,
        grid=(3,),
        in_specs=[
            whole((rows, d)),
            pl.BlockSpec((d, d), lambda t: (0, t)),
            whole((1, d)),
            whole((1, d)),
            pl.BlockSpec((1, d), lambda t: (0, t)),
        ],
        out_specs=[whole((rows, d)), pl.BlockSpec((rows, d), lambda t: (0, t))],
        out_shape=[
            jax.ShapeDtypeStruct((rows, d), BF),
            jax.ShapeDtypeStruct((rows, 3 * d), BF),
        ],
        compiler_params=params(),
        cost_estimate=cost(6 * rows * d * d, 2 * (5 * rows * d + 3 * d * d)),
        name="project",
    )(x, w_in, gain, shift, offset)


VEC_ROWS = 16
UP_ROW = 10


def placed(value, width, device):
    size = value.shape[-1]
    row = lax.broadcasted_iota(jnp.int32, (size, width), 0)
    column = lax.broadcasted_iota(jnp.int32, (size, width), 1)
    return dot(value, (column == row + device * size).astype(BF), 1, 0)


def enter_kernel(sizes, tile, x_ref, w_ref, seg_ref, wo_ref, wu_ref, *refs):
    vec_refs, (a1_out, qkv_out, w_out, vecs_ref, mark_ref, far_ref, wo_full, wu_full) = refs[:10], refs[10:18]
    a1_ref, qkv_ref, w_full, unit_ref, mine_ref, third_ref = refs[18:24]
    small_refs, gather_refs, ahead_refs, out_sems = refs[24:28], refs[28:37], refs[37:43], refs[43]
    rows, d = x_ref.shape
    near = Near(sizes)
    near.greet()
    device = lax.axis_index(AXES)
    mine_ref[...] = jnp.zeros_like(mine_ref)
    in_bias, *plain = vec_refs
    up_bias = plain.pop(4)
    for i, ref in enumerate(plain):
        mine_ref[i : i + 1, :] = placed(ref[...], d, device)
    both = placed(in_bias[...], 2 * d, device)
    mine_ref[8:9, :] = both[:, :d]
    mine_ref[9:10, :] = both[:, d:]
    up = placed(up_bias[...], 4 * d, device)
    for i in range(4):
        mine_ref[UP_ROW + i : UP_ROW + i + 1, :] = up[:, d * i : d * (i + 1)]
    plans = [
        gather_stages(near, w_ref, w_full, *gather_refs[3 * t : 3 * t + 3], base=d * t, width=d) for t in range(3)
    ]
    ahead = [
        gather_stages(near, wo_ref, wo_full, *ahead_refs[:3], part="first"),
        gather_stages(near, wu_ref, wu_full, *ahead_refs[3:], part="first"),
    ]
    small = total_stages(near, mine_ref, vecs_ref, *small_refs)
    for plan in plans:
        plan[0]()

    def body(index, carry):
        span = pl.ds(pl.multiple_of(index * tile, tile), tile)
        unit_ref[span, :], _ = normalised(x_ref[span, :].astype(F32))
        for step in range(3):
            pl.when(index == step)(small[step])
        return carry

    lax.fori_loop(0, rows // tile, body, 0)
    plans[0][1]()
    small[3]()
    for plan in ahead:
        plan[0]()
    image = lax.broadcasted_iota(jnp.int32, (128, rows), 0) % HD
    same = seg_ref[...] == image
    mark_ref[...] = same.astype(F32).T.astype(BF)
    far_ref[...] = jnp.where(same | (image > PADDING), 0.0, FAR).T.astype(BF)
    plans[1][1]()
    plans[0][2]()
    plans[2][1]()
    plans[1][2]()
    small[4]()

    def shifted(span):
        a1_ref[span, :] = (unit_ref[span, :] * vecs_ref[1:2, :] + vecs_ref[2:3, :]).astype(BF)

    row_loop(rows, tile, shifted)
    sends = [pltpu.make_async_copy(a1_ref, a1_out, out_sems.at[0])]
    sends[0].start()

    def third(t):
        cols = slice(d * t, d * (t + 1))
        third_ref[...] = w_full[:, :, :, :, :, cols].astype(F32).reshape(d, d).astype(BF)

        def body(span):
            value = dot(a1_ref[span, :], third_ref[...], 1, 0)
            if t != 1:
                value = value + vecs_ref[8 + t // 2 : 9 + t // 2, :]
            qkv_ref[span, cols] = value.astype(BF)

        row_loop(rows, rows // 2, body)

    def store(t):
        cols = pl.ds(d * t, d)
        sends.append(pltpu.make_async_copy(qkv_ref.at[:, cols], qkv_out.at[:, cols], out_sems.at[1 + t]))
        sends[-1].start()

    plans[0][3]()
    plans[2][2]()
    plans[0][4]()
    third(0)
    plans[1][3]()
    store(0)
    plans[1][4]()
    plans[2][3]()
    third(1)
    store(1)
    plans[2][4]()
    sends.append(pltpu.make_async_copy(w_full, w_out, out_sems.at[4]))
    sends[-1].start()
    third(2)
    store(2)
    for plan in ahead:
        plan[1]()
    for copy in sends:
        copy.wait()


def enter(sizes, x, w_in, segment_ids, w_out, w_up, vectors, tile=352):
    rows, d = x.shape
    vmem, hbm = pl.BlockSpec(memory_space=pltpu.VMEM), pl.BlockSpec(memory_space=pltpu.HBM)
    full = lead(sizes) + w_in.shape
    return pl.pallas_call(
        functools.partial(enter_kernel, sizes, tile),
        in_specs=[vmem] * 15,
        out_specs=[hbm, hbm, hbm, vmem, vmem, vmem, hbm, hbm],
        out_shape=[
            jax.ShapeDtypeStruct((rows, d), BF),
            jax.ShapeDtypeStruct((rows, 3 * d), BF),
            jax.ShapeDtypeStruct(full, BF),
            jax.ShapeDtypeStruct((VEC_ROWS, d), F32),
            jax.ShapeDtypeStruct((rows, 128), BF),
            jax.ShapeDtypeStruct((rows, 128), BF),
            *gathered(sizes, [w_out, w_up]),
        ],
        scratch_shapes=[
            pltpu.VMEM((rows, d), BF),
            pltpu.VMEM((rows, 3 * d), BF),
            pltpu.VMEM(full, BF),
            pltpu.VMEM((rows, d), F32),
            pltpu.VMEM((VEC_ROWS, d), F32),
            pltpu.VMEM((d, d), BF),
            *total_scratch(sizes, (VEC_ROWS, d)),
            *gather_scratch(sizes) * 5,
            pltpu.SemaphoreType.DMA((5,)),
        ],
        compiler_params=params(collective_id=0, has_side_effects=True),
        name="enter",
    )(x, w_in, segment_ids[None], w_out, w_up, *[v[None] for v in vectors])


def chunks(rows, size):
    return [(start, min(size, rows - start)) for start in range(0, rows, size)]


GATHER_AT = {
    (0, 0): [(2, 0), (1, 1), (0, 1)],
    (1, 0): [(1, 2)],
    (2, 0): [(2, 1)],
    (3, 0): [(0, 2), (1, 3), (2, 2)],
    (4, 0): [(0, 3)],
    (5, 0): [(2, 3), (0, 4)],
    (5, -1): [(1, 4), (2, 4)],
}


def attend_kernel(chunk, sizes, count, q_ref, k_ref, v_ref, mark_ref, far_ref, *refs):
    shards, (o_ref, e_ref, inv_ref) = refs[:count][::-1], refs[count : count + 3]
    full, (vt_ref, k2_ref), sems = refs[count + 3 : 2 * count + 3], refs[2 * count + 3 : 2 * count + 5], refs[2 * count + 5 :]
    rows = q_ref.shape[0]
    plans, schedule = [], {}
    if count:
        near, schedule = Near(sizes), GATHER_AT
        pl.when(pl.program_id(0) == 0)(near.greet)
        plans = [
            gather_stages(near, shards[i], full[i], *sems[3 * i : 3 * i + 3], part="all" if i == 2 else "rest") for i in range(count)
        ]
    vt_ref[...] = v_ref[...].astype(F32).T.astype(BF)
    low = lax.broadcasted_iota(jnp.int32, (1, 128), 1) < HD
    for half in range(2):
        mine = low if half == 0 else jnp.logical_not(low)
        k2_ref[half] = jnp.where(mine, k_ref[...], far_ref[...])
    for turn, (start, size) in enumerate(chunks(rows, chunk)):
        pump(schedule, plans, turn)
        for half in range(2):
            mine = low if half == 0 else jnp.logical_not(low)
            span = pl.ds(start, size)
            query = jnp.where(mine, q_ref[span, :], mark_ref[span, :])
            scores = dot(k2_ref[half], query, 1, 1)
            top = jnp.max(scores, axis=0, keepdims=True)
            weights = jnp.exp2((scores - top) * (LOG2E * HD ** (-0.5)))
            total = jnp.sum(weights, axis=0, keepdims=True)
            weights_low = weights.astype(BF)
            e_ref[half, :, span] = weights_low
            inverse = 1.0 / total
            inv_ref[0, half : half + 1, span] = inverse
            head = pl.ds(half * HD, HD)
            o_ref[head, span] = (dot(vt_ref[head, :], weights_low, 1, 0) * inverse).astype(BF)
    pump(schedule, plans, -1)


def attend(qkv, mark, far, sizes, shards, chunk=704):
    count = len(shards)
    hbm = pl.BlockSpec(memory_space=pltpu.HBM)
    rows, width = qkv.shape
    pairs = width // 384
    return pl.pallas_call(
        functools.partial(attend_kernel, chunk, sizes, count),
        grid=(pairs,),
        in_specs=[
            pl.BlockSpec((rows, 128), lambda p: (0, p)),
            pl.BlockSpec((rows, 128), lambda p: (0, pairs + p)),
            pl.BlockSpec((rows, 128), lambda p: (0, 2 * pairs + p)),
            whole((rows, 128)),
            whole((rows, 128)),
            *([whole(shards[2].shape), hbm, hbm] if count else []),
        ],
        out_specs=[
            pl.BlockSpec((128, rows), lambda p: (p, 0)),
            pl.BlockSpec((2, rows, rows), lambda p: (p, 0, 0)),
            pl.BlockSpec((1, 2, rows), lambda p: (p, 0, 0)),
            *[hbm] * count,
        ],
        out_shape=[
            jax.ShapeDtypeStruct((pairs * 128, rows), BF),
            jax.ShapeDtypeStruct((2 * pairs, rows, rows), BF),
            jax.ShapeDtypeStruct((pairs, 2, rows), F32),
            *([*shards[:2], *gathered(sizes, shards[2:])] if count else []),
        ],
        scratch_shapes=[
            pltpu.VMEM((128, rows), BF),
            pltpu.VMEM((2, rows, 128), BF),
            *(gather_scratch(sizes) * count if count else []),
        ],
        compiler_params=params(collective_id=1, has_side_effects=True) if count else params(),
        cost_estimate=cost(2 * pairs * 4 * rows * rows * 256, 4 * pairs * rows * rows, 2 * pairs * rows * rows),
        input_output_aliases={7: 3, 6: 4} if count else {},
        name="attend",
    )(qkv, qkv, qkv, mark, far, *shards[::-1])


def masked(g_ref, mark_ref, rows):
    padding = mark_ref[rows, PADDING : PADDING + 1].astype(F32)
    return jnp.where(padding > 0, 0.0, g_ref[rows, :].astype(F32))


def middle_kernel(o_ref, x_ref, g_ref, mark_ref, w_ref, vec_ref, m1_ref, a2_ref, gm_ref, gmsum_ref):
    bias, scale1, gain2, shift2, scale2 = (vec_ref[i : i + 1, :] for i in (0, 3, 5, 6, 7))
    m1_ref[...] = dot(o_ref[...], w_ref[...], 0, 0)
    gmsum_ref[...] = jnp.zeros_like(gmsum_ref)

    def body(rows):
        m1 = x_ref[rows, :].astype(F32) + scale1 * (m1_ref[rows, :] + bias)
        m1_ref[rows, :] = m1
        unit, _ = normalised(m1)
        a2_ref[rows, :] = (unit * gain2 + shift2).astype(BF)
        gm = (scale2 * masked(g_ref, mark_ref, rows)).astype(BF)
        gm_ref[rows, :] = gm
        gmsum_ref[...] += jnp.sum(gm.astype(F32).reshape(-1, 8, gm.shape[-1]), axis=0)

    row_loop(x_ref.shape[0], 352, body)


def middle(o, x, g, mark, w_out, vec):
    rows, d = x.shape
    return pl.pallas_call(
        middle_kernel,
        out_shape=[
            jax.ShapeDtypeStruct((rows, d), F32),
            jax.ShapeDtypeStruct((rows, d), BF),
            jax.ShapeDtypeStruct((rows, d), BF),
            jax.ShapeDtypeStruct((8, d), F32),
        ],
        compiler_params=params(),
        cost_estimate=cost(2 * rows * d * d, 14 * rows * d),
        name="middle",
    )(o, x, g, mark, w_out, vec)


def gelu_parts(u):
    near = jnp.abs(u)
    t = 1.0 / (1.0 + (0.3275911 * 0.7071067811865476) * near)
    bell = jnp.exp2((-0.5 * LOG2E) * (u * u))
    poly = t * (
        0.5 * 0.254829592
        + t * (0.5 * -0.284496736 + t * (0.5 * 1.421413741 + t * (0.5 * -1.453152027 + t * (0.5 * 1.061405429))))
    )
    tail = poly * bell
    phi = jnp.where(u < 0, tail, 1.0 - tail)
    return u * phi, phi + u * bell * 0.3989422804014327


def feed_kernel(chunk, a2_ref, gm_ref, up_ref, vec_ref, down_ref, bm_ref, ga_ref, dup_ref, ddown_ref, dub_ref, gl_ref, gu_ref):
    first = pl.program_id(0) == 0

    @pl.when(first)
    def _():
        bm_ref[...] = jnp.zeros_like(bm_ref)
        ga_ref[...] = jnp.zeros_like(ga_ref)

    d = vec_ref.shape[-1]
    spread = up_ref.shape[-1] // d
    bias = jnp.concatenate([vec_ref[pl.ds(UP_ROW + pl.program_id(0) * spread + i, 1), :] for i in range(spread)], axis=1)
    dub_ref[...] = jnp.zeros_like(dub_ref)

    def body(rows):
        u = dot(a2_ref[rows, :], up_ref[...], 1, 0) + bias
        back = dot(gm_ref[rows, :], down_ref[...], 1, 1)
        active, slope = gelu_parts(u)
        low = active.astype(BF)
        gl_ref[rows, :] = low
        gu = (slope * back).astype(BF)
        gu_ref[rows, :] = gu
        dub_ref[...] += jnp.sum(gu.astype(F32).reshape(-1, 8, gu.shape[-1]), axis=0)
        bm_ref[rows, :] += dot(low, down_ref[...], 1, 0)
        ga_ref[rows, :] += dot(gu, up_ref[...], 1, 1)

    row_loop(a2_ref.shape[0], chunk, body)

    def weights(span):
        ddown_ref[span, :] = dot(gl_ref[:, span], gm_ref[...], 0, 0).astype(ddown_ref.dtype)
        dup_ref[span, :] = dot(a2_ref[:, span], gu_ref[...], 0, 0).astype(dup_ref.dtype)

    row_loop(dup_ref.shape[0], 256, weights)


def feed(a2, gm, w_up, vecs, w_down, block=768, chunk=704, kind=BF):
    rows, d = a2.shape
    ff = w_up.shape[1]
    return pl.pallas_call(
        functools.partial(feed_kernel, chunk),
        grid=(ff // block,),
        in_specs=[
            whole((rows, d)),
            whole((rows, d)),
            pl.BlockSpec((d, block), lambda f: (0, f)),
            whole((VEC_ROWS, d)),
            pl.BlockSpec((block, d), lambda f: (f, 0)),
        ],
        out_specs=[
            whole((rows, d)),
            whole((rows, d)),
            pl.BlockSpec((d, block), lambda f: (0, f)),
            pl.BlockSpec((block, d), lambda f: (f, 0)),
            pl.BlockSpec((8, block), lambda f: (0, f)),
        ],
        out_shape=[
            jax.ShapeDtypeStruct((rows, d), F32),
            jax.ShapeDtypeStruct((rows, d), F32),
            jax.ShapeDtypeStruct((d, ff), kind),
            jax.ShapeDtypeStruct((ff, d), kind),
            jax.ShapeDtypeStruct((8, ff), F32),
        ],
        scratch_shapes=[pltpu.VMEM((rows, block), BF), pltpu.VMEM((rows, block), BF)],
        compiler_params=params(),
        cost_estimate=cost(12 * rows * d * ff, 4 * 4 * d * ff),
        name="feed",
    )(a2, gm, w_up, vecs, w_down)


def join_kernel(size, m1_ref, bm_ref, ga_ref, x_ref, g_ref, mark_ref, o_ref, w_ref, vec_ref, out_ref, gm1_ref, go_ref, dout_ref, sums_ref, gb_ref):
    bias2, scale1, gain2, scale2 = (vec_ref[i : i + 1, :] for i in (4, 3, 5, 7))
    step = pl.program_id(0)

    @pl.when(step == 0)
    def _():
        sums_ref[...] = jnp.zeros_like(sums_ref)

    base = step * m1_ref.shape[0]

    def body(rows):
        m1 = m1_ref[rows, :]
        bm = bm_ref[rows, :] + bias2
        g = masked(g_ref, mark_ref, rows)
        out_ref[rows, :] = (m1 + scale2 * bm).astype(BF)
        unit, inverse = normalised(m1)
        ga = ga_ref[rows, :]
        gm1 = g + norm_back(unit, inverse, ga * gain2)
        gm1_ref[rows, :] = gm1
        gb = (scale1 * gm1).astype(BF)
        gb_ref[pl.ds(pl.multiple_of(base + rows.start, size), size), :] = gb
        for index, value in enumerate(
            (g * bm, ga * unit, ga, gm1 * (m1 - x_ref[rows, :].astype(F32)), gb.astype(F32))
        ):
            sums_ref[index] += jnp.sum(value.reshape(-1, 8, value.shape[-1]), axis=0)

    row_loop(m1_ref.shape[0], size, body)

    @pl.when(step == pl.num_programs(0) - 1)
    def _():
        go_ref[...] = dot(w_ref[...], gb_ref[...], 1, 1).astype(BF)
        dout_ref[...] = dot(o_ref[...], gb_ref[...], 1, 0).astype(dout_ref.dtype)


def join(m1, bm, ga, x, g, mark, o, w_out, vec, tile=352, kind=BF):
    rows, d = x.shape
    by_rows = pl.BlockSpec((tile, d), lambda i: (i, 0))
    return pl.pallas_call(
        functools.partial(join_kernel, 352),
        grid=(rows // tile,),
        in_specs=[by_rows] * 5 + [pl.BlockSpec((tile, 128), lambda i: (i, 0)), whole((d, rows)), whole((d, d)), whole((VEC_ROWS, d))],
        out_specs=[by_rows, by_rows, whole((d, rows)), whole((d, d)), whole((5, 8, d))],
        out_shape=[
            jax.ShapeDtypeStruct((rows, d), BF),
            jax.ShapeDtypeStruct((rows, d), F32),
            jax.ShapeDtypeStruct((d, rows), BF),
            jax.ShapeDtypeStruct((d, d), kind),
            jax.ShapeDtypeStruct((5, 8, d), F32),
        ],
        scratch_shapes=[pltpu.VMEM((rows, d), BF)],
        compiler_params=params(),
        cost_estimate=cost(4 * rows * d * d, 26 * rows * d),
        name="join",
    )(m1, bm, ga, x, g, mark, o, w_out, vec)


SCATTER_AT = {
    (0, 0): [(0, 0), (2, 0)],
    (1, 0): [(0, 1)],
    (2, 0): [(1, 0), (2, 1)],
    (3, 0): [(0, 2), (1, 1)],
    (4, 0): [(2, 2), (0, 3)],
    (5, 0): [(1, 2), (2, 3)],
    (5, -1): [(1, 3), (2, 4), (0, 4)],
}


def attend_back_kernel(chunk, sizes, count, q_ref, k_ref, v_ref, go_ref, o_ref, e_ref, inv_ref, *refs):
    grads, out_ref, sums = refs[:count], refs[count], refs[count + 1 : 2 * count + 1]
    (kt_ref, gq_ref, gs_ref, gp_ref), rest = refs[2 * count + 1 : 2 * count + 5], refs[2 * count + 5 :]
    rows = q_ref.shape[0]
    plans, schedule = [], {}
    if count:
        near, schedule = Near(sizes), SCATTER_AT
        pl.when(pl.program_id(0) == 0)(near.greet)
        plans = [
            scatter_stages(near, grads[i], sums[i], *rest[SCATTER_REFS * i : SCATTER_REFS * (i + 1)], early=i == 1)
            for i in range(count)
        ]
    factor = HD ** (-0.5)
    kt_ref[...] = k_ref[...].astype(F32).T.astype(BF)
    low = lax.broadcasted_iota(jnp.int32, (1, 128), 1) < HD
    below = lax.broadcasted_iota(jnp.int32, (128, 1), 0) < HD
    gp_ref[...] = jnp.zeros_like(gp_ref)
    for turn, (start, size) in enumerate(chunks(rows, chunk)):
        pump(schedule, plans, turn)
        span = pl.ds(start, size)
        for half in range(2):
            head = pl.ds(half * HD, HD)
            incoming = go_ref[head, span].astype(F32) * inv_ref[0, half : half + 1, span]
            centre = jnp.sum(incoming * o_ref[head, span].astype(F32), axis=0, keepdims=True)
            gp_ref[half, head, span] = incoming.astype(BF)
            gp = dot(v_ref[...], gp_ref[half, :, span], 1, 0)
            gs = (e_ref[half, :, span].astype(F32) * (gp - centre)).astype(BF)
            gs_ref[half, :, span] = gs
            gq_ref[head, span] = dot(kt_ref[head, :], gs, 1, 0) * factor
    out_ref[0] = gq_ref[...].T.astype(BF)
    gk = [dot(gs_ref[half], q_ref[...], 1, 0) for half in range(2)]
    out_ref[1] = (jnp.where(low, gk[0], gk[1]) * factor).astype(BF)
    out_ref[2] = (dot(e_ref[0], gp_ref[0], 1, 1) + dot(e_ref[1], gp_ref[1], 1, 1)).astype(BF)
    pump(schedule, plans, -1)


def attend_back(qkv, go, o, e, inv, sizes, grads, chunk=512):
    blocks = blocks_of(sizes, grads) if grads else []
    count = len(blocks)
    sums = [jax.ShapeDtypeStruct(b.shape[-2:], F32) for b in blocks]
    if count:
        sums[1] = jax.ShapeDtypeStruct((sizes["z"],) + sums[1].shape, BF)
    rows, width = qkv.shape
    pairs = width // 384
    return pl.pallas_call(
        functools.partial(attend_back_kernel, chunk, sizes, count),
        grid=(pairs,),
        in_specs=[
            pl.BlockSpec((rows, 128), lambda p: (0, p)),
            pl.BlockSpec((rows, 128), lambda p: (0, pairs + p)),
            pl.BlockSpec((rows, 128), lambda p: (0, 2 * pairs + p)),
            pl.BlockSpec((128, rows), lambda p: (p, 0)),
            pl.BlockSpec((128, rows), lambda p: (p, 0)),
            pl.BlockSpec((2, rows, rows), lambda p: (p, 0, 0)),
            pl.BlockSpec((1, 2, rows), lambda p: (p, 0, 0)),
            *[pl.BlockSpec(memory_space=pltpu.HBM)] * count,
        ],
        out_specs=[pl.BlockSpec((3, rows, 128), lambda p: (0, 0, p)), *[whole(v.shape) for v in sums]],
        out_shape=[
            jax.ShapeDtypeStruct((3, rows, pairs * 128), BF),
            *sums,
        ],
        scratch_shapes=[
            pltpu.VMEM((128, rows), BF),
            pltpu.VMEM((128, rows), F32),
            pltpu.VMEM((2, rows, rows), BF),
            pltpu.VMEM((2, 128, rows), BF),
            *[s for b in blocks for s in scatter_scratch(sizes, *b.shape[-2:], b.dtype)],
        ],
        compiler_params=params(collective_id=2, has_side_effects=True) if count else params(),
        cost_estimate=cost(2 * pairs * 8 * rows * rows * 256, 4 * pairs * rows * rows),
        name="attend_back",
    )(qkv, qkv, qkv, go, o, e, inv, *blocks)


def finish_kernel(a1_ref, gqkv_ref, w_ref, x_ref, gm1_ref, gain_ref, dw_ref, cols_ref, gx_ref, sums_ref, ga_ref):
    step = pl.program_id(0)
    grads = gqkv_ref[0]
    dw_ref[...] = dot(a1_ref[...], grads, 0, 0).astype(dw_ref.dtype)
    cols_ref[0] = jnp.sum(grads.astype(F32).reshape(-1, 8, grads.shape[-1]), axis=0)
    part = dot(grads, w_ref[...], 1, 1)

    @pl.when(step == 0)
    def _():
        ga_ref[...] = part

    @pl.when(step > 0)
    def _():
        ga_ref[...] += part

    @pl.when(step == pl.num_programs(0) - 1)
    def _():
        sums_ref[...] = jnp.zeros_like(sums_ref)

        def body(rows):
            unit, inverse = normalised(x_ref[rows, :].astype(F32))
            ga = ga_ref[rows, :]
            gx_ref[rows, :] = gm1_ref[rows, :] + norm_back(unit, inverse, ga * gain_ref[...])
            for index, value in enumerate((ga * unit, ga)):
                sums_ref[index] += jnp.sum(value.reshape(-1, 8, value.shape[-1]), axis=0)

        row_loop(x_ref.shape[0], 352, body)


def finish(a1, gqkv, w_in, x, gm1, gain, kind=BF):
    rows, d = x.shape
    return pl.pallas_call(
        finish_kernel,
        grid=(3,),
        in_specs=[
            whole((rows, d)),
            pl.BlockSpec((1, rows, d), lambda t: (t, 0, 0)),
            pl.BlockSpec((d, d), lambda t: (0, t)),
            whole((rows, d)),
            whole((rows, d)),
            whole((1, d)),
        ],
        out_specs=[
            pl.BlockSpec((d, d), lambda t: (0, t)),
            pl.BlockSpec((1, 8, d), lambda t: (t, 0, 0)),
            whole((rows, d)),
            whole((2, 8, d)),
        ],
        out_shape=[
            jax.ShapeDtypeStruct((d, 3 * d), kind),
            jax.ShapeDtypeStruct((3, 8, d), F32),
            jax.ShapeDtypeStruct((rows, d), F32),
            jax.ShapeDtypeStruct((2, 8, d), F32),
        ],
        scratch_shapes=[pltpu.VMEM((rows, d), F32)],
        compiler_params=params(),
        cost_estimate=cost(12 * rows * d * d, 20 * rows * d),
        name="finish",
    )(a1, gqkv, w_in, x, gm1, gain)


def leave_kernel(sizes, tile, a1_in, gqkv_in, w_in, x_in, gm1_in, vec_ref, join_ref, ub_ref, gmsum_ref, column_ref, gx_out, dw_ref, early_ref, late_ref, ddown_ref, *refs):
    a1_ref, gqkv_ref, w_ref, x_ref, gm1_ref, gx_ref, ga_ref, sums_ref, mine_ref, last_ref = refs[:10]
    grad_refs, refs = refs[10:13], refs[13:]
    scatter_refs, refs = [refs[9 * t : 9 * t + 9] for t in range(3)], refs[27:]
    early_refs, late_refs, column_refs, in_sems, out_sems = refs[:4], refs[4:8], refs[8:11], refs[11], refs[12]
    rows, d = x_in.shape
    count = rows // tile
    moves = [(a1_in, a1_ref), *[(gqkv_in.at[t], gqkv_ref.at[t]) for t in range(3)], (w_in, w_ref), (x_in, x_ref), (gm1_in, gm1_ref)]
    fetch = [pltpu.make_async_copy(src, dst, in_sems.at[n]) for n, (src, dst) in enumerate(moves)]
    for copy in fetch:
        copy.start()
    near = Near(sizes)
    near.greet()
    row = lambda value: jnp.sum(value, axis=0, keepdims=True)
    mine_ref[...] = jnp.zeros_like(mine_ref)
    for i, value in enumerate(
        (row(join_ref[4]), row(join_ref[3]) / vec_ref[3:4, :], row(gmsum_ref[...]), row(join_ref[1]), row(join_ref[2]), row(join_ref[0]))
    ):
        mine_ref[i : i + 1, :] = value
    for i in range(4):
        mine_ref[8 + i : 9 + i, :] = row(ub_ref[:, d * i : d * (i + 1)])
    plans = [
        scatter_stages(near, grad_refs[t], dw_ref.at[:, pl.ds(d * t, d)], *scatter_refs[t], None) for t in range(3)
    ]
    early = total_stages(near, mine_ref, early_ref, *early_refs)
    late = total_stages(near, last_ref, late_ref, *late_refs)
    column = column_stages(near, column_ref, ddown_ref, *column_refs)
    column[0]()
    last_ref[...] = jnp.zeros_like(last_ref)

    def weight(t):
        fetch[1 + t].wait()
        part = d // sizes["x"]

        def body(x, carry):
            value = dot(a1_ref[:, pl.ds(pl.multiple_of(x * part, part), part)], gqkv_ref[t], 0, 0)
            grad_refs[t][x] = value.reshape(grad_refs[t].shape[1:]).astype(BF)
            return carry

        lax.fori_loop(0, sizes["x"], body, 0)

    def back(t):
        def body(span):
            part = dot(gqkv_ref[t, span, :], w_ref[:, d * t : d * (t + 1)], 1, 1)
            ga_ref[span, :] = part if t == 0 else ga_ref[span, :] + part

        row_loop(rows, rows // 2, body)
        if t != 1:
            total = jnp.zeros((1, d), F32)
            for start_row, size in chunks(rows, tile):
                total += row(gqkv_ref[t, pl.ds(start_row, size), :].astype(F32))
            last_ref[2 + t // 2 : 3 + t // 2, :] = total

    fetch[0].wait()
    weight(0)
    early[0]()
    plans[0][0]()
    weight(1)
    plans[0][1]()
    plans[1][0]()
    early[1]()
    weight(2)
    plans[1][1]()
    plans[2][0]()
    fetch[4].wait()
    back(0)
    plans[0][2]()
    plans[2][1]()
    early[2]()
    back(1)
    plans[1][2]()
    back(2)
    plans[0][3]()
    column[1]()
    early[3]()
    fetch[5].wait()
    fetch[6].wait()
    sums_ref[...] = jnp.zeros_like(sums_ref)

    def send(index):
        span = pl.ds(pl.multiple_of(index * tile, tile), tile)
        return pltpu.make_async_copy(gx_ref.at[span], gx_out.at[span], out_sems.at[index])

    between = [[], [plans[2][2], plans[1][3]], []]

    def body(index, carry):
        span = pl.ds(pl.multiple_of(index * tile, tile), tile)
        unit, inverse = normalised(x_ref[span, :].astype(F32))
        ga = ga_ref[span, :]
        gx_ref[span, :] = gm1_ref[span, :] + norm_back(unit, inverse, ga * vec_ref[1:2, :])
        for n, value in enumerate((ga * unit, ga)):
            sums_ref[n] += jnp.sum(value.reshape(-1, 8, d), axis=0)
        for n, stages in enumerate(between):

            @pl.when(index == n)
            def _():
                for stage in stages:
                    stage()

        pl.when(index > 0)(lambda: send(index - 1).start())
        return carry

    lax.fori_loop(0, count, body, 0)
    for n in range(2):
        last_ref[n : n + 1, :] = row(sums_ref[n])
    late[0]()
    send(count - 1).start()
    early[4]()
    plans[2][3]()
    late[1]()
    plans[0][4]()
    late[2]()
    plans[1][4]()
    late[3]()
    plans[2][4]()
    late[4]()
    for index in range(count):
        send(index).wait()


def leave(sizes, a1, gqkv, w_in, x, gm1, vecs, join_sums, ub_sum, gm_sum, column, tile=352):
    rows, d = x.shape
    vmem, hbm = pl.BlockSpec(memory_space=pltpu.VMEM), pl.BlockSpec(memory_space=pltpu.HBM)
    block = d // (sizes["x"] * 2 * sizes["z"] * sizes["y"])
    return pl.pallas_call(
        functools.partial(leave_kernel, sizes, tile),
        in_specs=[hbm] * 5 + [vmem] * 5,
        out_specs=[hbm, vmem, vmem, vmem, vmem],
        out_shape=[
            jax.ShapeDtypeStruct((rows, d), F32),
            jax.ShapeDtypeStruct((block, 3 * d), F32),
            jax.ShapeDtypeStruct((16, d), F32),
            jax.ShapeDtypeStruct((8, d), F32),
            jax.ShapeDtypeStruct(column.shape[1:], F32),
        ],
        scratch_shapes=[
            pltpu.VMEM((rows, d), BF),
            pltpu.VMEM((3, rows, d), BF),
            pltpu.VMEM((d, 3 * d), BF),
            pltpu.VMEM((rows, d), BF),
            pltpu.VMEM((rows, d), F32),
            pltpu.VMEM((rows, d), F32),
            pltpu.VMEM((rows, d), F32),
            pltpu.VMEM((2, 8, d), F32),
            pltpu.VMEM((16, d), F32),
            pltpu.VMEM((8, d), F32),
            *[pltpu.VMEM(lead(sizes) + (block, d), BF)] * 3,
            *scatter_scratch(sizes, block, d, BF)[:-1] * 3,
            *total_scratch(sizes, (16, d)),
            *total_scratch(sizes, (8, d)),
            pltpu.VMEM((sizes["z"] - 1,) + column.shape[1:], BF),
            pltpu.SemaphoreType.DMA((sizes["z"] - 1,)),
            pltpu.SemaphoreType.DMA((sizes["z"] - 1,)),
            pltpu.SemaphoreType.DMA((7,)),
            pltpu.SemaphoreType.DMA((rows // tile,)),
        ],
        compiler_params=params(collective_id=3, has_side_effects=True),
        name="leave",
    )(a1, gqkv, w_in, x, gm1, vecs, join_sums, ub_sum, gm_sum, column)


def share_kernel(early_ref, late_ref, *refs):
    grads, outs, vec_outs = refs[:4], refs[4:8], refs[8:]
    for src, dst in zip(grads, outs):
        dst[...] = src[...]
    device = lax.axis_index(AXES)
    d = early_ref.shape[-1]

    def entries(ref, first_row, size):
        at = device * size
        line = ref[pl.ds(first_row + lax.div(at, d), 1), :]
        return pltpu.roll(jnp.broadcast_to(line, (8, d)), lax.rem(d - lax.rem(at, d), d), 1)[:1, :size]

    spots = [
        (late_ref, 2), (early_ref, 0), (late_ref, 0), (late_ref, 1), (early_ref, 1),
        (early_ref, 8), (early_ref, 2), (early_ref, 3), (early_ref, 4), (early_ref, 5),
    ]
    for (ref, first_row), out in zip(spots, vec_outs):
        out[...] = entries(ref, first_row, out.shape[-1])


def share(early, late, grads, sizes):
    vmem = pl.BlockSpec(memory_space=pltpu.VMEM)
    return pl.pallas_call(
        share_kernel,
        in_specs=[vmem] * 6,
        out_specs=[vmem] * 14,
        out_shape=[jax.ShapeDtypeStruct(g.shape, F32) for g in grads] + [jax.ShapeDtypeStruct((1, n), F32) for n in sizes],
        compiler_params=params(),
        name="share",
    )(early, late, *grads)


def take(a):
    return lax.all_gather(a, AXES, axis=0, tiled=True)


def give(g):
    return lax.psum_scatter(g, AXES, scatter_dimension=0, tiled=True).astype(F32)


def layer(
    sizes, inputs, segment_ids, cotangent, in_weight, in_bias, out_weight, out_bias, first_gain, first_shift, first_scale,
    up_weight, up_bias, down_weight, down_bias, second_gain, second_shift, second_scale,
):
    rows, d = inputs.shape
    vectors = (
        in_bias, out_bias, first_gain, first_shift, first_scale,
        up_bias, down_bias, second_gain, second_shift, second_scale,
    )
    own = all(w.shape[0] % 8 == 0 for w in (in_weight, out_weight, up_weight, down_weight))
    if own:
        a1, qkv, w_in, vecs, mark, far, *begun = enter(
            sizes, inputs, in_weight, segment_ids, out_weight, up_weight, vectors
        )
        w_in = w_in.reshape(d, 3 * d)
    else:
        w_in = take(in_weight)
        row = lambda v: take(v).astype(F32).reshape(-1, d)
        vecs = jnp.concatenate(
            [row(v) for v in (out_bias, first_gain, first_shift, first_scale, down_bias, second_gain, second_shift, second_scale, in_bias)]
            + [row(up_bias), jnp.zeros((VEC_ROWS - 14, d), F32)]
        )
        offset = jnp.concatenate([vecs[8:9], jnp.zeros((1, d), F32), vecs[9:10]], axis=1)
        a1, qkv = project(inputs, w_in, vecs[1:2], vecs[2:3], offset)
        lane = lax.broadcasted_iota(jnp.int32, (1, 128), 1) % HD
        same = segment_ids[:, None] == lane
        mark = same.astype(BF)
        far = jnp.where(same | (lane > PADDING), 0.0, FAR).astype(BF)
    o, e, inv, *full = attend(qkv, mark, far, sizes, [*begun, down_weight] if own else [])
    w_out, w_up, w_down = (
        (f.reshape(-1, f.shape[-1]) for f in full) if own else (take(w) for w in (out_weight, up_weight, down_weight))
    )
    m1, a2, gm, gm_sum = middle(o, inputs, cotangent, mark, w_out, vecs)
    bm, ga2, d_up, d_down, ub_sum = feed(a2, gm, w_up, vecs, w_down)
    outputs, gm1, go, d_out, join_sums = join(m1, bm, ga2, inputs, cotangent, mark, o, w_out, vecs)
    gqkv, *done = attend_back(qkv, go, o, e, inv, sizes, [d_up, d_down, d_out] if own else [])
    if own:
        d_up, column, d_out = done
        gx, d_in, early, late, d_down = leave(sizes, a1, gqkv, w_in, inputs, gm1, vecs, join_sums, ub_sum, gm_sum, column)
        d_up, d_down, d_out, d_in, *out = share(early, late, [d_up, d_down, d_out, d_in], [v.shape[0] for v in vectors])
        out = [v.reshape(-1) for v in out]
    else:
        d_in, col_sums, gx, last_sums = finish(a1, gqkv, w_in, inputs, gm1, vecs[1:2])
        d_in, d_up, d_down, d_out = (give(v) for v in (d_in, d_up, d_down, d_out))
        s = jnp.sum
        j, c, t = (s(v, axis=1) for v in (join_sums, col_sums, last_sums))
        sums = (
            jnp.concatenate([c[0], c[2]]), j[4], t[0], t[1], j[3] / vecs[3], s(ub_sum, axis=0), s(gm_sum, axis=0), j[1], j[2], j[0],
        )
        out = [give(v) for v in sums]
    return (
        outputs, gx, d_in, out[0], d_out, out[1], out[2], out[3], out[4],
        d_up, out[5], d_down, out[6], out[7], out[8], out[9],
    )


def solution(mesh):
    wide, flat = P(AXES, None), P(AXES)
    return jax.shard_map(
        functools.partial(layer, mesh_sizes(mesh)),
        mesh=mesh,
        in_specs=(wide, flat, wide, wide, flat, wide, flat, flat, flat, flat, wide, flat, wide, flat, flat, flat, flat),
        out_specs=(wide, wide, wide, flat, wide, flat, flat, flat, flat, wide, flat, wide, flat, flat, flat, flat),
        check_vma=False,
    )
```

```python
import functools

import jax
import jax.numpy as jnp
from jax import lax
from jax.experimental import pallas as pl
from jax.experimental.pallas import tpu as pltpu
from jax.sharding import PartitionSpec as P

HD = 64
PADDING = 5
EPSILON = 1e-06
LOG2E = 1.4426950408889634
FAR = -1e30
BF = jnp.bfloat16
F32 = jnp.float32
AXES = ("dp", "fsdp")
VMEM_LIMIT = 62 * 1024 * 1024


def dot(a, b, da, db):
    return lax.dot_general(a, b, (((da,), (db,)), ((), ())), preferred_element_type=F32)


def params(**more):
    return pltpu.CompilerParams(vmem_limit_bytes=VMEM_LIMIT, **more)


def cost(flops, moved, special=0):
    return pl.CostEstimate(flops=int(flops), bytes_accessed=int(moved), transcendentals=int(special))


def whole(shape):
    return pl.BlockSpec(shape, lambda *_: (0,) * len(shape), pipeline_mode=pl.Buffered(1))


def row_loop(rows, size, body):
    def step(index, carry):
        body(pl.ds(pl.multiple_of(index * size, size), size))
        return carry

    lax.fori_loop(0, rows // size, step, 0)


def normalised(values):
    centred = values - jnp.mean(values, axis=-1, keepdims=True)
    spread = jnp.mean(centred * centred, axis=-1, keepdims=True)
    inverse = lax.rsqrt(spread + EPSILON)
    return centred * inverse, inverse


def norm_back(unit, inverse, scaled):
    return inverse * (
        scaled
        - jnp.mean(scaled, axis=-1, keepdims=True)
        - unit * jnp.mean(scaled * unit, axis=-1, keepdims=True)
    )


MESH = pl.DeviceIdType.MESH
ALL = slice(None)


class Near:
    def __init__(self, sizes):
        self.sizes = sizes
        dp, fsdp = lax.axis_index("dp"), lax.axis_index("fsdp")
        ny = sizes["y"]
        self.at = {"x": lax.div(dp, 2), "c": lax.rem(dp, 2), "z": lax.div(fsdp, ny), "y": lax.rem(fsdp, ny)}

    def along(self, axis, shift):
        return lax.rem(self.at[axis] + shift, self.sizes[axis])

    def device(self, axis, shift):
        at = {**self.at, axis: self.along(axis, shift)}
        return (at["x"] * 2 + at["c"], at["z"] * self.sizes["y"] + at["y"])

    def shifts(self, axis):
        return range(1, self.sizes[axis])

    def greet(self):
        barrier = pltpu.get_barrier_semaphore()
        count = 0
        for axis in "cxyz":
            for shift in self.shifts(axis):
                pl.semaphore_signal(barrier, inc=1, device_id=self.device(axis, shift), device_id_type=MESH)
                count += 1
        pl.semaphore_wait(barrier, count)


class Wires:
    def __init__(self, near, send, recv):
        self.near, self.send, self.recv, self.used = near, send, recv, 0

    def wire(self, src, dst, axis, shift):
        n = self.used
        self.used += 1
        return lambda: pltpu.make_async_remote_copy(
            src_ref=src, dst_ref=dst, send_sem=self.send.at[n], recv_sem=self.recv.at[n],
            device_id=self.near.device(axis, shift), device_id_type=MESH,
        )


def start(*groups):
    for group in groups:
        for wire in group:
            wire().start()


def landed(*groups):
    for group in groups:
        for wire in group:
            wire().wait_recv()


def left(*groups):
    for group in groups:
        for wire in group:
            wire().wait_send()


def halves(width, base=0):
    cut = (width // 256) * 128
    return pl.ds(base, cut), pl.ds(base + cut, width - cut)


def gather_wires(sizes):
    return sizes["z"] + 4 * (sizes["x"] + sizes["y"] - 2)


def gather_stages(near, mine, full, send, recv, own, base=0, width=None, part="all"):
    wires = Wires(near, send, recv)
    at = near.at
    width = full.shape[-1] if width is None else width
    every = pl.ds(base, width)
    if part != "rest":
        mine = mine.at[:, every]

    def piece(cols, **fixed):
        return full.at[tuple(fixed.get(a, at[a]) for a in "xczy") + (ALL, cols)]

    def spread(axis, done, cols, src=None):
        here = piece(cols, **{a: ALL for a in done})
        return [wires.wire(here if src is None else src, here, axis, k) for k in near.shifts(axis)]

    def forward(axis, done, cols):
        size = near.sizes[axis]
        parts = [piece(cols, **{a: ALL for a in done}, **{axis: near.along(axis, size - k)}) for k in near.shifts(axis)]
        return [wires.wire(p, p, "c", 1) for p in parts]

    first, second = halves(width, base)
    whole_z = [] if part == "rest" else spread("z", "", every, mine)
    column = piece(every, z=ALL)
    pair = [wires.wire(column, column, "c", 1)]
    one, two, one_on, two_on = [], [], [], []
    for cols, (a, b) in ((first, "yx"), (second, "xy")):
        one += spread(a, "z", cols)
        one_on += forward(a, "z", cols)
        two += spread(b, "z" + a, cols)
        two_on += forward(b, "z" + a, cols)
    keep = lambda: pltpu.make_async_copy(mine, piece(every), own)

    def stage0():
        keep().start()
        start(whole_z)

    def arrive():
        keep().wait()
        landed(whole_z)
        left(whole_z)

    def stage1():
        if part != "rest":
            arrive()
        start(one, pair)

    def stage2():
        landed(one)
        start(two, one_on)

    def stage3():
        landed(two)
        start(two_on)

    def stage4():
        left(pair, one, two, one_on, two_on)
        landed(pair, one_on, two_on)

    return [stage0, arrive] if part == "first" else [stage0, stage1, stage2, stage3, stage4]


def gather_scratch(sizes):
    n = gather_wires(sizes)
    return [pltpu.SemaphoreType.DMA((n,)), pltpu.SemaphoreType.DMA((n,)), pltpu.SemaphoreType.DMA(())]


def lead(sizes):
    return (sizes["x"], 2, sizes["z"], sizes["y"])


def gathered(sizes, arrays):
    return [jax.ShapeDtypeStruct(lead(sizes) + a.shape, a.dtype) for a in arrays]


def scatter_wires(sizes):
    return 1 + 2 * (sizes["x"] + sizes["y"] - 2) + sizes["z"] - 1


SCATTER_REFS = 10


def scatter_scratch(sizes, block, width, kind):
    nx, ny, nz = sizes["x"], sizes["y"], sizes["z"]
    first, second = halves(width)
    a, b = first.size, second.size
    vmem = lambda *shape: pltpu.VMEM(shape, kind)
    n = scatter_wires(sizes)
    return [
        vmem(nx, nz, ny, block, width), vmem(nx, nz, ny, block, width),
        vmem(nx - 1, nz, ny, block, a), vmem(ny - 1, nx, nz, block, b),
        vmem(ny - 1, nz, block, a), vmem(nx - 1, nz, block, b),
        vmem(nz - 1, block, width),
        pltpu.SemaphoreType.DMA((n,)), pltpu.SemaphoreType.DMA((n,)), pltpu.SemaphoreType.DMA(()),
    ]


def scatter_stages(near, grad, out, held, got, x_first, y_first, y_then, x_then, z_last, send, recv, own, early=False):
    wires = Wires(near, send, recv)
    at, sizes = near.at, near.sizes
    nz, ny, nx = sizes["z"], sizes["y"], sizes["x"]
    x, y, z = at["x"], at["y"], at["z"]
    first, second = halves(held.shape[-1])
    loads = [] if own is None else [lambda: pltpu.make_async_copy(grad.at[:, at["c"]], held, own)]
    pair = [wires.wire(grad.at[:, 1 - at["c"]], got, "c", 1)]
    one = [wires.wire(held.at[near.along("x", k), :, :, :, first], x_first.at[k - 1], "x", k) for k in near.shifts("x")]
    one += [wires.wire(held.at[:, :, near.along("y", k), :, second], y_first.at[k - 1], "y", k) for k in near.shifts("y")]
    two = [wires.wire(held.at[x, :, near.along("y", k), :, first], y_then.at[k - 1], "y", k) for k in near.shifts("y")]
    two += [wires.wire(held.at[near.along("x", k), :, y, :, second], x_then.at[k - 1], "x", k) for k in near.shifts("x")]
    last = [wires.wire(held.at[x, near.along("z", k), y], z_last.at[k - 1], "z", k) for k in near.shifts("z")]

    def add(where, terms):
        held[where] = sum([t.astype(F32) for t in terms], held[where].astype(F32)).astype(held.dtype)

    def over_z(body):
        lax.fori_loop(0, nz, lambda i, carry: (body(i), carry)[1], 0)

    def stage0():
        start(pair, loads)

    def stage1():
        for load in loads:
            load().wait()
        landed(pair)

        @over_z
        def _(i):
            for a in range(nx):
                for b in range(ny):
                    if own is None:
                        held[a, i, b] = (grad[a, at["c"], i, b].astype(F32) + got[a, i, b].astype(F32)).astype(held.dtype)
                    else:
                        add((a, i, b), [got[a, i, b]])

        start(one)

    def stage2():
        landed(one)

        @over_z
        def _(i):
            for b in range(ny):
                add((x, i, b, ALL, first), [x_first[k - 1, i, b] for k in near.shifts("x")])
            for a in range(nx):
                add((a, i, y, ALL, second), [y_first[k - 1, a, i] for k in near.shifts("y")])

        start(two)

    def stage3():
        landed(two)

        @over_z
        def _(i):
            add((x, i, y, ALL, first), [y_then[k - 1, i] for k in near.shifts("y")])
            add((x, i, y, ALL, second), [x_then[k - 1, i] for k in near.shifts("x")])
            if early:
                out[i] = held[x, i, y]

        if early:
            left(pair, one, two)
        else:
            start(last)

    def stage4():
        landed(last)
        out[...] = sum([z_last[k - 1].astype(F32) for k in near.shifts("z")], held[x, z, y].astype(F32))
        left(pair, one, two, last)

    return [stage0, stage1, stage2, stage3] if early else [stage0, stage1, stage2, stage3, stage4]


def column_stages(near, column, out, z_last, send, recv):
    wires = Wires(near, send, recv)
    last = [wires.wire(column.at[near.along("z", k)], z_last.at[k - 1], "z", k) for k in near.shifts("z")]

    def finish():
        landed(last)
        out[...] = sum([z_last[k - 1].astype(F32) for k in near.shifts("z")], column[near.at["z"]].astype(F32))
        left(last)

    return [lambda: start(last), finish]


def total_scratch(sizes, shape):
    n = sum(sizes[a] - 1 for a in "cxyz")
    return [pltpu.VMEM((n,) + shape, F32), pltpu.VMEM((3,) + shape, F32), pltpu.SemaphoreType.DMA((n,)), pltpu.SemaphoreType.DMA((n,))]


def total_stages(near, mine, out, got, held, send, recv):
    wires = Wires(near, send, recv)
    groups, slots = [], []
    for step, axis in enumerate("cxyz"):
        src = mine if step == 0 else held.at[step - 1]
        slots.append([wires.used + k - 1 for k in near.shifts(axis)])
        groups.append([wires.wire(src, got.at[wires.used], axis, k) for k in near.shifts(axis)])

    def stage(step):
        def run():
            if step > 0:
                landed(groups[step - 1])
                total = mine[...] if step == 1 else held[step - 2]
                for slot in slots[step - 1]:
                    total = total + got[slot]
                if step < 4:
                    held[step - 1] = total
                else:
                    out[...] = total
                    left(*groups)
            if step < 4:
                start(groups[step])

        return run

    return [stage(step) for step in range(5)]


def blocks_of(sizes, grads):
    return [g.reshape(lead(sizes) + (-1, g.shape[1])) for g in grads]


def pump(schedule, plans, chunk):
    for step in sorted({at[0] for at in schedule if at[1] == chunk}):

        @pl.when(pl.program_id(0) == step)
        def _():
            for plan, stage in schedule[step, chunk]:
                plans[plan][stage]()


def mesh_sizes(mesh):
    fsdp = mesh.shape["fsdp"]
    ny = 1 << ((fsdp.bit_length() - 1) // 2)
    return {"x": mesh.shape["dp"] // 2, "c": 2, "z": fsdp // ny, "y": ny}


def project_kernel(x_ref, w_ref, gain_ref, shift_ref, offset_ref, a1_ref, qkv_ref):
    @pl.when(pl.program_id(0) == 0)
    def _():
        def body(rows):
            unit, _ = normalised(x_ref[rows, :].astype(F32))
            a1_ref[rows, :] = (unit * gain_ref[...] + shift_ref[...]).astype(BF)

        row_loop(x_ref.shape[0], 176, body)

    qkv_ref[...] = (dot(a1_ref[...], w_ref[...], 1, 0) + offset_ref[...]).astype(BF)


def project(x, w_in, gain, shift, offset):
    rows, d = x.shape
    return pl.pallas_call(
        project_kernel,
        grid=(3,),
        in_specs=[
            whole((rows, d)),
            pl.BlockSpec((d, d), lambda t: (0, t)),
            whole((1, d)),
            whole((1, d)),
            pl.BlockSpec((1, d), lambda t: (0, t)),
        ],
        out_specs=[whole((rows, d)), pl.BlockSpec((rows, d), lambda t: (0, t))],
        out_shape=[
            jax.ShapeDtypeStruct((rows, d), BF),
            jax.ShapeDtypeStruct((rows, 3 * d), BF),
        ],
        compiler_params=params(),
        cost_estimate=cost(6 * rows * d * d, 2 * (5 * rows * d + 3 * d * d)),
        name="project",
    )(x, w_in, gain, shift, offset)


VEC_ROWS = 16
UP_ROW = 10


def placed(value, width, device):
    size = value.shape[-1]
    row = lax.broadcasted_iota(jnp.int32, (size, width), 0)
    column = lax.broadcasted_iota(jnp.int32, (size, width), 1)
    return dot(value, (column == row + device * size).astype(BF), 1, 0)


def enter_kernel(sizes, tile, x_ref, w_ref, seg_ref, wo_ref, wu_ref, *refs):
    vec_refs, (a1_out, qkv_out, w_out, vecs_ref, mark_ref, far_ref, wo_full, wu_full) = refs[:10], refs[10:18]
    a1_ref, qkv_ref, w_full, unit_ref, mine_ref, third_ref = refs[18:24]
    small_refs, gather_refs, ahead_refs, out_sems = refs[24:28], refs[28:37], refs[37:43], refs[43]
    rows, d = x_ref.shape
    near = Near(sizes)
    near.greet()
    device = lax.axis_index(AXES)
    mine_ref[...] = jnp.zeros_like(mine_ref)
    in_bias, *plain = vec_refs
    up_bias = plain.pop(4)
    for i, ref in enumerate(plain):
        mine_ref[i : i + 1, :] = placed(ref[...], d, device)
    both = placed(in_bias[...], 2 * d, device)
    mine_ref[8:9, :] = both[:, :d]
    mine_ref[9:10, :] = both[:, d:]
    up = placed(up_bias[...], 4 * d, device)
    for i in range(4):
        mine_ref[UP_ROW + i : UP_ROW + i + 1, :] = up[:, d * i : d * (i + 1)]
    plans = [
        gather_stages(near, w_ref, w_full, *gather_refs[3 * t : 3 * t + 3], base=d * t, width=d) for t in range(3)
    ]
    ahead = [
        gather_stages(near, wo_ref, wo_full, *ahead_refs[:3], part="first"),
        gather_stages(near, wu_ref, wu_full, *ahead_refs[3:], part="first"),
    ]
    small = total_stages(near, mine_ref, vecs_ref, *small_refs)
    for plan in plans:
        plan[0]()

    def body(index, carry):
        span = pl.ds(pl.multiple_of(index * tile, tile), tile)
        unit_ref[span, :], _ = normalised(x_ref[span, :].astype(F32))
        for step in range(3):
            pl.when(index == step)(small[step])
        return carry

    lax.fori_loop(0, rows // tile, body, 0)
    plans[0][1]()
    small[3]()
    for plan in ahead:
        plan[0]()
    image = lax.broadcasted_iota(jnp.int32, (128, rows), 0) % HD
    same = seg_ref[...] == image
    mark_ref[...] = same.astype(F32).T.astype(BF)
    far_ref[...] = jnp.where(same | (image > PADDING), 0.0, FAR).T.astype(BF)
    plans[1][1]()
    plans[0][2]()
    plans[2][1]()
    plans[1][2]()
    small[4]()

    def shifted(span):
        a1_ref[span, :] = (unit_ref[span, :] * vecs_ref[1:2, :] + vecs_ref[2:3, :]).astype(BF)

    row_loop(rows, tile, shifted)
    sends = [pltpu.make_async_copy(a1_ref, a1_out, out_sems.at[0])]
    sends[0].start()

    def third(t):
        cols = slice(d * t, d * (t + 1))
        third_ref[...] = w_full[:, :, :, :, :, cols].astype(F32).reshape(d, d).astype(BF)

        def body(span):
            value = dot(a1_ref[span, :], third_ref[...], 1, 0)
            if t != 1:
                value = value + vecs_ref[8 + t // 2 : 9 + t // 2, :]
            qkv_ref[span, cols] = value.astype(BF)

        row_loop(rows, rows // 4, body)

    def store(t):
        cols = pl.ds(d * t, d)
        sends.append(pltpu.make_async_copy(qkv_ref.at[:, cols], qkv_out.at[:, cols], out_sems.at[1 + t]))
        sends[-1].start()

    plans[0][3]()
    plans[2][2]()
    plans[0][4]()
    third(0)
    plans[1][3]()
    store(0)
    plans[1][4]()
    plans[2][3]()
    third(1)
    store(1)
    plans[2][4]()
    sends.append(pltpu.make_async_copy(w_full, w_out, out_sems.at[4]))
    sends[-1].start()
    third(2)
    store(2)
    for plan in ahead:
        plan[1]()
    for copy in sends:
        copy.wait()


def enter(sizes, x, w_in, segment_ids, w_out, w_up, vectors, tile=352):
    rows, d = x.shape
    vmem, hbm = pl.BlockSpec(memory_space=pltpu.VMEM), pl.BlockSpec(memory_space=pltpu.HBM)
    full = lead(sizes) + w_in.shape
    return pl.pallas_call(
        functools.partial(enter_kernel, sizes, tile),
        in_specs=[vmem] * 15,
        out_specs=[hbm, hbm, hbm, vmem, vmem, vmem, hbm, hbm],
        out_shape=[
            jax.ShapeDtypeStruct((rows, d), BF),
            jax.ShapeDtypeStruct((rows, 3 * d), BF),
            jax.ShapeDtypeStruct(full, BF),
            jax.ShapeDtypeStruct((VEC_ROWS, d), F32),
            jax.ShapeDtypeStruct((rows, 128), BF),
            jax.ShapeDtypeStruct((rows, 128), BF),
            *gathered(sizes, [w_out, w_up]),
        ],
        scratch_shapes=[
            pltpu.VMEM((rows, d), BF),
            pltpu.VMEM((rows, 3 * d), BF),
            pltpu.VMEM(full, BF),
            pltpu.VMEM((rows, d), F32),
            pltpu.VMEM((VEC_ROWS, d), F32),
            pltpu.VMEM((d, d), BF),
            *total_scratch(sizes, (VEC_ROWS, d)),
            *gather_scratch(sizes) * 5,
            pltpu.SemaphoreType.DMA((5,)),
        ],
        compiler_params=params(collective_id=0, has_side_effects=True),
        name="enter",
    )(x, w_in, segment_ids[None], w_out, w_up, *[v[None] for v in vectors])


def chunks(rows, size):
    return [(start, min(size, rows - start)) for start in range(0, rows, size)]


GATHER_AT = {
    (0, 0): [(2, 0), (1, 1), (0, 1)],
    (1, 0): [(1, 2)],
    (2, 0): [(2, 1)],
    (3, 0): [(0, 2), (1, 3), (2, 2)],
    (4, 0): [(0, 3)],
    (5, 0): [(2, 3), (0, 4)],
    (5, -1): [(1, 4), (2, 4)],
}


def attend_kernel(chunk, sizes, count, q_ref, k_ref, v_ref, mark_ref, far_ref, *refs):
    shards, (o_ref, e_ref, inv_ref) = refs[:count][::-1], refs[count : count + 3]
    full, (vt_ref, k2_ref), sems = refs[count + 3 : 2 * count + 3], refs[2 * count + 3 : 2 * count + 5], refs[2 * count + 5 :]
    rows = q_ref.shape[0]
    plans, schedule = [], {}
    if count:
        near, schedule = Near(sizes), GATHER_AT
        pl.when(pl.program_id(0) == 0)(near.greet)
        plans = [
            gather_stages(near, shards[i], full[i], *sems[3 * i : 3 * i + 3], part="all" if i == 2 else "rest") for i in range(count)
        ]
    vt_ref[...] = v_ref[...].astype(F32).T.astype(BF)
    low = lax.broadcasted_iota(jnp.int32, (1, 128), 1) < HD
    for half in range(2):
        mine = low if half == 0 else jnp.logical_not(low)
        k2_ref[half] = jnp.where(mine, k_ref[...], far_ref[...])
    for turn, (start, size) in enumerate(chunks(rows, chunk)):
        pump(schedule, plans, turn)
        for half in range(2):
            mine = low if half == 0 else jnp.logical_not(low)
            span = pl.ds(start, size)
            query = jnp.where(mine, q_ref[span, :], mark_ref[span, :])
            scores = dot(k2_ref[half], query, 1, 1)
            top = jnp.max(scores, axis=0, keepdims=True)
            weights = jnp.exp2((scores - top) * (LOG2E * HD ** (-0.5)))
            total = jnp.sum(weights, axis=0, keepdims=True)
            weights_low = weights.astype(BF)
            e_ref[half, :, span] = weights_low
            inverse = 1.0 / total
            inv_ref[0, half : half + 1, span] = inverse
            head = pl.ds(half * HD, HD)
            o_ref[head, span] = (dot(vt_ref[head, :], weights_low, 1, 0) * inverse).astype(BF)
    pump(schedule, plans, -1)


def attend(qkv, mark, far, sizes, shards, chunk=704):
    count = len(shards)
    hbm = pl.BlockSpec(memory_space=pltpu.HBM)
    rows, width = qkv.shape
    pairs = width // 384
    return pl.pallas_call(
        functools.partial(attend_kernel, chunk, sizes, count),
        grid=(pairs,),
        in_specs=[
            pl.BlockSpec((rows, 128), lambda p: (0, p)),
            pl.BlockSpec((rows, 128), lambda p: (0, pairs + p)),
            pl.BlockSpec((rows, 128), lambda p: (0, 2 * pairs + p)),
            whole((rows, 128)),
            whole((rows, 128)),
            *([whole(shards[2].shape), hbm, hbm] if count else []),
        ],
        out_specs=[
            pl.BlockSpec((128, rows), lambda p: (p, 0)),
            pl.BlockSpec((2, rows, rows), lambda p: (p, 0, 0)),
            pl.BlockSpec((1, 2, rows), lambda p: (p, 0, 0)),
            *[hbm] * count,
        ],
        out_shape=[
            jax.ShapeDtypeStruct((pairs * 128, rows), BF),
            jax.ShapeDtypeStruct((2 * pairs, rows, rows), BF),
            jax.ShapeDtypeStruct((pairs, 2, rows), F32),
            *([*shards[:2], *gathered(sizes, shards[2:])] if count else []),
        ],
        scratch_shapes=[
            pltpu.VMEM((128, rows), BF),
            pltpu.VMEM((2, rows, 128), BF),
            *(gather_scratch(sizes) * count if count else []),
        ],
        compiler_params=params(collective_id=1, has_side_effects=True) if count else params(),
        cost_estimate=cost(2 * pairs * 4 * rows * rows * 256, 4 * pairs * rows * rows, 2 * pairs * rows * rows),
        input_output_aliases={7: 3, 6: 4} if count else {},
        name="attend",
    )(qkv, qkv, qkv, mark, far, *shards[::-1])


def masked(g_ref, mark_ref, rows):
    padding = mark_ref[rows, PADDING : PADDING + 1].astype(F32)
    return jnp.where(padding > 0, 0.0, g_ref[rows, :].astype(F32))


def middle_kernel(o_ref, x_ref, g_ref, mark_ref, w_ref, vec_ref, m1_ref, a2_ref, gm_ref, gmsum_ref):
    bias, scale1, gain2, shift2, scale2 = (vec_ref[i : i + 1, :] for i in (0, 3, 5, 6, 7))
    m1_ref[...] = dot(o_ref[...], w_ref[...], 0, 0)
    gmsum_ref[...] = jnp.zeros_like(gmsum_ref)

    def body(rows):
        m1 = x_ref[rows, :].astype(F32) + scale1 * (m1_ref[rows, :] + bias)
        m1_ref[rows, :] = m1
        unit, _ = normalised(m1)
        a2_ref[rows, :] = (unit * gain2 + shift2).astype(BF)
        gm = (scale2 * masked(g_ref, mark_ref, rows)).astype(BF)
        gm_ref[rows, :] = gm
        gmsum_ref[...] += jnp.sum(gm.astype(F32).reshape(-1, 8, gm.shape[-1]), axis=0)

    row_loop(x_ref.shape[0], 176, body)


def middle(o, x, g, mark, w_out, vec):
    rows, d = x.shape
    return pl.pallas_call(
        middle_kernel,
        out_shape=[
            jax.ShapeDtypeStruct((rows, d), F32),
            jax.ShapeDtypeStruct((rows, d), BF),
            jax.ShapeDtypeStruct((rows, d), BF),
            jax.ShapeDtypeStruct((8, d), F32),
        ],
        compiler_params=params(),
        cost_estimate=cost(2 * rows * d * d, 14 * rows * d),
        name="middle",
    )(o, x, g, mark, w_out, vec)


def gelu_parts(u):
    near = jnp.abs(u)
    t = 1.0 / (1.0 + (0.3275911 * 0.7071067811865476) * near)
    bell = jnp.exp2((-0.5 * LOG2E) * (u * u))
    poly = t * (
        0.5 * 0.254829592
        + t * (0.5 * -0.284496736 + t * (0.5 * 1.421413741 + t * (0.5 * -1.453152027 + t * (0.5 * 1.061405429))))
    )
    tail = poly * bell
    phi = jnp.where(u < 0, tail, 1.0 - tail)
    return u * phi, phi + u * bell * 0.3989422804014327


def feed_kernel(chunk, a2_ref, gm_ref, up_ref, vec_ref, down_ref, bm_ref, ga_ref, dup_ref, ddown_ref, dub_ref, gl_ref, gu_ref):
    first = pl.program_id(0) == 0

    @pl.when(first)
    def _():
        bm_ref[...] = jnp.zeros_like(bm_ref)
        ga_ref[...] = jnp.zeros_like(ga_ref)

    d = vec_ref.shape[-1]
    spread = up_ref.shape[-1] // d
    bias = jnp.concatenate([vec_ref[pl.ds(UP_ROW + pl.program_id(0) * spread + i, 1), :] for i in range(spread)], axis=1)
    dub_ref[...] = jnp.zeros_like(dub_ref)

    def body(rows):
        u = dot(a2_ref[rows, :], up_ref[...], 1, 0) + bias
        back = dot(gm_ref[rows, :], down_ref[...], 1, 1)
        active, slope = gelu_parts(u)
        low = active.astype(BF)
        gl_ref[rows, :] = low
        gu = (slope * back).astype(BF)
        gu_ref[rows, :] = gu
        dub_ref[...] += jnp.sum(gu.astype(F32).reshape(-1, 8, gu.shape[-1]), axis=0)
        bm_ref[rows, :] += dot(low, down_ref[...], 1, 0)
        ga_ref[rows, :] += dot(gu, up_ref[...], 1, 1)

    row_loop(a2_ref.shape[0], chunk, body)

    def weights(span):
        ddown_ref[span, :] = dot(gl_ref[:, span], gm_ref[...], 0, 0).astype(ddown_ref.dtype)
        dup_ref[span, :] = dot(a2_ref[:, span], gu_ref[...], 0, 0).astype(dup_ref.dtype)

    row_loop(dup_ref.shape[0], 256, weights)


def feed(a2, gm, w_up, vecs, w_down, block=768, chunk=704, kind=BF):
    rows, d = a2.shape
    ff = w_up.shape[1]
    return pl.pallas_call(
        functools.partial(feed_kernel, chunk),
        grid=(ff // block,),
        in_specs=[
            whole((rows, d)),
            whole((rows, d)),
            pl.BlockSpec((d, block), lambda f: (0, f)),
            whole((VEC_ROWS, d)),
            pl.BlockSpec((block, d), lambda f: (f, 0)),
        ],
        out_specs=[
            whole((rows, d)),
            whole((rows, d)),
            pl.BlockSpec((d, block), lambda f: (0, f)),
            pl.BlockSpec((block, d), lambda f: (f, 0)),
            pl.BlockSpec((8, block), lambda f: (0, f)),
        ],
        out_shape=[
            jax.ShapeDtypeStruct((rows, d), F32),
            jax.ShapeDtypeStruct((rows, d), F32),
            jax.ShapeDtypeStruct((d, ff), kind),
            jax.ShapeDtypeStruct((ff, d), kind),
            jax.ShapeDtypeStruct((8, ff), F32),
        ],
        scratch_shapes=[pltpu.VMEM((rows, block), BF), pltpu.VMEM((rows, block), BF)],
        compiler_params=params(),
        cost_estimate=cost(12 * rows * d * ff, 4 * 4 * d * ff),
        name="feed",
    )(a2, gm, w_up, vecs, w_down)


def join_kernel(size, m1_ref, bm_ref, ga_ref, x_ref, g_ref, mark_ref, o_ref, w_ref, vec_ref, out_ref, gm1_ref, go_ref, dout_ref, sums_ref, gb_ref):
    bias2, scale1, gain2, scale2 = (vec_ref[i : i + 1, :] for i in (4, 3, 5, 7))
    step = pl.program_id(0)

    @pl.when(step == 0)
    def _():
        sums_ref[...] = jnp.zeros_like(sums_ref)

    base = step * m1_ref.shape[0]

    def body(rows):
        m1 = m1_ref[rows, :]
        bm = bm_ref[rows, :] + bias2
        g = masked(g_ref, mark_ref, rows)
        out_ref[rows, :] = (m1 + scale2 * bm).astype(BF)
        unit, inverse = normalised(m1)
        ga = ga_ref[rows, :]
        gm1 = g + norm_back(unit, inverse, ga * gain2)
        gm1_ref[rows, :] = gm1
        gb = (scale1 * gm1).astype(BF)
        gb_ref[pl.ds(pl.multiple_of(base + rows.start, size), size), :] = gb
        for index, value in enumerate(
            (g * bm, ga * unit, ga, gm1 * (m1 - x_ref[rows, :].astype(F32)), gb.astype(F32))
        ):
            sums_ref[index] += jnp.sum(value.reshape(-1, 8, value.shape[-1]), axis=0)

    row_loop(m1_ref.shape[0], size, body)

    @pl.when(step == pl.num_programs(0) - 1)
    def _():
        go_ref[...] = dot(w_ref[...], gb_ref[...], 1, 1).astype(BF)
        dout_ref[...] = dot(o_ref[...], gb_ref[...], 1, 0).astype(dout_ref.dtype)


def join(m1, bm, ga, x, g, mark, o, w_out, vec, tile=352, kind=BF):
    rows, d = x.shape
    by_rows = pl.BlockSpec((tile, d), lambda i: (i, 0))
    return pl.pallas_call(
        functools.partial(join_kernel, 176),
        grid=(rows // tile,),
        in_specs=[by_rows] * 5 + [pl.BlockSpec((tile, 128), lambda i: (i, 0)), whole((d, rows)), whole((d, d)), whole((VEC_ROWS, d))],
        out_specs=[by_rows, by_rows, whole((d, rows)), whole((d, d)), whole((5, 8, d))],
        out_shape=[
            jax.ShapeDtypeStruct((rows, d), BF),
            jax.ShapeDtypeStruct((rows, d), F32),
            jax.ShapeDtypeStruct((d, rows), BF),
            jax.ShapeDtypeStruct((d, d), kind),
            jax.ShapeDtypeStruct((5, 8, d), F32),
        ],
        scratch_shapes=[pltpu.VMEM((rows, d), BF)],
        compiler_params=params(),
        cost_estimate=cost(4 * rows * d * d, 26 * rows * d),
        name="join",
    )(m1, bm, ga, x, g, mark, o, w_out, vec)


SCATTER_AT = {
    (0, 0): [(0, 0), (2, 0)],
    (1, 0): [(0, 1)],
    (2, 0): [(1, 0), (2, 1)],
    (3, 0): [(0, 2), (1, 1)],
    (4, 0): [(2, 2), (0, 3)],
    (5, 0): [(1, 2), (2, 3)],
    (5, -1): [(1, 3), (2, 4), (0, 4)],
}


def attend_back_kernel(chunk, sizes, count, q_ref, k_ref, v_ref, go_ref, o_ref, e_ref, inv_ref, *refs):
    grads, out_ref, sums = refs[:count], refs[count], refs[count + 1 : 2 * count + 1]
    (kt_ref, gq_ref, gs_ref, gp_ref), rest = refs[2 * count + 1 : 2 * count + 5], refs[2 * count + 5 :]
    rows = q_ref.shape[0]
    plans, schedule = [], {}
    if count:
        near, schedule = Near(sizes), SCATTER_AT
        pl.when(pl.program_id(0) == 0)(near.greet)
        plans = [
            scatter_stages(near, grads[i], sums[i], *rest[SCATTER_REFS * i : SCATTER_REFS * (i + 1)], early=i == 1)
            for i in range(count)
        ]
    factor = HD ** (-0.5)
    kt_ref[...] = k_ref[...].astype(F32).T.astype(BF)
    low = lax.broadcasted_iota(jnp.int32, (1, 128), 1) < HD
    below = lax.broadcasted_iota(jnp.int32, (128, 1), 0) < HD
    gp_ref[...] = jnp.zeros_like(gp_ref)
    for turn, (start, size) in enumerate(chunks(rows, chunk)):
        pump(schedule, plans, turn)
        span = pl.ds(start, size)
        for half in range(2):
            head = pl.ds(half * HD, HD)
            incoming = go_ref[head, span].astype(F32) * inv_ref[0, half : half + 1, span]
            centre = jnp.sum(incoming * o_ref[head, span].astype(F32), axis=0, keepdims=True)
            gp_ref[half, head, span] = incoming.astype(BF)
            gp = dot(v_ref[...], gp_ref[half, :, span], 1, 0)
            gs = (e_ref[half, :, span].astype(F32) * (gp - centre)).astype(BF)
            gs_ref[half, :, span] = gs
            gq_ref[head, span] = dot(kt_ref[head, :], gs, 1, 0) * factor
    out_ref[0] = gq_ref[...].T.astype(BF)

    def keys(span):
        gk = [dot(gs_ref[half, span, :], q_ref[...], 1, 0) for half in range(2)]
        out_ref[1, span, :] = (jnp.where(low, gk[0], gk[1]) * factor).astype(BF)
        out_ref[2, span, :] = (dot(e_ref[0, span, :], gp_ref[0], 1, 1) + dot(e_ref[1, span, :], gp_ref[1], 1, 1)).astype(BF)

    row_loop(rows, rows // 2, keys)
    pump(schedule, plans, -1)


def attend_back(qkv, go, o, e, inv, sizes, grads, chunk=512):
    blocks = blocks_of(sizes, grads) if grads else []
    count = len(blocks)
    sums = [jax.ShapeDtypeStruct(b.shape[-2:], F32) for b in blocks]
    if count:
        sums[1] = jax.ShapeDtypeStruct((sizes["z"],) + sums[1].shape, BF)
    rows, width = qkv.shape
    pairs = width // 384
    return pl.pallas_call(
        functools.partial(attend_back_kernel, chunk, sizes, count),
        grid=(pairs,),
        in_specs=[
            pl.BlockSpec((rows, 128), lambda p: (0, p)),
            pl.BlockSpec((rows, 128), lambda p: (0, pairs + p)),
            pl.BlockSpec((rows, 128), lambda p: (0, 2 * pairs + p)),
            pl.BlockSpec((128, rows), lambda p: (p, 0)),
            pl.BlockSpec((128, rows), lambda p: (p, 0)),
            pl.BlockSpec((2, rows, rows), lambda p: (p, 0, 0)),
            pl.BlockSpec((1, 2, rows), lambda p: (p, 0, 0)),
            *[pl.BlockSpec(memory_space=pltpu.HBM)] * count,
        ],
        out_specs=[pl.BlockSpec((3, rows, 128), lambda p: (0, 0, p)), *[whole(v.shape) for v in sums]],
        out_shape=[
            jax.ShapeDtypeStruct((3, rows, pairs * 128), BF),
            *sums,
        ],
        scratch_shapes=[
            pltpu.VMEM((128, rows), BF),
            pltpu.VMEM((128, rows), F32),
            pltpu.VMEM((2, rows, rows), BF),
            pltpu.VMEM((2, 128, rows), BF),
            *[s for b in blocks for s in scatter_scratch(sizes, *b.shape[-2:], b.dtype)],
        ],
        compiler_params=params(collective_id=2, has_side_effects=True) if count else params(),
        cost_estimate=cost(2 * pairs * 8 * rows * rows * 256, 4 * pairs * rows * rows),
        name="attend_back",
    )(qkv, qkv, qkv, go, o, e, inv, *blocks)


def finish_kernel(a1_ref, gqkv_ref, w_ref, x_ref, gm1_ref, gain_ref, dw_ref, cols_ref, gx_ref, sums_ref, ga_ref):
    step = pl.program_id(0)
    grads = gqkv_ref[0]
    dw_ref[...] = dot(a1_ref[...], grads, 0, 0).astype(dw_ref.dtype)
    cols_ref[0] = jnp.sum(grads.astype(F32).reshape(-1, 8, grads.shape[-1]), axis=0)
    part = dot(grads, w_ref[...], 1, 1)

    @pl.when(step == 0)
    def _():
        ga_ref[...] = part

    @pl.when(step > 0)
    def _():
        ga_ref[...] += part

    @pl.when(step == pl.num_programs(0) - 1)
    def _():
        sums_ref[...] = jnp.zeros_like(sums_ref)

        def body(rows):
            unit, inverse = normalised(x_ref[rows, :].astype(F32))
            ga = ga_ref[rows, :]
            gx_ref[rows, :] = gm1_ref[rows, :] + norm_back(unit, inverse, ga * gain_ref[...])
            for index, value in enumerate((ga * unit, ga)):
                sums_ref[index] += jnp.sum(value.reshape(-1, 8, value.shape[-1]), axis=0)

        row_loop(x_ref.shape[0], 176, body)


def finish(a1, gqkv, w_in, x, gm1, gain, kind=BF):
    rows, d = x.shape
    return pl.pallas_call(
        finish_kernel,
        grid=(3,),
        in_specs=[
            whole((rows, d)),
            pl.BlockSpec((1, rows, d), lambda t: (t, 0, 0)),
            pl.BlockSpec((d, d), lambda t: (0, t)),
            whole((rows, d)),
            whole((rows, d)),
            whole((1, d)),
        ],
        out_specs=[
            pl.BlockSpec((d, d), lambda t: (0, t)),
            pl.BlockSpec((1, 8, d), lambda t: (t, 0, 0)),
            whole((rows, d)),
            whole((2, 8, d)),
        ],
        out_shape=[
            jax.ShapeDtypeStruct((d, 3 * d), kind),
            jax.ShapeDtypeStruct((3, 8, d), F32),
            jax.ShapeDtypeStruct((rows, d), F32),
            jax.ShapeDtypeStruct((2, 8, d), F32),
        ],
        scratch_shapes=[pltpu.VMEM((rows, d), F32)],
        compiler_params=params(),
        cost_estimate=cost(12 * rows * d * d, 20 * rows * d),
        name="finish",
    )(a1, gqkv, w_in, x, gm1, gain)


def leave_kernel(sizes, tile, a1_in, gqkv_in, w_in, x_in, gm1_in, vec_ref, join_ref, ub_ref, gmsum_ref, column_ref, gx_out, dw_ref, early_ref, late_ref, ddown_ref, *refs):
    a1_ref, gqkv_ref, w_ref, x_ref, gm1_ref, gx_ref, ga_ref, sums_ref, mine_ref, last_ref = refs[:10]
    grad_refs, refs = refs[10:13], refs[13:]
    scatter_refs, refs = [refs[9 * t : 9 * t + 9] for t in range(3)], refs[27:]
    early_refs, late_refs, column_refs, in_sems, out_sems = refs[:4], refs[4:8], refs[8:11], refs[11], refs[12]
    rows, d = x_in.shape
    count = rows // tile
    moves = [(a1_in, a1_ref), *[(gqkv_in.at[t], gqkv_ref.at[t]) for t in range(3)], (w_in, w_ref), (x_in, x_ref), (gm1_in, gm1_ref)]
    fetch = [pltpu.make_async_copy(src, dst, in_sems.at[n]) for n, (src, dst) in enumerate(moves)]
    for copy in fetch:
        copy.start()
    near = Near(sizes)
    near.greet()
    row = lambda value: jnp.sum(value, axis=0, keepdims=True)
    mine_ref[...] = jnp.zeros_like(mine_ref)
    for i, value in enumerate(
        (row(join_ref[4]), row(join_ref[3]) / vec_ref[3:4, :], row(gmsum_ref[...]), row(join_ref[1]), row(join_ref[2]), row(join_ref[0]))
    ):
        mine_ref[i : i + 1, :] = value
    for i in range(4):
        mine_ref[8 + i : 9 + i, :] = row(ub_ref[:, d * i : d * (i + 1)])
    plans = [
        scatter_stages(near, grad_refs[t], dw_ref.at[:, pl.ds(d * t, d)], *scatter_refs[t], None) for t in range(3)
    ]
    early = total_stages(near, mine_ref, early_ref, *early_refs)
    late = total_stages(near, last_ref, late_ref, *late_refs)
    column = column_stages(near, column_ref, ddown_ref, *column_refs)
    column[0]()
    last_ref[...] = jnp.zeros_like(last_ref)

    def weight(t):
        fetch[1 + t].wait()
        part = d // sizes["x"]

        def body(x, carry):
            value = dot(a1_ref[:, pl.ds(pl.multiple_of(x * part, part), part)], gqkv_ref[t], 0, 0)
            grad_refs[t][x] = value.reshape(grad_refs[t].shape[1:]).astype(BF)
            return carry

        lax.fori_loop(0, sizes["x"], body, 0)

    def back(t):
        def body(span):
            part = dot(gqkv_ref[t, span, :], w_ref[:, d * t : d * (t + 1)], 1, 1)
            ga_ref[span, :] = part if t == 0 else ga_ref[span, :] + part

        row_loop(rows, rows // 4, body)
        if t != 1:
            total = jnp.zeros((1, d), F32)
            for start_row, size in chunks(rows, tile):
                total += row(gqkv_ref[t, pl.ds(start_row, size), :].astype(F32))
            last_ref[2 + t // 2 : 3 + t // 2, :] = total

    fetch[0].wait()
    weight(0)
    early[0]()
    plans[0][0]()
    weight(1)
    plans[0][1]()
    plans[1][0]()
    early[1]()
    weight(2)
    plans[1][1]()
    plans[2][0]()
    fetch[4].wait()
    back(0)
    plans[0][2]()
    plans[2][1]()
    early[2]()
    back(1)
    plans[1][2]()
    back(2)
    plans[0][3]()
    column[1]()
    early[3]()
    fetch[5].wait()
    fetch[6].wait()
    sums_ref[...] = jnp.zeros_like(sums_ref)

    def send(index):
        span = pl.ds(pl.multiple_of(index * tile, tile), tile)
        return pltpu.make_async_copy(gx_ref.at[span], gx_out.at[span], out_sems.at[index])

    between = [[], [plans[2][2], plans[1][3]], []]

    def body(index, carry):
        span = pl.ds(pl.multiple_of(index * tile, tile), tile)
        unit, inverse = normalised(x_ref[span, :].astype(F32))
        ga = ga_ref[span, :]
        gx_ref[span, :] = gm1_ref[span, :] + norm_back(unit, inverse, ga * vec_ref[1:2, :])
        for n, value in enumerate((ga * unit, ga)):
            sums_ref[n] += jnp.sum(value.reshape(-1, 8, d), axis=0)
        for n, stages in enumerate(between):

            @pl.when(index == n)
            def _():
                for stage in stages:
                    stage()

        pl.when(index > 0)(lambda: send(index - 1).start())
        return carry

    lax.fori_loop(0, count, body, 0)
    for n in range(2):
        last_ref[n : n + 1, :] = row(sums_ref[n])
    late[0]()
    send(count - 1).start()
    early[4]()
    plans[2][3]()
    late[1]()
    plans[0][4]()
    late[2]()
    plans[1][4]()
    late[3]()
    plans[2][4]()
    late[4]()
    for index in range(count):
        send(index).wait()


def leave(sizes, a1, gqkv, w_in, x, gm1, vecs, join_sums, ub_sum, gm_sum, column, tile=352):
    rows, d = x.shape
    vmem, hbm = pl.BlockSpec(memory_space=pltpu.VMEM), pl.BlockSpec(memory_space=pltpu.HBM)
    block = d // (sizes["x"] * 2 * sizes["z"] * sizes["y"])
    return pl.pallas_call(
        functools.partial(leave_kernel, sizes, tile),
        in_specs=[hbm] * 5 + [vmem] * 5,
        out_specs=[hbm, vmem, vmem, vmem, vmem],
        out_shape=[
            jax.ShapeDtypeStruct((rows, d), F32),
            jax.ShapeDtypeStruct((block, 3 * d), F32),
            jax.ShapeDtypeStruct((16, d), F32),
            jax.ShapeDtypeStruct((8, d), F32),
            jax.ShapeDtypeStruct(column.shape[1:], F32),
        ],
        scratch_shapes=[
            pltpu.VMEM((rows, d), BF),
            pltpu.VMEM((3, rows, d), BF),
            pltpu.VMEM((d, 3 * d), BF),
            pltpu.VMEM((rows, d), BF),
            pltpu.VMEM((rows, d), F32),
            pltpu.VMEM((rows, d), F32),
            pltpu.VMEM((rows, d), F32),
            pltpu.VMEM((2, 8, d), F32),
            pltpu.VMEM((16, d), F32),
            pltpu.VMEM((8, d), F32),
            *[pltpu.VMEM(lead(sizes) + (block, d), BF)] * 3,
            *scatter_scratch(sizes, block, d, BF)[:-1] * 3,
            *total_scratch(sizes, (16, d)),
            *total_scratch(sizes, (8, d)),
            pltpu.VMEM((sizes["z"] - 1,) + column.shape[1:], BF),
            pltpu.SemaphoreType.DMA((sizes["z"] - 1,)),
            pltpu.SemaphoreType.DMA((sizes["z"] - 1,)),
            pltpu.SemaphoreType.DMA((7,)),
            pltpu.SemaphoreType.DMA((rows // tile,)),
        ],
        compiler_params=params(collective_id=3, has_side_effects=True),
        name="leave",
    )(a1, gqkv, w_in, x, gm1, vecs, join_sums, ub_sum, gm_sum, column)


def share_kernel(early_ref, late_ref, *refs):
    grads, outs, vec_outs = refs[:4], refs[4:8], refs[8:]
    for src, dst in zip(grads, outs):
        dst[...] = src[...]
    device = lax.axis_index(AXES)
    d = early_ref.shape[-1]

    def entries(ref, first_row, size):
        at = device * size
        line = ref[pl.ds(first_row + lax.div(at, d), 1), :]
        return pltpu.roll(jnp.broadcast_to(line, (8, d)), lax.rem(d - lax.rem(at, d), d), 1)[:1, :size]

    spots = [
        (late_ref, 2), (early_ref, 0), (late_ref, 0), (late_ref, 1), (early_ref, 1),
        (early_ref, 8), (early_ref, 2), (early_ref, 3), (early_ref, 4), (early_ref, 5),
    ]
    for (ref, first_row), out in zip(spots, vec_outs):
        out[...] = entries(ref, first_row, out.shape[-1])


def share(early, late, grads, sizes):
    vmem = pl.BlockSpec(memory_space=pltpu.VMEM)
    return pl.pallas_call(
        share_kernel,
        in_specs=[vmem] * 6,
        out_specs=[vmem] * 14,
        out_shape=[jax.ShapeDtypeStruct(g.shape, F32) for g in grads] + [jax.ShapeDtypeStruct((1, n), F32) for n in sizes],
        compiler_params=params(),
        name="share",
    )(early, late, *grads)


def take(a):
    return lax.all_gather(a, AXES, axis=0, tiled=True)


def give(g):
    return lax.psum_scatter(g, AXES, scatter_dimension=0, tiled=True).astype(F32)


def layer(
    sizes, inputs, segment_ids, cotangent, in_weight, in_bias, out_weight, out_bias, first_gain, first_shift, first_scale,
    up_weight, up_bias, down_weight, down_bias, second_gain, second_shift, second_scale,
):
    rows, d = inputs.shape
    vectors = (
        in_bias, out_bias, first_gain, first_shift, first_scale,
        up_bias, down_bias, second_gain, second_shift, second_scale,
    )
    own = all(w.shape[0] % 8 == 0 for w in (in_weight, out_weight, up_weight, down_weight))
    if own:
        a1, qkv, w_in, vecs, mark, far, *begun = enter(
            sizes, inputs, in_weight, segment_ids, out_weight, up_weight, vectors
        )
        w_in = w_in.reshape(d, 3 * d)
    else:
        w_in = take(in_weight)
        row = lambda v: take(v).astype(F32).reshape(-1, d)
        vecs = jnp.concatenate(
            [row(v) for v in (out_bias, first_gain, first_shift, first_scale, down_bias, second_gain, second_shift, second_scale, in_bias)]
            + [row(up_bias), jnp.zeros((VEC_ROWS - 14, d), F32)]
        )
        offset = jnp.concatenate([vecs[8:9], jnp.zeros((1, d), F32), vecs[9:10]], axis=1)
        a1, qkv = project(inputs, w_in, vecs[1:2], vecs[2:3], offset)
        lane = lax.broadcasted_iota(jnp.int32, (1, 128), 1) % HD
        same = segment_ids[:, None] == lane
        mark = same.astype(BF)
        far = jnp.where(same | (lane > PADDING), 0.0, FAR).astype(BF)
    o, e, inv, *full = attend(qkv, mark, far, sizes, [*begun, down_weight] if own else [])
    w_out, w_up, w_down = (
        (f.reshape(-1, f.shape[-1]) for f in full) if own else (take(w) for w in (out_weight, up_weight, down_weight))
    )
    m1, a2, gm, gm_sum = middle(o, inputs, cotangent, mark, w_out, vecs)
    bm, ga2, d_up, d_down, ub_sum = feed(a2, gm, w_up, vecs, w_down)
    outputs, gm1, go, d_out, join_sums = join(m1, bm, ga2, inputs, cotangent, mark, o, w_out, vecs)
    gqkv, *done = attend_back(qkv, go, o, e, inv, sizes, [d_up, d_down, d_out] if own else [])
    if own:
        d_up, column, d_out = done
        gx, d_in, early, late, d_down = leave(sizes, a1, gqkv, w_in, inputs, gm1, vecs, join_sums, ub_sum, gm_sum, column)
        d_up, d_down, d_out, d_in, *out = share(early, late, [d_up, d_down, d_out, d_in], [v.shape[0] for v in vectors])
        out = [v.reshape(-1) for v in out]
    else:
        d_in, col_sums, gx, last_sums = finish(a1, gqkv, w_in, inputs, gm1, vecs[1:2])
        d_in, d_up, d_down, d_out = (give(v) for v in (d_in, d_up, d_down, d_out))
        s = jnp.sum
        j, c, t = (s(v, axis=1) for v in (join_sums, col_sums, last_sums))
        sums = (
            jnp.concatenate([c[0], c[2]]), j[4], t[0], t[1], j[3] / vecs[3], s(ub_sum, axis=0), s(gm_sum, axis=0), j[1], j[2], j[0],
        )
        out = [give(v) for v in sums]
    return (
        outputs, gx, d_in, out[0], d_out, out[1], out[2], out[3], out[4],
        d_up, out[5], d_down, out[6], out[7], out[8], out[9],
    )


def solution(mesh):
    wide, flat = P(AXES, None), P(AXES)
    return jax.shard_map(
        functools.partial(layer, mesh_sizes(mesh)),
        mesh=mesh,
        in_specs=(wide, flat, wide, wide, flat, wide, flat, flat, flat, flat, wide, flat, wide, flat, flat, flat, flat),
        out_specs=(wide, wide, wide, flat, wide, flat, flat, flat, flat, wide, flat, wide, flat, flat, flat, flat),
        check_vma=False,
    )
```
